256 devices in a mesh: dp: 8 (over y, z_lo), space: 32 (over x, z_hi, core).
Axes of the slice: x: 4, y: 4, z: 8 (z_hi: 4, z_lo: 2; z = z_hi * 2 + z_lo), core: 2. Of those that a mesh axis runs over, the one named last changes fastest.
Arguments:
- inputs: bfloat16 [8, 32, 48, 4096], P('dp', 'space'), may hold values from -6 to 6
- cotangent: bfloat16 [8, 32, 48, 4096], P('dp', 'space'), may hold values from -6 to 6
- conv_one: bfloat16 [9, 48, 48], replicated, may hold values from -0.3125 to 0.3125
- bias_one: float32 [48], replicated, may hold values from -3 to 3
- conv_two: bfloat16 [9, 48, 48], replicated, may hold values from -0.3125 to 0.3125
- bias_two: float32 [48], replicated, may hold values from -3 to 3
- neighbours: int32 [32, 4, 3], replicated, may hold values from 0 to 31, as said below
- corner_rule: int32 [32, 4], replicated, may hold values from 0 to 2
Outputs:
- output: bfloat16 [8, 32, 48, 4096], P('dp', 'space')
- grad_in: bfloat16 [8, 32, 48, 4096], P('dp', 'space')
- grad_conv_one: float32 [9, 48, 48], P(None, 'dp')
- grad_bias_one: float32 [48], P('dp')
- grad_conv_two: float32 [9, 48, 48], P(None, 'dp')
- grad_bias_two: float32 [48], P('dp')
The draws below stay inside these ranges and needn't reach their ends.
Inputs may be any that keep to these rules, and one draw needn't show every extreme that they name: Slot neighbours[t, e, 0] of a tile on the device block d (tiles d * 1 to d + 1 - 1) lies on block d - 1, d + 8, d + 1, d - 8 (cyclically over the 32 blocks) for e = 0, 1, 2, 3; neighbours[t, e, 1] and neighbours[t, e, 2] are 0 to 3.
All inputs are finite; a program needn't handle non-finite values.
Results may differ from the reference program's by a relative error of at most 0.009.
Values may be sent and summed in bfloat16 or wider, within the bound.
A program may use at most 64 MiB of HBM per device.

```python
import jax
import jax.numpy as jnp
from jax import lax

C = 48
S = 64
TILE_DEV = 1
P_SIZE = 4096
TILES = 32
BATCH = 8
HOP = 8


def permute_block(block_key):
    return jax.random.permutation(block_key, TILE_DEV)


def draw_neighbours(key, part):
    devices = TILES // TILE_DEV
    slot_ids = jnp.arange(TILES, dtype=jnp.int32)
    device_of = slot_ids // TILE_DEV
    local_ids = slot_ids % TILE_DEV
    offsets = (-1, HOP, 1, -HOP)
    columns = []
    for edge_id in range(4):
        block_keys = jax.random.split(jax.random.fold_in(key, edge_id), devices)
        perms = jax.vmap(permute_block)(block_keys).astype(jnp.int32)
        source_device = (device_of + offsets[edge_id]) % devices
        columns.append(source_device * TILE_DEV + perms[device_of, local_ids])
    slots = jnp.stack(columns, axis=1)
    edges = jax.random.randint(jax.random.fold_in(key, 10), (TILES, 4), 0, 4, dtype=jnp.int32)
    rotations = jax.random.randint(jax.random.fold_in(key, 11), (TILES, 4), 0, 4, dtype=jnp.int32)
    return jnp.stack([slots, edges, rotations], axis=2).astype(jnp.int32)


def set_ends(values, rng, low, top_value):
    index_at = [jax.random.randint(jax.random.fold_in(rng, axis), (), 0, length) for axis, length in enumerate(values.shape)]
    main_axis = values.shape.index(max(values.shape))
    neighbour = index_at[:main_axis] + [(index_at[main_axis] + 1) % values.shape[main_axis]] + index_at[main_axis + 1:]
    return values.at[tuple(index_at)].set(low).at[tuple(neighbour)].set(top_value)


def level_of(rng, dims, shards, low, high):
    def one(position, parts):
        steps = jax.random.uniform(jax.random.fold_in(jax.random.fold_in(rng, 6), position), (parts,), jnp.float32, low / len(shards), high / len(shards))
        return jnp.repeat(jnp.exp(steps), dims[position] // parts).reshape((-1,) + (1,) * (len(dims) - position - 1))

    factor_of = one(*shards[0])
    for cut in shards[1:]:
        factor_of = factor_of * one(*cut)
    return factor_of


def scatter_about(key, shape, scale, most, cuts=(), kind=jnp.bfloat16):
    level = level_of(key, shape, cuts, -0.22, 0.18) if cuts else 1.0
    drawn = jax.random.normal(key, shape, jnp.float32) * scale * level
    return jnp.minimum(jnp.maximum(drawn, -most), most).astype(kind)


def setup_inputs(seed: int = 0) -> dict:
    key_list = jax.random.split(jax.random.key(seed), 9)
    return {
        "inputs": scatter_about(key_list[0], (BATCH, TILES, C, P_SIZE), 1.0, 6.0, ((0, 8), (1, 32))),
        "cotangent": scatter_about(key_list[1], (BATCH, TILES, C, P_SIZE), 1.0, 6.0, ((0, 8), (1, 32))),
        "conv_one": scatter_about(key_list[2], (9, C, C), (9 * C) ** -0.5, 0.3125),
        "bias_one": scatter_about(key_list[3], (C,), 0.5, 3.0, (), jnp.float32),
        "conv_two": scatter_about(key_list[4], (9, C, C), (9 * C) ** -0.5, 0.3125),
        "bias_two": scatter_about(key_list[5], (C,), 0.5, 3.0, (), jnp.float32),
        "neighbours": draw_neighbours(jax.random.fold_in(key_list[8], 71), 0),
        "corner_rule": set_ends(jax.random.randint(key_list[7], (TILES, 4), 0, 3), jax.random.fold_in(key_list[7], 1), 0, 2).astype(jnp.int32),
    }


def lines_of(tile_image):
    return jnp.stack([tile_image[..., 0, :], tile_image[..., :, -1], tile_image[..., -1, :], tile_image[..., :, 0]], axis=2)

def assemble(tile_image, edge_lines, tile_rules):
    top_line = edge_lines[:, :, 0]
    right_line = edge_lines[:, :, 1]
    bottom_line = edge_lines[:, :, 2]
    left_line = edge_lines[:, :, 3]
    pairs = ((top_line[..., 0], left_line[..., 0]), (top_line[..., -1], right_line[..., 0]), (bottom_line[..., 0], left_line[..., -1]), (bottom_line[..., -1], right_line[..., -1]))
    corners = []
    for corner_id in range(4):
        first_value, second_value = pairs[corner_id]
        rule_now = tile_rules[:, corner_id][None, :, None]
        mean_value = ((first_value.astype(jnp.float32) + second_value.astype(jnp.float32)) * 0.5).astype(tile_image.dtype)
        corners.append(jnp.where(rule_now == 0, first_value, jnp.where(rule_now == 1, second_value, mean_value)))
    middle = jnp.concatenate([left_line[..., :, None], tile_image, right_line[..., :, None]], axis=-1)
    top_row = jnp.concatenate([corners[0][..., None], top_line, corners[1][..., None]], axis=-1)
    bottom_row = jnp.concatenate([corners[2][..., None], bottom_line, corners[3][..., None]], axis=-1)
    return jnp.concatenate([top_row[..., None, :], middle, bottom_row[..., None, :]], axis=-2)

def halo_ref(field, neighbours, corner_rule):
    batch_len, tile_count, channels, pixels = field.shape
    side_len = S
    tile_image = field.reshape(batch_len, tile_count, channels, side_len, side_len)
    all_lines = lines_of(tile_image).reshape(batch_len, tile_count * 4, channels, side_len)
    picked = all_lines[:, neighbours[:, :, 0] * 4 + neighbours[:, :, 1]]
    flip_mask = (neighbours[:, :, 2] == 1) | (neighbours[:, :, 2] == 2)
    picked = jnp.where(flip_mask[None, :, :, None, None], picked[..., ::-1], picked)
    return assemble(tile_image, picked, corner_rule)

def conv_apply(padded, weights):
    lead = padded.shape[:3]
    row_width = padded.shape[-1]
    side_len = row_width - 2
    out_span = side_len * row_width
    flat_pad = jnp.pad(padded.reshape(lead + (row_width * row_width,)), ((0, 0), (0, 0), (0, 0), (0, 2))).astype(jnp.float32)
    summed = jnp.zeros(lead[:2] + (weights.shape[1], out_span), jnp.float32)
    for tap_id in range(9):
        start_at = tap_id // 3 * row_width + tap_id % 3
        window = lax.slice_in_dim(flat_pad, start_at, start_at + out_span, axis=3)
        summed = summed + jnp.einsum('oc,btcq->btoq', weights[tap_id].astype(jnp.float32), window)
    return summed.reshape(lead[:2] + (weights.shape[1], side_len, row_width))[..., :side_len].reshape(lead[:2] + (weights.shape[1], side_len * side_len))

def spread_rows(grad, side_len):
    lead = grad.shape[:3]
    squared = grad.reshape(lead + (side_len, side_len))
    return jnp.pad(squared, ((0, 0), (0, 0), (0, 0), (0, 0), (0, 2))).reshape(lead + (side_len * (side_len + 2),))

def conv_transpose(grad, weights, side_len):
    lead = grad.shape[:2]
    row_width = side_len + 2
    out_span = side_len * row_width
    full_len = row_width * row_width + 2
    flat_grad = spread_rows(grad, side_len).astype(jnp.float32)
    summed = jnp.zeros(lead + (weights.shape[2], full_len), jnp.float32)
    for tap_id in range(9):
        start_at = tap_id // 3 * row_width + tap_id % 3
        placed = jnp.einsum('oc,btoq->btcq', weights[tap_id].astype(jnp.float32), flat_grad)
        summed = summed + jnp.pad(placed, ((0, 0), (0, 0), (0, 0), (start_at, full_len - out_span - start_at)))
    return summed[..., :row_width * row_width].reshape(lead + (weights.shape[2], row_width, row_width))

def weight_grad(grad, padded):
    lead = padded.shape[:3]
    row_width = padded.shape[-1]
    side_len = row_width - 2
    out_span = side_len * row_width
    flat_grad = spread_rows(grad, side_len).astype(jnp.float32)
    flat_pad = jnp.pad(padded.reshape(lead + (row_width * row_width,)), ((0, 0), (0, 0), (0, 0), (0, 2))).astype(jnp.float32)
    taps = []
    for tap_id in range(9):
        start_at = tap_id // 3 * row_width + tap_id % 3
        window = lax.slice_in_dim(flat_pad, start_at, start_at + out_span, axis=3)
        taps.append(jnp.einsum('btoq,btcq->oc', flat_grad, window))
    return jnp.stack(taps, axis=0)

def activate(values):
    return jax.nn.gelu(values, approximate=True)

def reference(inputs, cotangent, conv_one, bias_one, conv_two, bias_two, neighbours, corner_rule):

    def halo_linear(field):
        return halo_ref(field, neighbours, corner_rule)

    def one_sample(pair):
        sample_in = pair[0][None]
        sample_grad = pair[1][None]
        pad_in = halo_ref(sample_in, neighbours, corner_rule)
        pre_one = conv_apply(pad_in, conv_one) + bias_one[None, None, :, None]
        act_one = activate(pre_one).astype(jnp.bfloat16)
        pad_act = halo_ref(act_one, neighbours, corner_rule)
        output = (sample_in.astype(jnp.float32) + conv_apply(pad_act, conv_two) + bias_two[None, None, :, None]).astype(jnp.bfloat16)
        d_pad_act = conv_transpose(sample_grad, conv_two, S)
        pull_act = jax.vjp(halo_linear, act_one.astype(jnp.float32))[1]
        d_act = pull_act(d_pad_act)[0]
        pull_gelu = jax.vjp(activate, pre_one)[1]
        d_pre = pull_gelu(d_act)[0].astype(jnp.bfloat16)
        grad_two = weight_grad(sample_grad, pad_act)
        bias_grad_two = lax.optimization_barrier(jnp.sum(sample_grad.astype(jnp.float32), axis=(0, 1, 3)))
        grad_one = weight_grad(d_pre, pad_in)
        bias_grad_one = lax.optimization_barrier(jnp.sum(d_pre.astype(jnp.float32), axis=(0, 1, 3)))
        d_pad_in = conv_transpose(d_pre, conv_one, S)
        pull_in = jax.vjp(halo_linear, sample_in.astype(jnp.float32))[1]
        grad_in = (sample_grad.astype(jnp.float32) + pull_in(d_pad_in)[0]).astype(jnp.bfloat16)
        return (output[0], grad_in[0], grad_one, bias_grad_one, grad_two, bias_grad_two)
    results = lax.map(one_sample, (inputs, cotangent))
    return (results[0], results[1], lax.optimization_barrier(jnp.sum(results[2], axis=0)), lax.optimization_barrier(jnp.sum(results[3], axis=0)), lax.optimization_barrier(jnp.sum(results[4], axis=0)), lax.optimization_barrier(jnp.sum(results[5], axis=0)))
```

```python
import functools
import math

import jax
import jax.numpy as jnp
from jax import lax
from jax.experimental import pallas as pl
from jax.experimental.pallas import tpu as pltpu
from jax.sharding import PartitionSpec as P

MESH = pl.DeviceIdType.MESH
F32 = jnp.float32
BF16 = jnp.bfloat16
LANES = 128
CH = 48
SIDE = 64
GROUPS = 32
EXTRA = 32
WIDE = (GROUPS + 1) * LANES
K3 = 3 * CH
ROOT = math.sqrt(2.0 / math.pi)


def grp(v):
    return slice(v * LANES, (v + 1) * LANES)


def roll(values, shift):
    shift = shift % LANES
    return pltpu.roll(values, shift, 1) if shift else values


def dot(a, b, dims):
    return lax.dot_general(a, b, (dims, ((), ())), preferred_element_type=F32)


def line_lane(edge, q):
    odd = (q & 1) == 1
    col_left = jnp.where(odd, q + 63, q)
    col_right = jnp.where(odd, (q + 126) & 127, q + 63)
    return jnp.where(
        edge == 0, q, jnp.where(edge == 2, q + 64, jnp.where(edge == 3, col_left, col_right))
    )


def halo_index(edge, lane):
    if edge == 0:
        return jnp.where(lane >= 64, lane - 64, -1000)
    if edge == 2:
        return jnp.where(lane < 64, lane, -1000)
    even = (lane & 1) == 0
    if edge == 3:
        return jnp.where(even, jnp.where(lane < 64, lane, lane - 63), -1000)
    return jnp.where(even, -1000, jnp.where(lane == 127, 1, jnp.where(lane >= 63, lane - 63, lane + 2)))


def mover(edge, line, rotation):
    lane = lax.broadcasted_iota(jnp.int32, (8, LANES), 1)
    q = halo_index(edge, lane)
    turned = jnp.where((rotation == 1) | (rotation == 2), 63 - q, q)
    source = jnp.where(q < 0, -1, line_lane(line, turned))
    rows = lax.broadcasted_iota(jnp.int32, (LANES, LANES), 0)
    return jnp.where(rows == jnp.broadcast_to(source[0:1], (LANES, LANES)), 1.0, 0.0).astype(BF16)


def column(vector):
    rows = lax.broadcasted_iota(jnp.int32, (CH, CH), 0)
    cols = lax.broadcasted_iota(jnp.int32, (CH, CH), 1)
    spread = jnp.broadcast_to(vector, (CH, CH))
    return jnp.sum(jnp.where(rows == cols, spread, 0.0), axis=1, keepdims=True)


def block_kernel(
    n_dp,
    n_space,
    x_hbm,
    g_hbm,
    w1_ref,
    b1_ref,
    w2_ref,
    b2_ref,
    nb_ref,
    rule_ref,
    out_hbm,
    gin_hbm,
    gw1_ref,
    gb1_ref,
    gw2_ref,
    gb2_ref,
    x_v,
    g_v,
    act_v,
    dpre_v,
    out_v,
    gin_v,
    slope_v,
    ex_v,
    ea_v,
    gs2_v,
    gs1_v,
    y_fwd,
    y_two,
    y_one,
    fwd_send,
    fwd_recv,
    adj_send,
    adj_recv,
    part_send,
    buf_a,
    buf_b,
    buf_c,
    load_sem,
    store_sem,
    halo_ssem,
    halo_rsem,
    a_ssem,
    a_rsem,
    b_ssem,
    b_rsem,
    c_ssem,
    c_rsem,
):
    hop = n_space // 4
    n_c = 4
    n_b = n_space // n_c
    rows_dev = CH // n_dp
    rows_pad = (rows_dev + 7) // 8 * 8
    me = lax.axis_index("space")
    my_dp = lax.axis_index("dp")
    my_b = lax.rem(me, n_b)
    my_c = lax.div(me, n_b)
    offsets = (-1, hop, 1, -hop)
    toward = [lax.rem(me + off + n_space, n_space) for off in offsets]
    reader = [lax.rem(me - off + n_space, n_space) for off in offsets]
    peers_a = [lax.rem(my_dp + s, n_dp) for s in range(1, n_dp)]
    peers_b = [my_c * n_b + lax.rem(my_b + s, n_b) for s in range(1, n_b)]
    peers_c = [lax.rem(my_c + s, n_c) * n_b + my_b for s in range(1, n_c)]

    load_x = pltpu.make_async_copy(x_hbm.at[0, 0], x_v, load_sem.at[0])
    load_g = pltpu.make_async_copy(g_hbm.at[0, 0], g_v, load_sem.at[1])
    load_x.start()
    load_g.start()

    barrier = pltpu.get_barrier_semaphore()
    for dev in toward:
        pl.semaphore_signal(barrier, inc=1, device_id={"space": dev}, device_id_type=MESH)
    for dev in peers_a:
        pl.semaphore_signal(barrier, inc=1, device_id={"dp": dev}, device_id_type=MESH)
    for dev in peers_b + peers_c:
        pl.semaphore_signal(barrier, inc=1, device_id={"space": dev}, device_id_type=MESH)

    lane = lax.broadcasted_iota(jnp.int32, (CH, LANES), 1)
    low = lane < 64
    first_col = (lane & 63) == 0
    last_col = (lane & 63) == 63
    edge_col = first_col | last_col
    zero = jnp.zeros((CH, LANES), F32)

    def remote(src, dst, ssem, rsem, device):
        return pltpu.make_async_remote_copy(
            src_ref=src,
            dst_ref=dst,
            send_sem=ssem,
            recv_sem=rsem,
            device_id=device,
            device_id_type=MESH,
        )

    def halo_copy(sends, recvs, slot, edge, dev):
        at = slot * 4 + edge
        return remote(
            sends.at[edge], recvs.at[edge], halo_ssem.at[at], halo_rsem.at[at], {"space": dev}
        )

    fwd_line = [nb_ref[reader[e], e, 1] for e in range(4)]
    fwd_turn = [nb_ref[reader[e], e, 2] for e in range(4)]
    own_line = [nb_ref[me, e, 1] for e in range(4)]
    own_turn = [nb_ref[me, e, 2] for e in range(4)]
    fwd_movers = [mover(e, fwd_line[e], fwd_turn[e]) for e in range(4)]

    def forward_messages(group_of, sends):
        rows = jnp.where(low, group_of(0), group_of(GROUPS - 1))
        cols = [zero, zero, zero, zero]
        for v in range(GROUPS):
            cols[v % 4] = cols[v % 4] + roll(jnp.where(edge_col, group_of(v), 0.0), 2 * v)
        cols = (cols[0] + cols[1]) + (cols[2] + cols[3])
        for e in range(4):
            source = jnp.where((fwd_line[e] & 1) == 1, cols, rows).astype(BF16)
            sends[e] = dot(source, fwd_movers[e], ((1,), (0,))).astype(BF16)

    def corner_seconds(spread):
        return jnp.where(low, roll(spread, 2), roll(spread, 64))

    rules = [rule_ref[me, c] for c in range(4)]
    rule_at = jnp.where(
        lane == 64,
        rules[0],
        jnp.where(lane == 127, rules[1], jnp.where(lane == 0, rules[2], rules[3])),
    )

    def fill_padded(group_of, recvs, padded):
        spread = recvs[1].astype(F32) + recvs[3].astype(F32)
        outer = recvs[0].astype(F32) + recvs[2].astype(F32)
        second = corner_seconds(spread)
        mean = ((outer + second) * 0.5).astype(BF16).astype(F32)
        corners = jnp.where(rule_at == 0, outer, jnp.where(rule_at == 1, second, mean))
        for v in range(GROUPS + 1):
            here = outer if v == EXTRA else group_of(v)
            sides = corners if v == EXTRA else roll(spread, -2 * v)
            padded[0:CH, grp(v)] = jnp.where(first_col, sides, roll(here, 1)).astype(BF16)
            padded[CH : 2 * CH, grp(v)] = here.astype(BF16)
            padded[2 * CH : K3, grp(v)] = jnp.where(last_col, sides, roll(here, -1)).astype(BF16)
        padded[K3 : K3 + 16, :] = jnp.ones((16, WIDE), BF16)

    def stacked(w_ref):
        return jnp.concatenate(
            [
                jnp.concatenate([w_ref[3 * a + b] for b in range(3)], axis=1)
                for a in range(3)
            ],
            axis=0,
        )

    def conv(weights, padded, y_ref):
        y_ref[...] = dot(weights, padded[0:K3, :], ((1,), (0,)))

    def conv_group(y_ref, v):
        prev = EXTRA if v == 0 else v - 1
        both = jnp.where(
            low,
            y_ref[0:CH, grp(v)] + y_ref[2 * CH : K3, grp(v + 1)],
            y_ref[2 * CH : K3, grp(v)] + y_ref[0:CH, grp(prev)],
        )
        return y_ref[CH : 2 * CH, grp(v)] + roll(both, 64)

    def stack_rows(grad_v, gs_ref):
        turned = None
        for v in range(GROUPS + 1):
            before = turned
            if v == EXTRA:
                gs_ref[CH : 2 * CH, grp(v)] = zero.astype(BF16)
                gs_ref[2 * CH : K3, grp(v)] = jnp.where(low, before, 0.0).astype(BF16)
                gs_ref[0:CH, grp(v - 1)] = jnp.where(low, before, 0.0).astype(BF16)
                gs_ref[0:CH, grp(v)] = jnp.where(
                    low, 0.0, roll(grad_v[:, grp(0)].astype(F32), 64)
                ).astype(BF16)
                continue
            here = grad_v[:, grp(v)]
            turned = roll(here.astype(F32), 64)
            gs_ref[CH : 2 * CH, grp(v)] = here
            gs_ref[2 * CH : K3, grp(v)] = jnp.where(
                low, 0.0 if v == 0 else before, turned
            ).astype(BF16)
            if v > 0:
                gs_ref[0:CH, grp(v - 1)] = jnp.where(low, before, turned).astype(BF16)

    def transpose_conv(weights, gs_ref, y_ref):
        y_ref[...] = dot(weights, gs_ref[...], ((0,), (0,)))

    def inner_group(y_ref, v):
        left = jnp.where(last_col, 0.0, roll(y_ref[0:CH, grp(v)], -1))
        right = jnp.where(first_col, 0.0, roll(y_ref[2 * CH : K3, grp(v)], 1))
        return y_ref[CH : 2 * CH, grp(v)] + (left + right)

    first_weight = jnp.where(rule_at == 0, 1.0, jnp.where(rule_at == 1, 0.0, 0.5))

    def adjoint_messages(y_ref, sends):
        def sides(v):
            return jnp.where(
                edge_col,
                jnp.where(last_col, y_ref[2 * CH : K3, grp(v)], y_ref[0:CH, grp(v)]),
                0.0,
            )

        cols = [zero, zero, zero, zero]
        for v in range(GROUPS):
            cols[v % 4] = cols[v % 4] + roll(sides(v), 2 * v)
        corners = sides(EXTRA)
        firsts = first_weight * corners
        seconds = corners - firsts
        cols = (
            (cols[0] + cols[1])
            + (cols[2] + cols[3])
            + roll(jnp.where(low, seconds, 0.0), -2)
            + roll(jnp.where(low, 0.0, seconds), 64)
        ).astype(BF16)
        rows = (inner_group(y_ref, EXTRA) + firsts).astype(BF16)
        for e in range(4):
            move = mover(e, own_line[e], own_turn[e])
            source = cols if e % 2 else rows
            sends[e] = dot(source, move, ((1,), (1,))).astype(BF16)

    def returned_lines(recvs):
        rows, cols = zero, zero
        for e in range(4):
            message = recvs[e].astype(F32)
            is_col = (fwd_line[e] & 1) == 1
            rows = rows + jnp.where(is_col, 0.0, message)
            cols = cols + jnp.where(is_col, message, 0.0)
        return rows, cols

    def pulled_back(y_ref, rows, cols, v):
        total = inner_group(y_ref, v) + jnp.where(edge_col, roll(cols, -2 * v), 0.0)
        if v == 0:
            total = total + jnp.where(low, rows, 0.0)
        if v == GROUPS - 1:
            total = total + jnp.where(low, 0.0, rows)
        return total

    def put_part(grads, main, rest_shift):
        rest = grads[:, LANES:]
        for d in range(n_dp):
            for a in range(3):
                at = a * CH + d * rows_dev
                part_send[d, main, a * rows_pad : a * rows_pad + rows_dev, :] = grads[
                    at : at + rows_dev, 0:LANES
                ]
                part_send[
                    d, 2, a * rows_pad : a * rows_pad + rows_dev, rest_shift : rest_shift + 32
                ] = rest[at : at + rows_dev]

    part_send[...] = jnp.zeros(part_send.shape, F32)
    load_x.wait()

    def x_group(v):
        return x_v[:, grp(v)].astype(F32)

    forward_messages(x_group, fwd_send.at[0])
    pl.semaphore_wait(barrier, 4 + len(peers_a) + len(peers_b) + len(peers_c))
    in_fwd = [halo_copy(fwd_send.at[0], fwd_recv.at[0], 0, e, reader[e]) for e in range(4)]
    for copy in in_fwd:
        copy.start()

    load_g.wait()
    w_two = stacked(w2_ref)
    stack_rows(g_v, gs2_v)
    transpose_conv(w_two, gs2_v, y_two)
    adjoint_messages(y_two, adj_send.at[0])
    two_adj = [halo_copy(adj_send.at[0], adj_recv.at[0], 1, e, toward[e]) for e in range(4)]
    for copy in two_adj:
        copy.start()

    w_one = stacked(w1_ref)
    bias_one = jnp.broadcast_to(column(b1_ref[...].reshape(1, CH)), (CH, LANES))
    bias_two = jnp.broadcast_to(column(b2_ref[...].reshape(1, CH)), (CH, LANES))
    for copy in in_fwd:
        copy.wait_recv()
    fill_padded(x_group, fwd_recv.at[0], ex_v)
    conv(w_one, ex_v, y_fwd)
    for v in range(GROUPS):
        pre = conv_group(y_fwd, v) + bias_one
        square = pre * pre
        th = jnp.tanh(ROOT * (pre + 0.044715 * (square * pre)))
        cdf = 0.5 * (1.0 + th)
        act_v[:, grp(v)] = (pre * cdf).astype(BF16)
        slope_v[:, grp(v)] = cdf + (0.5 * pre) * (1.0 - th * th) * (
            ROOT * (1.0 + (3.0 * 0.044715) * square)
        )

    def act_group(v):
        return act_v[:, grp(v)].astype(F32)

    forward_messages(act_group, fwd_send.at[1])
    act_fwd = [halo_copy(fwd_send.at[1], fwd_recv.at[1], 2, e, reader[e]) for e in range(4)]
    for copy in act_fwd:
        copy.start()

    for copy in two_adj:
        copy.wait_recv()
    rows, cols = returned_lines(adj_recv.at[0])
    for v in range(GROUPS):
        dpre_v[:, grp(v)] = (pulled_back(y_two, rows, cols, v) * slope_v[:, grp(v)]).astype(BF16)
    stack_rows(dpre_v, gs1_v)
    transpose_conv(w_one, gs1_v, y_one)
    adjoint_messages(y_one, adj_send.at[1])
    one_adj = [halo_copy(adj_send.at[1], adj_recv.at[1], 3, e, toward[e]) for e in range(4)]
    for copy in one_adj:
        copy.start()
    put_part(dot(gs1_v[...], ex_v[...], ((1,), (1,))), 0, 0)

    for copy in act_fwd:
        copy.wait_recv()
    fill_padded(act_group, fwd_recv.at[1], ea_v)
    put_part(dot(gs2_v[...], ea_v[...], ((1,), (1,))), 1, 32)
    dp_copies = [
        remote(
            part_send.at[dev], buf_a.at[my_dp], a_ssem.at[s], a_rsem.at[s], {"dp": dev}
        )
        for s, dev in enumerate(peers_a)
    ]
    for copy in dp_copies:
        copy.start()
    buf_a[my_dp] = part_send[my_dp]

    conv(w_two, ea_v, y_fwd)
    for v in range(GROUPS):
        out_v[:, grp(v)] = (x_group(v) + conv_group(y_fwd, v) + bias_two).astype(BF16)
    store_out = pltpu.make_async_copy(out_v, out_hbm.at[0, 0], store_sem.at[0])
    store_out.start()

    for copy in one_adj:
        copy.wait_recv()
    rows, cols = returned_lines(adj_recv.at[1])
    for v in range(GROUPS):
        gin_v[:, grp(v)] = (
            g_v[:, grp(v)].astype(F32) + pulled_back(y_one, rows, cols, v)
        ).astype(BF16)
    store_gin = pltpu.make_async_copy(gin_v, gin_hbm.at[0, 0], store_sem.at[1])
    store_gin.start()

    def summed(buf, count):
        total = buf[0]
        for s in range(1, count):
            total = total + buf[s]
        return total

    for copy in dp_copies:
        copy.wait_recv()
    buf_b[my_b] = summed(buf_a, n_dp)
    b_copies = [
        remote(buf_b.at[my_b], buf_b.at[my_b], b_ssem.at[s], b_rsem.at[s], {"space": dev})
        for s, dev in enumerate(peers_b)
    ]
    for copy in b_copies:
        copy.start()
    for copy in b_copies:
        copy.wait_recv()
    buf_c[my_c] = summed(buf_b, n_b)
    c_copies = [
        remote(buf_c.at[my_c], buf_c.at[my_c], c_ssem.at[s], c_rsem.at[s], {"space": dev})
        for s, dev in enumerate(peers_c)
    ]
    for copy in c_copies:
        copy.start()
    for copy in c_copies:
        copy.wait_recv()
    total = summed(buf_c, n_c)

    for main, shift, gw_ref, gb_ref in ((0, 0, gw1_ref, gb1_ref), (1, 32, gw2_ref, gb2_ref)):
        full = jnp.concatenate([total[main], roll(total[2], -shift)], axis=1)
        for a in range(3):
            part = full[a * rows_pad : a * rows_pad + rows_dev]
            for b in range(3):
                gw_ref[3 * a + b] = part[:, b * CH : (b + 1) * CH]
        bias_col = full[rows_pad : rows_pad + rows_dev, K3 : K3 + 1]
        eye_r = lax.broadcasted_iota(jnp.int32, (rows_dev, rows_dev), 0)
        eye_c = lax.broadcasted_iota(jnp.int32, (rows_dev, rows_dev), 1)
        spread = jnp.broadcast_to(bias_col, (rows_dev, rows_dev))
        gb_ref[...] = jnp.sum(jnp.where(eye_r == eye_c, spread, 0.0), axis=0)

    for copy in in_fwd + two_adj + act_fwd + one_adj + dp_copies + b_copies + c_copies:
        copy.wait_send()
    store_out.wait()
    store_gin.wait()


def on_device(n_dp, n_space, *args):
    rows_dev = CH // n_dp
    rows_pad = (rows_dev + 7) // 8 * 8
    n_c = 4
    n_b = n_space // n_c
    share = (3, 3 * rows_pad, LANES)
    field = args[0].shape
    anywhere = pl.BlockSpec(memory_space=pl.ANY)
    vmem = pl.BlockSpec(memory_space=pltpu.VMEM)
    smem = pl.BlockSpec(memory_space=pltpu.SMEM)
    dma = pltpu.SemaphoreType.DMA
    return pl.pallas_call(
        functools.partial(block_kernel, n_dp, n_space),
        out_shape=(
            jax.ShapeDtypeStruct(field, BF16),
            jax.ShapeDtypeStruct(field, BF16),
            jax.ShapeDtypeStruct((9, rows_dev, CH), F32),
            jax.ShapeDtypeStruct((rows_dev,), F32),
            jax.ShapeDtypeStruct((9, rows_dev, CH), F32),
            jax.ShapeDtypeStruct((rows_dev,), F32),
        ),
        in_specs=[anywhere, anywhere, vmem, vmem, vmem, vmem, smem, smem],
        out_specs=(anywhere, anywhere, vmem, vmem, vmem, vmem),
        scratch_shapes=[
            pltpu.VMEM((CH, GROUPS * LANES), BF16),
            pltpu.VMEM((CH, GROUPS * LANES), BF16),
            pltpu.VMEM((CH, GROUPS * LANES), BF16),
            pltpu.VMEM((CH, GROUPS * LANES), BF16),
            pltpu.VMEM((CH, GROUPS * LANES), BF16),
            pltpu.VMEM((CH, GROUPS * LANES), BF16),
            pltpu.VMEM((CH, GROUPS * LANES), F32),
            pltpu.VMEM((K3 + 16, WIDE), BF16),
            pltpu.VMEM((K3 + 16, WIDE), BF16),
            pltpu.VMEM((K3, WIDE), BF16),
            pltpu.VMEM((K3, WIDE), BF16),
            pltpu.VMEM((K3, WIDE), F32),
            pltpu.VMEM((K3, WIDE), F32),
            pltpu.VMEM((K3, WIDE), F32),
            pltpu.VMEM((2, 4, CH, LANES), BF16),
            pltpu.VMEM((2, 4, CH, LANES), BF16),
            pltpu.VMEM((2, 4, CH, LANES), BF16),
            pltpu.VMEM((2, 4, CH, LANES), BF16),
            pltpu.VMEM((n_dp,) + share, F32),
            pltpu.VMEM((n_dp,) + share, F32),
            pltpu.VMEM((n_b,) + share, F32),
            pltpu.VMEM((n_c,) + share, F32),
            dma((2,)),
            dma((2,)),
            dma((16,)),
            dma((16,)),
            dma((max(n_dp - 1, 1),)),
            dma((max(n_dp - 1, 1),)),
            dma((max(n_b - 1, 1),)),
            dma((max(n_b - 1, 1),)),
            dma((n_c - 1,)),
            dma((n_c - 1,)),
        ],
        compiler_params=pltpu.CompilerParams(
            collective_id=0, has_side_effects=True, vmem_limit_bytes=40 << 20
        ),
        name="unet_block",
    )(*args)


def solution(mesh):
    tiled = P("dp", "space", None, None)
    return jax.shard_map(
        functools.partial(on_device, mesh.shape["dp"], mesh.shape["space"]),
        mesh=mesh,
        in_specs=(tiled, tiled, P(), P(), P(), P(), P(), P()),
        out_specs=(tiled, tiled, P(None, "dp", None), P("dp"), P(None, "dp", None), P("dp")),
        check_vma=False,
    )
```

```python
import functools
import math

import jax
import jax.numpy as jnp
from jax import lax
from jax.experimental import pallas as pl
from jax.experimental.pallas import tpu as pltpu
from jax.sharding import PartitionSpec as P

MESH = pl.DeviceIdType.MESH
F32 = jnp.float32
BF16 = jnp.bfloat16
LANES = 128
CH = 48
SIDE = 64
GROUPS = 32
EXTRA = 32
WIDE = (GROUPS + 1) * LANES
K3 = 3 * CH
ROOT = math.sqrt(2.0 / math.pi)


def grp(v):
    return slice(v * LANES, (v + 1) * LANES)


def roll(values, shift):
    shift = shift % LANES
    return pltpu.roll(values, shift, 1) if shift else values


def dot(a, b, dims):
    return lax.dot_general(a, b, (dims, ((), ())), preferred_element_type=F32)


def line_lane(edge, q):
    odd = (q & 1) == 1
    col_left = jnp.where(odd, q + 63, q)
    col_right = jnp.where(odd, (q + 126) & 127, q + 63)
    return jnp.where(
        edge == 0, q, jnp.where(edge == 2, q + 64, jnp.where(edge == 3, col_left, col_right))
    )


def halo_index(edge, lane):
    if edge == 0:
        return jnp.where(lane >= 64, lane - 64, -1000)
    if edge == 2:
        return jnp.where(lane < 64, lane, -1000)
    even = (lane & 1) == 0
    if edge == 3:
        return jnp.where(even, jnp.where(lane < 64, lane, lane - 63), -1000)
    return jnp.where(even, -1000, jnp.where(lane == 127, 1, jnp.where(lane >= 63, lane - 63, lane + 2)))


def line_index(line, lane):
    even = (lane & 1) == 0
    row = jnp.where(line == 0, lane, lane - 64)
    row = jnp.where((row >= 0) & (row < 64), row, -1000)
    left = jnp.where(even, jnp.where(lane < 64, lane, lane - 63), -1000)
    right = jnp.where(
        even, -1000, jnp.where(lane == 127, 1, jnp.where(lane >= 63, lane - 63, lane + 2))
    )
    return jnp.where((line & 1) == 0, row, jnp.where(line == 3, left, right))


def shifted_mover(edge, line, rotation, shift, end_weight):
    lane = lax.broadcasted_iota(jnp.int32, (8, LANES), 1)
    p = line_index(line, lane)
    q = jnp.where((rotation == 1) | (rotation == 2), 63 - p, p)
    valid = p >= 0
    tap = q + 1 - shift
    source = jnp.where(valid & (tap >= 0) & (tap < 64), line_lane(edge, tap), -1)
    rows = lax.broadcasted_iota(jnp.int32, (LANES, LANES), 0)
    table = jnp.where(rows == jnp.broadcast_to(source[0:1], (LANES, LANES)), 1.0, 0.0)
    if shift != 1:
        end = 0 if shift == 0 else 63
        corner = jnp.where(valid & (q == end), line_lane(edge, q), -1)
        table = table + jnp.where(
            rows == jnp.broadcast_to(corner[0:1], (LANES, LANES)), end_weight, 0.0
        )
    return table.astype(BF16)


def mover(edge, line, rotation):
    lane = lax.broadcasted_iota(jnp.int32, (8, LANES), 1)
    q = halo_index(edge, lane)
    turned = jnp.where((rotation == 1) | (rotation == 2), 63 - q, q)
    source = jnp.where(q < 0, -1, line_lane(line, turned))
    rows = lax.broadcasted_iota(jnp.int32, (LANES, LANES), 0)
    return jnp.where(rows == jnp.broadcast_to(source[0:1], (LANES, LANES)), 1.0, 0.0).astype(BF16)


def column(vector):
    rows = lax.broadcasted_iota(jnp.int32, (CH, CH), 0)
    cols = lax.broadcasted_iota(jnp.int32, (CH, CH), 1)
    spread = jnp.broadcast_to(vector, (CH, CH))
    return jnp.sum(jnp.where(rows == cols, spread, 0.0), axis=1, keepdims=True)


def block_kernel(
    n_dp,
    n_space,
    x_hbm,
    g_hbm,
    w1_hbm,
    b1_hbm,
    w2_hbm,
    b2_hbm,
    nb_hbm,
    rule_hbm,
    out_hbm,
    gin_hbm,
    gw1_ref,
    gb1_ref,
    gw2_ref,
    gb2_ref,
    x_v,
    g_v,
    w1_ref,
    b1_ref,
    w2_ref,
    b2_ref,
    nb_ref,
    rule_ref,
    dpre_v,
    out_v,
    gin_v,
    ex_v,
    ea_v,
    gs2_v,
    gs1_v,
    y_fwd,
    y_two,
    y_one,
    fwd_send,
    fwd_recv,
    tap_send,
    tap_recv,
    adj_send,
    adj_recv,
    part,
    buf_core,
    sum_core,
    buf_y,
    sum_y,
    buf_z,
    buf_x,
    load_sem,
    store_sem,
    halo_ssem,
    halo_rsem,
    red_ssem,
    red_rsem,
):
    hop = n_space // 4
    n_y, n_x, n_z = n_dp // 2, 4, n_space // 4
    rows_dev = CH // n_dp
    rows_pad = (rows_dev + 7) // 8 * 8
    me = lax.axis_index("space")
    my_dp = lax.axis_index("dp")
    core = lax.rem(me, 2)
    my_x = lax.div(me, hop)
    my_y, z_lo = lax.div(my_dp, 2), lax.rem(my_dp, 2)
    my_z = lax.div(lax.rem(me, hop), 2) * 2 + z_lo
    offsets = (-1, hop, 1, -hop)
    toward = [lax.rem(me + off + n_space, n_space) for off in offsets]
    reader = [lax.rem(me - off + n_space, n_space) for off in offsets]

    loads = [
        pltpu.make_async_copy(src, dst, load_sem.at[i])
        for i, (src, dst) in enumerate(
            (
                (nb_hbm, nb_ref),
                (rule_hbm, rule_ref),
                (x_hbm.at[0, 0], x_v),
                (g_hbm.at[0, 0], g_v),
                (w1_hbm, w1_ref),
                (w2_hbm, w2_ref),
                (b1_hbm, b1_ref),
                (b2_hbm, b2_ref),
            )
        )
    ]
    load_nb, load_rule, load_x, load_g, load_w1, load_w2, load_b1, load_b2 = loads

    core_peer = {"space": me + 1 - 2 * core}
    y_at = [lax.rem(my_y + s, n_y) for s in range(1, n_y)]
    y_peers = [{"dp": y * 2 + z_lo} for y in y_at]
    z_at = [lax.rem(my_z + s, n_z) for s in range(1, n_z)]
    z_peers = [
        {
            "dp": my_y * 2 + lax.rem(z, 2),
            "space": my_x * hop + lax.div(z, 2) * 2 + core,
        }
        for z in z_at
    ]
    in_x = lax.rem(me, hop)
    x_peers = [
        {"space": lax.rem(my_x + s, n_x) * hop + in_x + other * (1 - 2 * core)}
        for s in range(n_x)
        for other in range(2)
        if s or other
    ]

    barrier = pltpu.get_barrier_semaphore()
    everyone = [{"space": dev} for dev in toward] + [core_peer] + y_peers + z_peers + x_peers
    for dev in everyone:
        pl.semaphore_signal(barrier, inc=1, device_id=dev, device_id_type=MESH)
    for copy in loads:
        copy.start()

    lane = lax.broadcasted_iota(jnp.int32, (CH, LANES), 1)
    low = lane < 64
    first_col = (lane & 63) == 0
    last_col = (lane & 63) == 63
    edge_col = first_col | last_col
    zero = jnp.zeros((CH, LANES), F32)

    def remote(src, dst, ssem, rsem, device):
        return pltpu.make_async_remote_copy(
            src_ref=src,
            dst_ref=dst,
            send_sem=ssem,
            recv_sem=rsem,
            device_id=device,
            device_id_type=MESH,
        )

    def halo_copy(sends, recvs, slot, edge, dev):
        at = slot * 4 + edge
        return remote(
            sends.at[edge], recvs.at[edge], halo_ssem.at[at], halo_rsem.at[at], {"space": dev}
        )

    load_nb.wait()
    load_rule.wait()
    fwd_line = [nb_ref[1, e, reader[e]] for e in range(4)]
    fwd_turn = [nb_ref[2, e, reader[e]] for e in range(4)]
    own_line = [nb_ref[1, e, me] for e in range(4)]
    own_turn = [nb_ref[2, e, me] for e in range(4)]
    fwd_movers = [mover(e, fwd_line[e], fwd_turn[e]) for e in range(4)]

    def lines_of(group_of):
        rows = jnp.where(low, group_of(0), group_of(GROUPS - 1))
        cols = [zero, zero, zero, zero]
        for v in range(GROUPS):
            cols[v % 4] = cols[v % 4] + roll(jnp.where(edge_col, group_of(v), 0.0), 2 * v)
        cols = (cols[0] + cols[1]) + (cols[2] + cols[3])
        return rows.astype(BF16), cols.astype(BF16)

    def line_of(lines, edge):
        return jnp.where((fwd_line[edge] & 1) == 1, lines[1], lines[0])

    def forward_messages(lines, sends):
        for e in range(4):
            sends[e] = dot(line_of(lines, e), fwd_movers[e], ((1,), (0,))).astype(BF16)

    rules = [rule_ref[c, me] for c in range(4)]
    rule_at = jnp.where(
        lane == 64,
        rules[0],
        jnp.where(lane == 127, rules[1], jnp.where(lane == 0, rules[2], rules[3])),
    )
    first_weight = jnp.where(rule_at == 0, 1.0, jnp.where(rule_at == 1, 0.0, 0.5))
    corner_first = [jnp.where(r == 0, 1.0, jnp.where(r == 1, 0.0, 0.5)) for r in rules]
    end_weights = (
        (corner_first[0], corner_first[1]),
        (1.0 - corner_first[1], 1.0 - corner_first[3]),
        (corner_first[2], corner_first[3]),
        (1.0 - corner_first[0], 1.0 - corner_first[2]),
    )

    def tap_messages(lines, sends):
        for e in range(4):
            for s in range(3):
                move = shifted_mover(
                    e, own_line[e], own_turn[e], s, end_weights[e][0 if s == 0 else 1]
                )
                sends[e, s * CH : (s + 1) * CH, :] = dot(
                    lines[e % 2], move, ((1,), (0,))
                ).astype(BF16)

    def fill_inner(padded, v, here):
        padded[0:CH, grp(v)] = jnp.where(first_col, 0.0, roll(here, 1)).astype(BF16)
        padded[CH : 2 * CH, grp(v)] = here.astype(BF16)
        padded[2 * CH : K3, grp(v)] = jnp.where(last_col, 0.0, roll(here, -1)).astype(BF16)

    def fill_halo(padded, recvs):
        spread = recvs[1].astype(F32) + recvs[3].astype(F32)
        outer = recvs[0].astype(F32) + recvs[2].astype(F32)
        second = jnp.where(low, roll(spread, 2), roll(spread, 64))
        mean = ((outer + second) * 0.5).astype(BF16).astype(F32)
        corners = jnp.where(rule_at == 0, outer, jnp.where(rule_at == 1, second, mean))
        fill_inner(padded, EXTRA, outer)
        for v in range(GROUPS + 1):
            sides = (corners if v == EXTRA else roll(spread, -2 * v)).astype(BF16)
            padded[0:CH, grp(v)] = jnp.where(first_col, sides, padded[0:CH, grp(v)])
            padded[2 * CH : K3, grp(v)] = jnp.where(last_col, sides, padded[2 * CH : K3, grp(v)])

    def stacked(w_ref, tap_of):
        return jnp.concatenate(
            [
                jnp.concatenate([w_ref[tap_of(i, j)] for j in range(3)], axis=1)
                for i in range(3)
            ],
            axis=0,
        )

    def conv(weights, padded, y_ref):
        y_ref[...] = dot(weights, padded[0:K3, :], ((1,), (0,)))

    def conv_group(y_ref, v):
        prev = EXTRA if v == 0 else v - 1
        both = jnp.where(
            low,
            y_ref[0:CH, grp(v)] + y_ref[2 * CH : K3, grp(v + 1)],
            y_ref[2 * CH : K3, grp(v)] + y_ref[0:CH, grp(prev)],
        )
        return y_ref[CH : 2 * CH, grp(v)] + roll(both, 64)

    def stack_rows(grad_v, gs_ref):
        turned = None
        for v in range(GROUPS + 1):
            before = turned
            if v == EXTRA:
                gs_ref[CH : 2 * CH, grp(v)] = zero.astype(BF16)
                gs_ref[2 * CH : K3, grp(v)] = jnp.where(low, before, 0.0).astype(BF16)
                gs_ref[0:CH, grp(v - 1)] = jnp.where(low, before, 0.0).astype(BF16)
                gs_ref[0:CH, grp(v)] = jnp.where(
                    low, 0.0, roll(grad_v[:, grp(0)].astype(F32), 64)
                ).astype(BF16)
                continue
            here = grad_v[:, grp(v)]
            turned = roll(here.astype(F32), 64)
            gs_ref[CH : 2 * CH, grp(v)] = here
            gs_ref[2 * CH : K3, grp(v)] = jnp.where(
                low, 0.0 if v == 0 else before, turned
            ).astype(BF16)
            if v > 0:
                gs_ref[0:CH, grp(v - 1)] = jnp.where(low, before, turned).astype(BF16)

    def transpose_conv(weights, gs_ref, y_ref):
        y_ref[...] = dot(weights, gs_ref[...], ((0,), (0,)))

    def inner_group(y_ref, v):
        left = jnp.where(last_col, 0.0, roll(y_ref[0:CH, grp(v)], -1))
        right = jnp.where(first_col, 0.0, roll(y_ref[2 * CH : K3, grp(v)], 1))
        return y_ref[CH : 2 * CH, grp(v)] + (left + right)

    def adjoint_messages(y_ref, sends):
        def sides(v):
            return jnp.where(
                edge_col,
                jnp.where(last_col, y_ref[2 * CH : K3, grp(v)], y_ref[0:CH, grp(v)]),
                0.0,
            )

        cols = [zero, zero, zero, zero]
        for v in range(GROUPS):
            cols[v % 4] = cols[v % 4] + roll(sides(v), 2 * v)
        corners = sides(EXTRA)
        firsts = first_weight * corners
        seconds = corners - firsts
        cols = (
            (cols[0] + cols[1])
            + (cols[2] + cols[3])
            + roll(jnp.where(low, seconds, 0.0), -2)
            + roll(jnp.where(low, 0.0, seconds), 64)
        ).astype(BF16)
        rows = (inner_group(y_ref, EXTRA) + firsts).astype(BF16)
        for e in range(4):
            move = mover(e, own_line[e], own_turn[e])
            source = cols if e % 2 else rows
            sends[e] = dot(source, move, ((1,), (1,))).astype(BF16)

    def returned_lines(messages):
        rows, cols = zero, zero
        for e in range(4):
            is_col = (fwd_line[e] & 1) == 1
            rows = rows + jnp.where(is_col, 0.0, messages[e])
            cols = cols + jnp.where(is_col, messages[e], 0.0)
        return rows, cols

    def pulled_back(y_ref, rows, cols, v):
        total = inner_group(y_ref, v) + jnp.where(edge_col, roll(cols, -2 * v), 0.0)
        if v == 0:
            total = total + jnp.where(low, rows, 0.0)
        if v == GROUPS - 1:
            total = total + jnp.where(low, 0.0, rows)
        return total

    def put_part(grads, which):
        for d in range(n_dp):
            for a in range(3):
                at = a * CH + d * rows_dev
                to = a * rows_pad
                part[which, d, to : to + rows_dev, :] = grads[at : at + rows_dev, 0:LANES]
                part[
                    which, d, 3 * rows_pad : 3 * rows_pad + rows_dev, a * 32 : a * 32 + 32
                ] = grads[at : at + rows_dev, LANES : LANES + 32]

    def x_group(v):
        return x_v[:, grp(v)].astype(F32)

    def g_group(v):
        return g_v[:, grp(v)].astype(F32)

    def act_group(v):
        return ea_v[CH : 2 * CH, grp(v)].astype(F32)

    load_x.wait()
    forward_messages(lines_of(x_group), fwd_send.at[0])
    load_g.wait()
    tap_messages(lines_of(g_group), tap_send)
    pl.semaphore_wait(barrier, len(everyone))
    in_fwd = [halo_copy(fwd_send.at[0], fwd_recv.at[0], 0, e, reader[e]) for e in range(4)]
    two_tap = [halo_copy(tap_send, tap_recv, 1, e, toward[e]) for e in range(4)]
    for copy in in_fwd + two_tap:
        copy.start()

    part[...] = jnp.zeros(part.shape, F32)
    ex_v[K3 : K3 + 16, :] = jnp.ones((16, WIDE), BF16)
    ea_v[K3 : K3 + 16, :] = jnp.ones((16, WIDE), BF16)
    for v in range(GROUPS):
        fill_inner(ex_v, v, x_group(v))
    stack_rows(g_v, gs2_v)
    for copy in (load_w1, load_w2, load_b1, load_b2):
        copy.wait()
    w_one = stacked(w1_ref, lambda i, j: 3 * i + j)
    w_two = stacked(w2_ref, lambda i, j: 3 * i + j)
    w_two_by_col = stacked(w2_ref, lambda i, j: 3 * j + i)
    bias_one = jnp.broadcast_to(column(b1_ref[...].reshape(1, CH)), (CH, LANES))
    bias_two = jnp.broadcast_to(column(b2_ref[...].reshape(1, CH)), (CH, LANES))
    transpose_conv(w_two, gs2_v, y_two)

    for copy in in_fwd:
        copy.wait_recv()
    fill_halo(ex_v, fwd_recv.at[0])
    conv(w_one, ex_v, y_fwd)
    for copy in two_tap:
        copy.wait_recv()
    edge_weights = (
        w_two_by_col[:, 0:CH],
        w_two[:, 2 * CH : K3],
        w_two_by_col[:, 2 * CH : K3],
        w_two[:, 0:CH],
    )
    rows, cols = returned_lines(
        [dot(edge_weights[e], tap_recv[e], ((0,), (0,))) for e in range(4)]
    )
    for v in range(GROUPS):
        pre = conv_group(y_fwd, v) + bias_one
        square = pre * pre
        th = jnp.tanh(ROOT * (pre + 0.044715 * (square * pre)))
        cdf = 0.5 * (1.0 + th)
        fill_inner(ea_v, v, (pre * cdf).astype(BF16).astype(F32))
        slope = cdf + (0.5 * pre) * (1.0 - th * th) * (ROOT * (1.0 + (3.0 * 0.044715) * square))
        dpre_v[:, grp(v)] = (pulled_back(y_two, rows, cols, v) * slope).astype(BF16)

    act_lines = lines_of(act_group)
    forward_messages(act_lines, fwd_send.at[1])
    act_fwd = [halo_copy(fwd_send.at[1], fwd_recv.at[1], 2, e, reader[e]) for e in range(4)]
    for copy in act_fwd:
        copy.start()

    inner = slice(0, GROUPS * LANES)
    by_edge = [dot(tap_recv[e], line_of(act_lines, e), ((1,), (1,))) for e in range(4)]
    tail = jnp.zeros((CH, CH), F32)

    def halo_blocks(i):
        blocks = [tail, tail, tail]
        if i != 1:
            blocks = [by_edge[i][b * CH : (b + 1) * CH] for b in range(3)]
        blocks[0] = blocks[0] + by_edge[3][i * CH : (i + 1) * CH]
        blocks[2] = blocks[2] + by_edge[1][i * CH : (i + 1) * CH]
        return jnp.concatenate(blocks + [jnp.zeros((CH, 16), F32)], axis=1)

    halo_two = jnp.concatenate([halo_blocks(i) for i in range(3)], axis=0)
    put_part(dot(gs2_v[:, inner], ea_v[:, inner], ((1,), (1,))) + halo_two, 1)
    stack_rows(dpre_v, gs1_v)
    put_part(dot(gs1_v[...], ex_v[...], ((1,), (1,))), 0)
    core_copy = remote(
        part.at[1 - core], buf_core, red_ssem.at[0], red_rsem.at[0], core_peer
    )
    core_copy.start()

    transpose_conv(w_one, gs1_v, y_one)
    adjoint_messages(y_one, adj_send)
    one_adj = [halo_copy(adj_send, adj_recv, 3, e, toward[e]) for e in range(4)]
    for copy in one_adj:
        copy.start()

    core_copy.wait_recv()
    for d in range(n_dp):
        sum_core[d] = part[core, d] + buf_core[d]
    y_copies = [
        remote(
            sum_core.at[pl.ds(y * 2, 2)],
            buf_y.at[my_y],
            red_ssem.at[1 + s],
            red_rsem.at[1 + s],
            y_peers[s],
        )
        for s, y in enumerate(y_at)
    ]
    for copy in y_copies:
        copy.start()
    buf_y[my_y] = sum_core[pl.ds(my_y * 2, 2)]

    for copy in act_fwd:
        copy.wait_recv()
    fill_halo(ea_v, fwd_recv.at[1])
    conv(w_two, ea_v, y_fwd)
    for v in range(GROUPS):
        out_v[:, grp(v)] = (x_group(v) + conv_group(y_fwd, v) + bias_two).astype(BF16)
    store_out = pltpu.make_async_copy(out_v, out_hbm.at[0, 0], store_sem.at[0])
    store_out.start()

    def summed(buf, count):
        total = buf[0]
        for s in range(1, count):
            total = total + buf[s]
        return total

    for copy in y_copies:
        copy.wait_recv()
    sum_y[...] = summed(buf_y, n_y)
    at = n_y
    z_copies = [
        remote(
            sum_y.at[lax.rem(z, 2)],
            buf_z.at[my_z],
            red_ssem.at[at + s],
            red_rsem.at[at + s],
            z_peers[s],
        )
        for s, z in enumerate(z_at)
    ]
    for copy in z_copies:
        copy.start()
    buf_z[my_z] = sum_y[z_lo]

    for copy in one_adj:
        copy.wait_recv()
    rows, cols = returned_lines([adj_recv[e].astype(F32) for e in range(4)])
    for v in range(GROUPS):
        gin_v[:, grp(v)] = (g_group(v) + pulled_back(y_one, rows, cols, v)).astype(BF16)
    store_gin = pltpu.make_async_copy(gin_v, gin_hbm.at[0, 0], store_sem.at[1])
    store_gin.start()

    for copy in z_copies:
        copy.wait_recv()
    buf_x[core, my_x] = summed(buf_z, n_z)
    at = n_y + n_z - 1
    x_copies = [
        remote(
            buf_x.at[core, my_x],
            buf_x.at[core, my_x],
            red_ssem.at[at + s],
            red_rsem.at[at + s],
            dev,
        )
        for s, dev in enumerate(x_peers)
    ]
    for copy in x_copies:
        copy.start()
    for copy in x_copies:
        copy.wait_recv()

    for which, gw_ref, gb_ref in ((0, gw1_ref, gb1_ref), (1, gw2_ref, gb2_ref)):
        total = summed(buf_x.at[which], n_x)
        for a in range(3):
            full = jnp.concatenate(
                [
                    total[a * rows_pad : a * rows_pad + rows_dev],
                    total[3 * rows_pad : 3 * rows_pad + rows_dev, a * 32 : a * 32 + 32],
                ],
                axis=1,
            )
            for b in range(3):
                gw_ref[3 * a + b] = full[:, b * CH : (b + 1) * CH]
            if a == 1:
                eye_r = lax.broadcasted_iota(jnp.int32, (rows_dev, rows_dev), 0)
                eye_c = lax.broadcasted_iota(jnp.int32, (rows_dev, rows_dev), 1)
                spread = jnp.broadcast_to(full[:, K3 : K3 + 1], (rows_dev, rows_dev))
                gb_ref[...] = jnp.sum(jnp.where(eye_r == eye_c, spread, 0.0), axis=0)

    for copy in in_fwd + two_tap + act_fwd + one_adj + [core_copy]:
        copy.wait_send()
    for copy in y_copies + z_copies + x_copies:
        copy.wait_send()
    store_out.wait()
    store_gin.wait()


def write_kernel(count, *refs):
    sources, results, sem = refs[:count], refs[count : 2 * count], refs[2 * count]
    copies = [
        pltpu.make_async_copy(src, dst, sem.at[i])
        for i, (src, dst) in enumerate(zip(sources, results))
    ]
    for copy in copies:
        copy.start()
    for copy in copies:
        copy.wait()


def on_device(n_dp, n_space, x, g, w1, b1, w2, b2, neighbours, corner_rule):
    rows_dev = CH // n_dp
    rows_pad = (rows_dev + 7) // 8 * 8
    n_y, n_x, n_z = n_dp // 2, 4, n_space // 4
    share = (4 * rows_pad, LANES)
    field = x.shape
    shapes = (
        jax.ShapeDtypeStruct(field, BF16),
        jax.ShapeDtypeStruct(field, BF16),
        jax.ShapeDtypeStruct((9, rows_dev, CH), F32),
        jax.ShapeDtypeStruct((rows_dev,), F32),
        jax.ShapeDtypeStruct((9, rows_dev, CH), F32),
        jax.ShapeDtypeStruct((rows_dev,), F32),
    )
    anywhere = pl.BlockSpec(memory_space=pl.ANY)
    hbm = pl.BlockSpec(memory_space=pltpu.HBM)
    vmem = pl.BlockSpec(memory_space=pltpu.VMEM)
    dma = pltpu.SemaphoreType.DMA
    tile = (CH, GROUPS * LANES)
    reductions = 1 + (n_y - 1) + (n_z - 1) + (2 * n_x - 1)
    results = pl.pallas_call(
        functools.partial(block_kernel, n_dp, n_space),
        out_shape=shapes,
        in_specs=[hbm] * 8,
        out_specs=(anywhere, anywhere, vmem, vmem, vmem, vmem),
        scratch_shapes=[
            pltpu.VMEM(tile, BF16),
            pltpu.VMEM(tile, BF16),
            pltpu.VMEM((9, CH, CH), BF16),
            pltpu.VMEM((CH,), F32),
            pltpu.VMEM((9, CH, CH), BF16),
            pltpu.VMEM((CH,), F32),
            pltpu.SMEM((3, 4, n_space), jnp.int32),
            pltpu.SMEM((4, n_space), jnp.int32),
            pltpu.VMEM(tile, BF16),
            pltpu.VMEM(tile, BF16),
            pltpu.VMEM(tile, BF16),
            pltpu.VMEM((K3 + 16, WIDE), BF16),
            pltpu.VMEM((K3 + 16, WIDE), BF16),
            pltpu.VMEM((K3, WIDE), BF16),
            pltpu.VMEM((K3, WIDE), BF16),
            pltpu.VMEM((K3, WIDE), F32),
            pltpu.VMEM((K3, WIDE), F32),
            pltpu.VMEM((K3, WIDE), F32),
            pltpu.VMEM((2, 4, CH, LANES), BF16),
            pltpu.VMEM((2, 4, CH, LANES), BF16),
            pltpu.VMEM((4, K3, LANES), BF16),
            pltpu.VMEM((4, K3, LANES), BF16),
            pltpu.VMEM((4, CH, LANES), BF16),
            pltpu.VMEM((4, CH, LANES), BF16),
            pltpu.VMEM((2, n_dp) + share, F32),
            pltpu.VMEM((n_dp,) + share, F32),
            pltpu.VMEM((n_dp,) + share, F32),
            pltpu.VMEM((n_y, 2) + share, F32),
            pltpu.VMEM((2,) + share, F32),
            pltpu.VMEM((n_z,) + share, F32),
            pltpu.VMEM((2, n_x) + share, F32),
            dma((8,)),
            dma((2,)),
            dma((16,)),
            dma((16,)),
            dma((reductions,)),
            dma((reductions,)),
        ],
        compiler_params=pltpu.CompilerParams(
            collective_id=0, has_side_effects=True, vmem_limit_bytes=63 << 20
        ),
        name="unet_block",
    )(x, g, w1, b1, w2, b2, neighbours.transpose(2, 1, 0), corner_rule.T)
    return pl.pallas_call(
        functools.partial(write_kernel, len(shapes)),
        out_shape=shapes,
        in_specs=[anywhere] * len(shapes),
        out_specs=(hbm,) * len(shapes),
        scratch_shapes=[dma((len(shapes),))],
        name="write_results",
    )(*results)


def solution(mesh):
    tiled = P("dp", "space", None, None)
    return jax.shard_map(
        functools.partial(on_device, mesh.shape["dp"], mesh.shape["space"]),
        mesh=mesh,
        in_specs=(tiled, tiled, P(), P(), P(), P(), P(), P()),
        out_specs=(tiled, tiled, P(None, "dp", None), P("dp"), P(None, "dp", None), P("dp")),
        check_vma=False,
    )
```

```python
import functools
import math

import jax
import jax.numpy as jnp
from jax import lax
from jax.experimental import pallas as pl
from jax.experimental.pallas import tpu as pltpu
from jax.sharding import PartitionSpec as P

MESH = pl.DeviceIdType.MESH
F32 = jnp.float32
BF16 = jnp.bfloat16
LANES = 128
CH = 48
SIDE = 64
GROUPS = 32
EXTRA = 32
WIDE = (GROUPS + 1) * LANES
K3 = 3 * CH
ROOT = math.sqrt(2.0 / math.pi)


def grp(v):
    return slice(v * LANES, (v + 1) * LANES)


def roll(values, shift):
    shift = shift % LANES
    return pltpu.roll(values, shift, 1) if shift else values


def dot(a, b, dims):
    return lax.dot_general(a, b, (dims, ((), ())), preferred_element_type=F32)


def line_lane(edge, q):
    odd = (q & 1) == 1
    col_left = jnp.where(odd, q + 63, q)
    col_right = jnp.where(odd, (q + 126) & 127, q + 63)
    return jnp.where(
        edge == 0, q, jnp.where(edge == 2, q + 64, jnp.where(edge == 3, col_left, col_right))
    )


def halo_index(edge, lane):
    if edge == 0:
        return jnp.where(lane >= 64, lane - 64, -1000)
    if edge == 2:
        return jnp.where(lane < 64, lane, -1000)
    even = (lane & 1) == 0
    if edge == 3:
        return jnp.where(even, jnp.where(lane < 64, lane, lane - 63), -1000)
    return jnp.where(even, -1000, jnp.where(lane == 127, 1, jnp.where(lane >= 63, lane - 63, lane + 2)))


def line_index(line, lane):
    even = (lane & 1) == 0
    row = jnp.where(line == 0, lane, lane - 64)
    row = jnp.where((row >= 0) & (row < 64), row, -1000)
    left = jnp.where(even, jnp.where(lane < 64, lane, lane - 63), -1000)
    right = jnp.where(
        even, -1000, jnp.where(lane == 127, 1, jnp.where(lane >= 63, lane - 63, lane + 2))
    )
    return jnp.where((line & 1) == 0, row, jnp.where(line == 3, left, right))


def shifted_mover(edge, line, rotation, shift, end_weight):
    lane = lax.broadcasted_iota(jnp.int32, (8, LANES), 1)
    p = line_index(line, lane)
    q = jnp.where((rotation == 1) | (rotation == 2), 63 - p, p)
    valid = p >= 0
    tap = q + 1 - shift
    source = jnp.where(valid & (tap >= 0) & (tap < 64), line_lane(edge, tap), -1)
    rows = lax.broadcasted_iota(jnp.int32, (LANES, LANES), 0)
    table = jnp.where(rows == jnp.broadcast_to(source[0:1], (LANES, LANES)), 1.0, 0.0)
    if shift != 1:
        end = 0 if shift == 0 else 63
        corner = jnp.where(valid & (q == end), line_lane(edge, q), -1)
        table = table + jnp.where(
            rows == jnp.broadcast_to(corner[0:1], (LANES, LANES)), end_weight, 0.0
        )
    return table.astype(BF16)


def mover(edge, line, rotation):
    lane = lax.broadcasted_iota(jnp.int32, (8, LANES), 1)
    q = halo_index(edge, lane)
    turned = jnp.where((rotation == 1) | (rotation == 2), 63 - q, q)
    source = jnp.where(q < 0, -1, line_lane(line, turned))
    rows = lax.broadcasted_iota(jnp.int32, (LANES, LANES), 0)
    return jnp.where(rows == jnp.broadcast_to(source[0:1], (LANES, LANES)), 1.0, 0.0).astype(BF16)


def column(vector):
    rows = lax.broadcasted_iota(jnp.int32, (CH, CH), 0)
    cols = lax.broadcasted_iota(jnp.int32, (CH, CH), 1)
    spread = jnp.broadcast_to(vector, (CH, CH))
    return jnp.sum(jnp.where(rows == cols, spread, 0.0), axis=1, keepdims=True)


def block_kernel(
    n_dp,
    n_space,
    x_hbm,
    g_hbm,
    w1_hbm,
    b1_hbm,
    w2_hbm,
    b2_hbm,
    nb_hbm,
    rule_hbm,
    out_ref,
    gin_ref,
    gw1_ref,
    gb1_ref,
    gw2_ref,
    gb2_ref,
    x_v,
    g_v,
    w1_ref,
    b1_ref,
    w2_ref,
    b2_ref,
    nb_ref,
    rule_ref,
    dpre_v,
    ex_v,
    ea_v,
    gs2_v,
    gs1_v,
    y_fwd,
    y_two,
    y_one,
    fwd_send,
    fwd_recv,
    tap_send,
    tap_recv,
    adj_send,
    adj_recv,
    part,
    buf_core,
    sum_core,
    buf_y,
    sum_y,
    buf_z,
    buf_x,
    load_sem,
    halo_ssem,
    halo_rsem,
    red_ssem,
    red_rsem,
):
    hop = n_space // 4
    n_y, n_x, n_z = n_dp // 2, 4, n_space // 4
    rows_dev = CH // n_dp
    rows_pad = (rows_dev + 7) // 8 * 8
    me = lax.axis_index("space")
    my_dp = lax.axis_index("dp")
    core = lax.rem(me, 2)
    my_x = lax.div(me, hop)
    my_y, z_lo = lax.div(my_dp, 2), lax.rem(my_dp, 2)
    my_z = lax.div(lax.rem(me, hop), 2) * 2 + z_lo
    offsets = (-1, hop, 1, -hop)
    toward = [lax.rem(me + off + n_space, n_space) for off in offsets]
    reader = [lax.rem(me - off + n_space, n_space) for off in offsets]

    loads = [
        pltpu.make_async_copy(src, dst, load_sem.at[i])
        for i, (src, dst) in enumerate(
            (
                (nb_hbm, nb_ref),
                (rule_hbm, rule_ref),
                (x_hbm.at[0, 0], x_v),
                (g_hbm.at[0, 0], g_v),
                (w1_hbm, w1_ref),
                (w2_hbm, w2_ref),
                (b1_hbm, b1_ref),
                (b2_hbm, b2_ref),
            )
        )
    ]
    load_nb, load_rule, load_x, load_g, load_w1, load_w2, load_b1, load_b2 = loads

    core_peer = {"space": me + 1 - 2 * core}
    y_at = [lax.rem(my_y + s, n_y) for s in range(1, n_y)]
    y_peers = [{"dp": y * 2 + z_lo} for y in y_at]
    z_at = [lax.rem(my_z + s, n_z) for s in range(1, n_z)]
    z_peers = [
        {
            "dp": my_y * 2 + lax.rem(z, 2),
            "space": my_x * hop + lax.div(z, 2) * 2 + core,
        }
        for z in z_at
    ]
    in_x = lax.rem(me, hop)
    x_peers = [
        {"space": lax.rem(my_x + s, n_x) * hop + in_x + other * (1 - 2 * core)}
        for s in range(n_x)
        for other in range(2)
        if s or other
    ]

    barrier = pltpu.get_barrier_semaphore()
    everyone = [{"space": dev} for dev in toward] + [core_peer] + y_peers + z_peers + x_peers
    for dev in everyone:
        pl.semaphore_signal(barrier, inc=1, device_id=dev, device_id_type=MESH)
    for copy in loads:
        copy.start()

    lane = lax.broadcasted_iota(jnp.int32, (CH, LANES), 1)
    low = lane < 64
    first_col = (lane & 63) == 0
    last_col = (lane & 63) == 63
    edge_col = first_col | last_col
    zero = jnp.zeros((CH, LANES), F32)

    def remote(src, dst, ssem, rsem, device):
        return pltpu.make_async_remote_copy(
            src_ref=src,
            dst_ref=dst,
            send_sem=ssem,
            recv_sem=rsem,
            device_id=device,
            device_id_type=MESH,
        )

    def halo_copy(sends, recvs, slot, edge, dev):
        at = slot * 4 + edge
        return remote(
            sends.at[edge], recvs.at[edge], halo_ssem.at[at], halo_rsem.at[at], {"space": dev}
        )

    load_nb.wait()
    load_rule.wait()
    fwd_line = [nb_ref[1, e, reader[e]] for e in range(4)]
    fwd_turn = [nb_ref[2, e, reader[e]] for e in range(4)]
    own_line = [nb_ref[1, e, me] for e in range(4)]
    own_turn = [nb_ref[2, e, me] for e in range(4)]
    fwd_movers = [mover(e, fwd_line[e], fwd_turn[e]) for e in range(4)]

    def lines_of(group_of):
        rows = jnp.where(low, group_of(0), group_of(GROUPS - 1))
        cols = [zero, zero, zero, zero]
        for v in range(GROUPS):
            cols[v % 4] = cols[v % 4] + roll(jnp.where(edge_col, group_of(v), 0.0), 2 * v)
        cols = (cols[0] + cols[1]) + (cols[2] + cols[3])
        return rows.astype(BF16), cols.astype(BF16)

    def line_of(lines, edge):
        return jnp.where((fwd_line[edge] & 1) == 1, lines[1], lines[0])

    def forward_messages(lines, sends):
        for e in range(4):
            sends[e] = dot(line_of(lines, e), fwd_movers[e], ((1,), (0,))).astype(BF16)

    rules = [rule_ref[c, me] for c in range(4)]
    rule_at = jnp.where(
        lane == 64,
        rules[0],
        jnp.where(lane == 127, rules[1], jnp.where(lane == 0, rules[2], rules[3])),
    )
    first_weight = jnp.where(rule_at == 0, 1.0, jnp.where(rule_at == 1, 0.0, 0.5))
    corner_first = [jnp.where(r == 0, 1.0, jnp.where(r == 1, 0.0, 0.5)) for r in rules]
    end_weights = (
        (corner_first[0], corner_first[1]),
        (1.0 - corner_first[1], 1.0 - corner_first[3]),
        (corner_first[2], corner_first[3]),
        (1.0 - corner_first[0], 1.0 - corner_first[2]),
    )

    def tap_messages(lines, sends):
        for e in range(4):
            for s in range(3):
                move = shifted_mover(
                    e, own_line[e], own_turn[e], s, end_weights[e][0 if s == 0 else 1]
                )
                sends[e, s * CH : (s + 1) * CH, :] = dot(
                    lines[e % 2], move, ((1,), (0,))
                ).astype(BF16)

    def fill_inner(padded, v, here):
        padded[0:CH, grp(v)] = jnp.where(first_col, 0.0, roll(here, 1)).astype(BF16)
        padded[CH : 2 * CH, grp(v)] = here.astype(BF16)
        padded[2 * CH : K3, grp(v)] = jnp.where(last_col, 0.0, roll(here, -1)).astype(BF16)

    def fill_halo(padded, recvs):
        spread = recvs[1].astype(F32) + recvs[3].astype(F32)
        outer = recvs[0].astype(F32) + recvs[2].astype(F32)
        second = jnp.where(low, roll(spread, 2), roll(spread, 64))
        mean = ((outer + second) * 0.5).astype(BF16).astype(F32)
        corners = jnp.where(rule_at == 0, outer, jnp.where(rule_at == 1, second, mean))
        fill_inner(padded, EXTRA, outer)
        for v in range(GROUPS + 1):
            sides = (corners if v == EXTRA else roll(spread, -2 * v)).astype(BF16)
            padded[0:CH, grp(v)] = jnp.where(first_col, sides, padded[0:CH, grp(v)])
            padded[2 * CH : K3, grp(v)] = jnp.where(last_col, sides, padded[2 * CH : K3, grp(v)])

    def stacked(w_ref, tap_of):
        return jnp.concatenate(
            [
                jnp.concatenate([w_ref[tap_of(i, j)] for j in range(3)], axis=1)
                for i in range(3)
            ],
            axis=0,
        )

    def conv(weights, padded, y_ref):
        y_ref[...] = dot(weights, padded[0:K3, :], ((1,), (0,)))

    def conv_group(y_ref, v):
        prev = EXTRA if v == 0 else v - 1
        both = jnp.where(
            low,
            y_ref[0:CH, grp(v)] + y_ref[2 * CH : K3, grp(v + 1)],
            y_ref[2 * CH : K3, grp(v)] + y_ref[0:CH, grp(prev)],
        )
        return y_ref[CH : 2 * CH, grp(v)] + roll(both, 64)

    def stack_rows(grad_v, gs_ref):
        turned = None
        for v in range(GROUPS + 1):
            before = turned
            if v == EXTRA:
                gs_ref[CH : 2 * CH, grp(v)] = zero.astype(BF16)
                gs_ref[2 * CH : K3, grp(v)] = jnp.where(low, before, 0.0).astype(BF16)
                gs_ref[0:CH, grp(v - 1)] = jnp.where(low, before, 0.0).astype(BF16)
                gs_ref[0:CH, grp(v)] = jnp.where(
                    low, 0.0, roll(grad_v[:, grp(0)].astype(F32), 64)
                ).astype(BF16)
                continue
            here = grad_v[:, grp(v)]
            turned = roll(here.astype(F32), 64)
            gs_ref[CH : 2 * CH, grp(v)] = here
            gs_ref[2 * CH : K3, grp(v)] = jnp.where(
                low, 0.0 if v == 0 else before, turned
            ).astype(BF16)
            if v > 0:
                gs_ref[0:CH, grp(v - 1)] = jnp.where(low, before, turned).astype(BF16)

    def transpose_conv(weights, gs_ref, y_ref):
        y_ref[...] = dot(weights, gs_ref[...], ((0,), (0,)))

    def inner_group(y_ref, v):
        left = jnp.where(last_col, 0.0, roll(y_ref[0:CH, grp(v)], -1))
        right = jnp.where(first_col, 0.0, roll(y_ref[2 * CH : K3, grp(v)], 1))
        return y_ref[CH : 2 * CH, grp(v)] + (left + right)

    def adjoint_messages(y_ref, sends):
        def sides(v):
            return jnp.where(
                edge_col,
                jnp.where(last_col, y_ref[2 * CH : K3, grp(v)], y_ref[0:CH, grp(v)]),
                0.0,
            )

        cols = [zero, zero, zero, zero]
        for v in range(GROUPS):
            cols[v % 4] = cols[v % 4] + roll(sides(v), 2 * v)
        corners = sides(EXTRA)
        firsts = first_weight * corners
        seconds = corners - firsts
        cols = (
            (cols[0] + cols[1])
            + (cols[2] + cols[3])
            + roll(jnp.where(low, seconds, 0.0), -2)
            + roll(jnp.where(low, 0.0, seconds), 64)
        ).astype(BF16)
        rows = (inner_group(y_ref, EXTRA) + firsts).astype(BF16)
        for e in range(4):
            move = mover(e, own_line[e], own_turn[e])
            source = cols if e % 2 else rows
            sends[e] = dot(source, move, ((1,), (1,))).astype(BF16)

    def returned_lines(messages):
        rows, cols = zero, zero
        for e in range(4):
            is_col = (fwd_line[e] & 1) == 1
            rows = rows + jnp.where(is_col, 0.0, messages[e])
            cols = cols + jnp.where(is_col, messages[e], 0.0)
        return rows, cols

    def pulled_back(y_ref, rows, cols, v):
        total = inner_group(y_ref, v) + jnp.where(edge_col, roll(cols, -2 * v), 0.0)
        if v == 0:
            total = total + jnp.where(low, rows, 0.0)
        if v == GROUPS - 1:
            total = total + jnp.where(low, 0.0, rows)
        return total

    def put_part(grads, which):
        for d in range(n_dp):
            for a in range(3):
                at = a * CH + d * rows_dev
                to = a * rows_pad
                part[which, d, to : to + rows_dev, :] = grads[at : at + rows_dev, 0:LANES]
                part[
                    which, d, 3 * rows_pad : 3 * rows_pad + rows_dev, a * 32 : a * 32 + 32
                ] = grads[at : at + rows_dev, LANES : LANES + 32]

    def x_group(v):
        return x_v[:, grp(v)].astype(F32)

    def g_group(v):
        return g_v[:, grp(v)].astype(F32)

    def act_group(v):
        return ea_v[CH : 2 * CH, grp(v)].astype(F32)

    load_x.wait()
    forward_messages(lines_of(x_group), fwd_send.at[0])
    load_g.wait()
    tap_messages(lines_of(g_group), tap_send)
    pl.semaphore_wait(barrier, len(everyone))
    in_fwd = [halo_copy(fwd_send.at[0], fwd_recv.at[0], 0, e, reader[e]) for e in range(4)]
    two_tap = [halo_copy(tap_send, tap_recv, 1, e, toward[e]) for e in range(4)]
    for copy in in_fwd + two_tap:
        copy.start()

    part[...] = jnp.zeros(part.shape, F32)
    ex_v[K3 : K3 + 16, :] = jnp.ones((16, WIDE), BF16)
    ea_v[K3 : K3 + 16, :] = jnp.ones((16, WIDE), BF16)
    for v in range(GROUPS):
        fill_inner(ex_v, v, x_group(v))
    stack_rows(g_v, gs2_v)
    for copy in (load_w1, load_w2, load_b1, load_b2):
        copy.wait()
    w_one = stacked(w1_ref, lambda i, j: 3 * i + j)
    w_two = stacked(w2_ref, lambda i, j: 3 * i + j)
    w_two_by_col = stacked(w2_ref, lambda i, j: 3 * j + i)
    bias_one = jnp.broadcast_to(column(b1_ref[...].reshape(1, CH)), (CH, LANES))
    bias_two = jnp.broadcast_to(column(b2_ref[...].reshape(1, CH)), (CH, LANES))
    transpose_conv(w_two, gs2_v, y_two)

    for copy in in_fwd:
        copy.wait_recv()
    fill_halo(ex_v, fwd_recv.at[0])
    conv(w_one, ex_v, y_fwd)
    for copy in two_tap:
        copy.wait_recv()
    edge_weights = (
        w_two_by_col[:, 0:CH],
        w_two[:, 2 * CH : K3],
        w_two_by_col[:, 2 * CH : K3],
        w_two[:, 0:CH],
    )
    rows, cols = returned_lines(
        [dot(edge_weights[e], tap_recv[e], ((0,), (0,))) for e in range(4)]
    )
    for v in range(GROUPS):
        pre = conv_group(y_fwd, v) + bias_one
        square = pre * pre
        th = jnp.tanh(ROOT * (pre + 0.044715 * (square * pre)))
        cdf = 0.5 * (1.0 + th)
        fill_inner(ea_v, v, (pre * cdf).astype(BF16).astype(F32))
        slope = cdf + (0.5 * pre) * (1.0 - th * th) * (ROOT * (1.0 + (3.0 * 0.044715) * square))
        dpre_v[:, grp(v)] = (pulled_back(y_two, rows, cols, v) * slope).astype(BF16)

    act_lines = lines_of(act_group)
    forward_messages(act_lines, fwd_send.at[1])
    act_fwd = [halo_copy(fwd_send.at[1], fwd_recv.at[1], 2, e, reader[e]) for e in range(4)]
    for copy in act_fwd:
        copy.start()

    inner = slice(0, GROUPS * LANES)
    by_edge = [dot(tap_recv[e], line_of(act_lines, e), ((1,), (1,))) for e in range(4)]
    tail = jnp.zeros((CH, CH), F32)

    def halo_blocks(i):
        blocks = [tail, tail, tail]
        if i != 1:
            blocks = [by_edge[i][b * CH : (b + 1) * CH] for b in range(3)]
        blocks[0] = blocks[0] + by_edge[3][i * CH : (i + 1) * CH]
        blocks[2] = blocks[2] + by_edge[1][i * CH : (i + 1) * CH]
        return jnp.concatenate(blocks + [jnp.zeros((CH, 16), F32)], axis=1)

    halo_two = jnp.concatenate([halo_blocks(i) for i in range(3)], axis=0)
    put_part(dot(gs2_v[:, inner], ea_v[:, inner], ((1,), (1,))) + halo_two, 1)
    stack_rows(dpre_v, gs1_v)
    put_part(dot(gs1_v[...], ex_v[...], ((1,), (1,))), 0)
    core_copy = remote(
        part.at[1 - core], buf_core, red_ssem.at[0], red_rsem.at[0], core_peer
    )
    core_copy.start()

    transpose_conv(w_one, gs1_v, y_one)
    adjoint_messages(y_one, adj_send)
    one_adj = [halo_copy(adj_send, adj_recv, 3, e, toward[e]) for e in range(4)]
    for copy in one_adj:
        copy.start()

    core_copy.wait_recv()
    for d in range(n_dp):
        sum_core[d] = part[core, d] + buf_core[d]
    y_copies = [
        remote(
            sum_core.at[pl.ds(y * 2, 2)],
            buf_y.at[my_y],
            red_ssem.at[1 + s],
            red_rsem.at[1 + s],
            y_peers[s],
        )
        for s, y in enumerate(y_at)
    ]
    for copy in y_copies:
        copy.start()
    buf_y[my_y] = sum_core[pl.ds(my_y * 2, 2)]

    for copy in act_fwd:
        copy.wait_recv()
    fill_halo(ea_v, fwd_recv.at[1])
    conv(w_two, ea_v, y_fwd)
    for v in range(GROUPS):
        out_ref[0, 0, :, grp(v)] = (x_group(v) + conv_group(y_fwd, v) + bias_two).astype(BF16)

    def summed(buf, count):
        total = buf[0]
        for s in range(1, count):
            total = total + buf[s]
        return total

    for copy in y_copies:
        copy.wait_recv()
    sum_y[...] = summed(buf_y, n_y)
    at = n_y
    z_copies = [
        remote(
            sum_y.at[lax.rem(z, 2)],
            buf_z.at[my_z],
            red_ssem.at[at + s],
            red_rsem.at[at + s],
            z_peers[s],
        )
        for s, z in enumerate(z_at)
    ]
    for copy in z_copies:
        copy.start()
    buf_z[my_z] = sum_y[z_lo]

    for copy in one_adj:
        copy.wait_recv()
    rows, cols = returned_lines([adj_recv[e].astype(F32) for e in range(4)])
    for v in range(GROUPS):
        gin_ref[0, 0, :, grp(v)] = (g_group(v) + pulled_back(y_one, rows, cols, v)).astype(BF16)

    for copy in z_copies:
        copy.wait_recv()
    buf_x[core, my_x] = summed(buf_z, n_z)
    at = n_y + n_z - 1
    x_copies = [
        remote(
            buf_x.at[core, my_x],
            buf_x.at[core, my_x],
            red_ssem.at[at + s],
            red_rsem.at[at + s],
            dev,
        )
        for s, dev in enumerate(x_peers)
    ]
    for copy in x_copies:
        copy.start()
    for copy in x_copies:
        copy.wait_recv()

    for which, gw_ref, gb_ref in ((0, gw1_ref, gb1_ref), (1, gw2_ref, gb2_ref)):
        total = summed(buf_x.at[which], n_x)
        for a in range(3):
            full = jnp.concatenate(
                [
                    total[a * rows_pad : a * rows_pad + rows_dev],
                    total[3 * rows_pad : 3 * rows_pad + rows_dev, a * 32 : a * 32 + 32],
                ],
                axis=1,
            )
            for b in range(3):
                gw_ref[3 * a + b] = full[:, b * CH : (b + 1) * CH]
            if a == 1:
                eye_r = lax.broadcasted_iota(jnp.int32, (rows_dev, rows_dev), 0)
                eye_c = lax.broadcasted_iota(jnp.int32, (rows_dev, rows_dev), 1)
                spread = jnp.broadcast_to(full[:, K3 : K3 + 1], (rows_dev, rows_dev))
                gb_ref[...] = jnp.sum(jnp.where(eye_r == eye_c, spread, 0.0), axis=0)

    for copy in in_fwd + two_tap + act_fwd + one_adj + [core_copy]:
        copy.wait_send()
    for copy in y_copies + z_copies + x_copies:
        copy.wait_send()


def write_kernel(count, *refs):
    sources, results, sem = refs[:count], refs[count : 2 * count], refs[2 * count]
    copies = [
        pltpu.make_async_copy(src, dst, sem.at[i])
        for i, (src, dst) in enumerate(zip(sources, results))
    ]
    for copy in copies:
        copy.start()
    for copy in copies:
        copy.wait()


def on_device(n_dp, n_space, x, g, w1, b1, w2, b2, neighbours, corner_rule):
    rows_dev = CH // n_dp
    rows_pad = (rows_dev + 7) // 8 * 8
    n_y, n_x, n_z = n_dp // 2, 4, n_space // 4
    share = (4 * rows_pad, LANES)
    field = x.shape
    shapes = (
        jax.ShapeDtypeStruct(field, BF16),
        jax.ShapeDtypeStruct(field, BF16),
        jax.ShapeDtypeStruct((9, rows_dev, CH), F32),
        jax.ShapeDtypeStruct((rows_dev,), F32),
        jax.ShapeDtypeStruct((9, rows_dev, CH), F32),
        jax.ShapeDtypeStruct((rows_dev,), F32),
    )
    hbm = pl.BlockSpec(memory_space=pltpu.HBM)
    vmem = pl.BlockSpec(memory_space=pltpu.VMEM)
    dma = pltpu.SemaphoreType.DMA
    tile = (CH, GROUPS * LANES)
    reductions = 1 + (n_y - 1) + (n_z - 1) + (2 * n_x - 1)
    operands = [
        pltpu.with_memory_space_constraint(leaf, pltpu.HBM)
        for leaf in (x, g, w1, b1, w2, b2, neighbours.transpose(2, 1, 0), corner_rule.T)
    ]
    results = pl.pallas_call(
        functools.partial(block_kernel, n_dp, n_space),
        out_shape=tuple(pltpu.VMEM(leaf.shape, leaf.dtype) for leaf in shapes),
        in_specs=[hbm] * 8,
        out_specs=(vmem,) * len(shapes),
        scratch_shapes=[
            pltpu.VMEM(tile, BF16),
            pltpu.VMEM(tile, BF16),
            pltpu.VMEM((9, CH, CH), BF16),
            pltpu.VMEM((CH,), F32),
            pltpu.VMEM((9, CH, CH), BF16),
            pltpu.VMEM((CH,), F32),
            pltpu.SMEM((3, 4, n_space), jnp.int32),
            pltpu.SMEM((4, n_space), jnp.int32),
            pltpu.VMEM(tile, BF16),
            pltpu.VMEM((K3 + 16, WIDE), BF16),
            pltpu.VMEM((K3 + 16, WIDE), BF16),
            pltpu.VMEM((K3, WIDE), BF16),
            pltpu.VMEM((K3, WIDE), BF16),
            pltpu.VMEM((K3, WIDE), F32),
            pltpu.VMEM((K3, WIDE), F32),
            pltpu.VMEM((K3, WIDE), F32),
            pltpu.VMEM((2, 4, CH, LANES), BF16),
            pltpu.VMEM((2, 4, CH, LANES), BF16),
            pltpu.VMEM((4, K3, LANES), BF16),
            pltpu.VMEM((4, K3, LANES), BF16),
            pltpu.VMEM((4, CH, LANES), BF16),
            pltpu.VMEM((4, CH, LANES), BF16),
            pltpu.VMEM((2, n_dp) + share, F32),
            pltpu.VMEM((n_dp,) + share, F32),
            pltpu.VMEM((n_dp,) + share, F32),
            pltpu.VMEM((n_y, 2) + share, F32),
            pltpu.VMEM((2,) + share, F32),
            pltpu.VMEM((n_z,) + share, F32),
            pltpu.VMEM((2, n_x) + share, F32),
            dma((8,)),
            dma((16,)),
            dma((16,)),
            dma((reductions,)),
            dma((reductions,)),
        ],
        compiler_params=pltpu.CompilerParams(
            collective_id=0, has_side_effects=True, vmem_limit_bytes=40 << 20
        ),
        name="unet_block",
    )(*operands)
    return pl.pallas_call(
        functools.partial(write_kernel, len(shapes)),
        out_shape=shapes,
        in_specs=[vmem] * len(shapes),
        out_specs=(hbm,) * len(shapes),
        scratch_shapes=[dma((len(shapes),))],
        name="write_results",
    )(*(pltpu.with_memory_space_constraint(leaf, pltpu.VMEM) for leaf in results))


def solution(mesh):
    tiled = P("dp", "space", None, None)
    return jax.shard_map(
        functools.partial(on_device, mesh.shape["dp"], mesh.shape["space"]),
        mesh=mesh,
        in_specs=(tiled, tiled, P(), P(), P(), P(), P(), P()),
        out_specs=(tiled, tiled, P(None, "dp", None), P("dp"), P(None, "dp", None), P("dp")),
        check_vma=False,
    )
```

```python
import functools
import math

import jax
import jax.numpy as jnp
from jax import lax
from jax.experimental import pallas as pl
from jax.experimental.pallas import tpu as pltpu
from jax.sharding import PartitionSpec as P

MESH = pl.DeviceIdType.MESH
F32 = jnp.float32
BF16 = jnp.bfloat16
LANES = 128
CH = 48
SIDE = 64
GROUPS = 32
EXTRA = 32
WIDE = (GROUPS + 1) * LANES
K3 = 3 * CH
ROOT = math.sqrt(2.0 / math.pi)


def grp(v):
    return slice(v * LANES, (v + 1) * LANES)


def roll(values, shift):
    shift = shift % LANES
    return pltpu.roll(values, shift, 1) if shift else values


def dot(a, b, dims):
    return lax.dot_general(a, b, (dims, ((), ())), preferred_element_type=F32)


def line_lane(edge, q):
    odd = (q & 1) == 1
    col_left = jnp.where(odd, q + 63, q)
    col_right = jnp.where(odd, (q + 126) & 127, q + 63)
    return jnp.where(
        edge == 0, q, jnp.where(edge == 2, q + 64, jnp.where(edge == 3, col_left, col_right))
    )


def halo_index(edge, lane):
    if edge == 0:
        return jnp.where(lane >= 64, lane - 64, -1000)
    if edge == 2:
        return jnp.where(lane < 64, lane, -1000)
    even = (lane & 1) == 0
    if edge == 3:
        return jnp.where(even, jnp.where(lane < 64, lane, lane - 63), -1000)
    return jnp.where(even, -1000, jnp.where(lane == 127, 1, jnp.where(lane >= 63, lane - 63, lane + 2)))


def line_index(line, lane):
    even = (lane & 1) == 0
    row = jnp.where(line == 0, lane, lane - 64)
    row = jnp.where((row >= 0) & (row < 64), row, -1000)
    left = jnp.where(even, jnp.where(lane < 64, lane, lane - 63), -1000)
    right = jnp.where(
        even, -1000, jnp.where(lane == 127, 1, jnp.where(lane >= 63, lane - 63, lane + 2))
    )
    return jnp.where((line & 1) == 0, row, jnp.where(line == 3, left, right))


def shifted_mover(edge, line, rotation, shift, end_weight):
    lane = lax.broadcasted_iota(jnp.int32, (8, LANES), 1)
    p = line_index(line, lane)
    q = jnp.where((rotation == 1) | (rotation == 2), 63 - p, p)
    valid = p >= 0
    tap = q + 1 - shift
    source = jnp.where(valid & (tap >= 0) & (tap < 64), line_lane(edge, tap), -1)
    rows = lax.broadcasted_iota(jnp.int32, (LANES, LANES), 0)
    table = jnp.where(rows == jnp.broadcast_to(source[0:1], (LANES, LANES)), 1.0, 0.0)
    if shift != 1:
        end = 0 if shift == 0 else 63
        corner = jnp.where(valid & (q == end), line_lane(edge, q), -1)
        table = table + jnp.where(
            rows == jnp.broadcast_to(corner[0:1], (LANES, LANES)), end_weight, 0.0
        )
    return table.astype(BF16)


def mover(edge, line, rotation):
    lane = lax.broadcasted_iota(jnp.int32, (8, LANES), 1)
    q = halo_index(edge, lane)
    turned = jnp.where((rotation == 1) | (rotation == 2), 63 - q, q)
    source = jnp.where(q < 0, -1, line_lane(line, turned))
    rows = lax.broadcasted_iota(jnp.int32, (LANES, LANES), 0)
    return jnp.where(rows == jnp.broadcast_to(source[0:1], (LANES, LANES)), 1.0, 0.0).astype(BF16)


def column(vector):
    rows = lax.broadcasted_iota(jnp.int32, (CH, CH), 0)
    cols = lax.broadcasted_iota(jnp.int32, (CH, CH), 1)
    spread = jnp.broadcast_to(vector, (CH, CH))
    return jnp.sum(jnp.where(rows == cols, spread, 0.0), axis=1, keepdims=True)


def block_kernel(
    n_dp,
    n_space,
    x_hbm,
    g_hbm,
    w1_hbm,
    b1_hbm,
    w2_hbm,
    b2_hbm,
    nb_hbm,
    rule_hbm,
    out_ref,
    gin_ref,
    gw1_ref,
    gb1_ref,
    gw2_ref,
    gb2_ref,
    x_v,
    g_v,
    w1_ref,
    b1_ref,
    w2_ref,
    b2_ref,
    nb_ref,
    rule_ref,
    dpre_v,
    ex_v,
    ea_v,
    gs2_v,
    gs1_v,
    y_fwd,
    y_two,
    y_one,
    fwd_send,
    fwd_recv,
    tap_send,
    tap_recv,
    adj_send,
    adj_recv,
    part,
    buf_core,
    sum_core,
    buf_y,
    sum_y,
    buf_z,
    buf_x,
    load_sem,
    halo_ssem,
    halo_rsem,
    red_ssem,
    red_rsem,
):
    hop = n_space // 4
    n_y, n_x, n_z = n_dp // 2, 4, n_space // 4
    rows_dev = CH // n_dp
    rows_pad = (rows_dev + 7) // 8 * 8
    me = lax.axis_index("space")
    my_dp = lax.axis_index("dp")
    core = lax.rem(me, 2)
    my_x = lax.div(me, hop)
    my_y, z_lo = lax.div(my_dp, 2), lax.rem(my_dp, 2)
    my_z = lax.div(lax.rem(me, hop), 2) * 2 + z_lo
    offsets = (-1, hop, 1, -hop)
    toward = [lax.rem(me + off + n_space, n_space) for off in offsets]
    reader = [lax.rem(me - off + n_space, n_space) for off in offsets]

    loads = [
        pltpu.make_async_copy(src, dst, load_sem.at[i])
        for i, (src, dst) in enumerate(
            (
                (nb_hbm, nb_ref),
                (rule_hbm, rule_ref),
                (x_hbm.at[0, 0], x_v),
                (g_hbm.at[0, 0], g_v),
                (w1_hbm, w1_ref),
                (w2_hbm, w2_ref),
                (b1_hbm, b1_ref),
                (b2_hbm, b2_ref),
            )
        )
    ]
    load_nb, load_rule, load_x, load_g, load_w1, load_w2, load_b1, load_b2 = loads

    core_peer = {"space": me + 1 - 2 * core}
    y_at = [lax.rem(my_y + s, n_y) for s in range(1, n_y)]
    y_peers = [{"dp": y * 2 + z_lo} for y in y_at]
    z_at = [lax.rem(my_z + s, n_z) for s in range(1, n_z)]
    z_peers = [
        {
            "dp": my_y * 2 + lax.rem(z, 2),
            "space": my_x * hop + lax.div(z, 2) * 2 + core,
        }
        for z in z_at
    ]
    in_x = lax.rem(me, hop)
    x_peers = [
        {"space": lax.rem(my_x + s, n_x) * hop + in_x + other * (1 - 2 * core)}
        for s in range(n_x)
        for other in range(2)
        if s or other
    ]

    barrier = pltpu.get_barrier_semaphore()
    everyone = [{"space": dev} for dev in toward] + [core_peer] + y_peers + z_peers + x_peers
    for dev in everyone:
        pl.semaphore_signal(barrier, inc=1, device_id=dev, device_id_type=MESH)
    for copy in loads:
        copy.start()

    lane = lax.broadcasted_iota(jnp.int32, (CH, LANES), 1)
    low = lane < 64
    first_col = (lane & 63) == 0
    last_col = (lane & 63) == 63
    edge_col = first_col | last_col
    zero = jnp.zeros((CH, LANES), F32)

    def remote(src, dst, ssem, rsem, device):
        return pltpu.make_async_remote_copy(
            src_ref=src,
            dst_ref=dst,
            send_sem=ssem,
            recv_sem=rsem,
            device_id=device,
            device_id_type=MESH,
        )

    def halo_copy(sends, recvs, slot, edge, dev):
        at = slot * 4 + edge
        return remote(
            sends.at[edge], recvs.at[edge], halo_ssem.at[at], halo_rsem.at[at], {"space": dev}
        )

    load_nb.wait()
    load_rule.wait()
    fwd_line = [nb_ref[1, e, reader[e]] for e in range(4)]
    fwd_turn = [nb_ref[2, e, reader[e]] for e in range(4)]
    own_line = [nb_ref[1, e, me] for e in range(4)]
    own_turn = [nb_ref[2, e, me] for e in range(4)]
    fwd_movers = [mover(e, fwd_line[e], fwd_turn[e]) for e in range(4)]

    def collected(values_of):
        cols = [zero, zero, zero, zero]
        for v in range(GROUPS):
            cols[v % 4] = cols[v % 4] + roll(jnp.where(edge_col, values_of(v), 0.0), 2 * v)
        return (cols[0] + cols[1]) + (cols[2] + cols[3])

    def lines_of(group_of):
        rows = jnp.where(low, group_of(0), group_of(GROUPS - 1))
        return rows.astype(BF16), collected(group_of).astype(BF16)

    def line_of(lines, edge):
        return jnp.where((fwd_line[edge] & 1) == 1, lines[1], lines[0])

    def forward_messages(lines, sends):
        for e in range(4):
            sends[e] = dot(line_of(lines, e), fwd_movers[e], ((1,), (0,))).astype(BF16)

    rules = [rule_ref[c, me] for c in range(4)]
    rule_at = jnp.where(
        lane == 64,
        rules[0],
        jnp.where(lane == 127, rules[1], jnp.where(lane == 0, rules[2], rules[3])),
    )
    first_weight = jnp.where(rule_at == 0, 1.0, jnp.where(rule_at == 1, 0.0, 0.5))
    corner_first = [jnp.where(r == 0, 1.0, jnp.where(r == 1, 0.0, 0.5)) for r in rules]
    end_weights = (
        (corner_first[0], corner_first[1]),
        (1.0 - corner_first[1], 1.0 - corner_first[3]),
        (corner_first[2], corner_first[3]),
        (1.0 - corner_first[0], 1.0 - corner_first[2]),
    )

    def tap_messages(lines, sends):
        for e in range(4):
            for s in range(3):
                move = shifted_mover(
                    e, own_line[e], own_turn[e], s, end_weights[e][0 if s == 0 else 1]
                )
                sends[e, s * CH : (s + 1) * CH, :] = dot(
                    lines[e % 2], move, ((1,), (0,))
                ).astype(BF16)

    def fill_inner(padded, v, here):
        padded[0:CH, grp(v)] = jnp.where(first_col, 0.0, roll(here, 1)).astype(BF16)
        padded[CH : 2 * CH, grp(v)] = here.astype(BF16)
        padded[2 * CH : K3, grp(v)] = jnp.where(last_col, 0.0, roll(here, -1)).astype(BF16)

    def fill_outer(padded, recvs):
        spread = recvs[1].astype(F32) + recvs[3].astype(F32)
        outer = recvs[0].astype(F32) + recvs[2].astype(F32)
        second = jnp.where(low, roll(spread, 2), roll(spread, 64))
        mean = ((outer + second) * 0.5).astype(BF16).astype(F32)
        corners = jnp.where(rule_at == 0, outer, jnp.where(rule_at == 1, second, mean))
        fill_inner(padded, EXTRA, outer)
        put_sides(padded, EXTRA, corners)
        return spread

    def put_sides(padded, v, sides):
        sides = sides.astype(BF16)
        padded[0:CH, grp(v)] = jnp.where(first_col, sides, padded[0:CH, grp(v)])
        padded[2 * CH : K3, grp(v)] = jnp.where(last_col, sides, padded[2 * CH : K3, grp(v)])

    def fill_columns(padded, spread):
        for v in range(GROUPS):
            put_sides(padded, v, roll(spread, -2 * v))

    def stacked(w_ref, tap_of):
        return jnp.concatenate(
            [
                jnp.concatenate([w_ref[tap_of(i, j)] for j in range(3)], axis=1)
                for i in range(3)
            ],
            axis=0,
        )

    odd_q = ((lane & 1) == 0) & (lane >= 64) | ((lane & 1) == 1) & ((lane < 63) | (lane == 127))

    def with_corners(rows, cols):
        to_rows = jnp.where(edge_col, jnp.where(low, cols, roll(cols, 66)), 0.0)
        near = (lane == 0) | (lane == 63)
        far = (lane == 126) | (lane == 61)
        to_cols = jnp.where(near, rows, jnp.where(far, roll(rows, 62), 0.0))
        return rows + to_rows, cols + to_cols

    def halo_share(weights, padded, spread):
        outer = dot(weights, padded[0:K3, grp(EXTRA)], ((1,), (0,)))
        rows = roll(jnp.where(low, outer[2 * CH : K3], outer[0:CH]), 64)
        left = dot(weights[:, 0:CH], spread, ((1,), (0,)))
        right = dot(weights[:, 2 * CH : K3], spread, ((1,), (0,)))
        even_lane = (lane & 1) == 0
        taps = [
            jnp.where(even_lane, left[a * CH : (a + 1) * CH], right[a * CH : (a + 1) * CH])
            for a in range(3)
        ]
        onward = jnp.where(odd_q, roll(taps[0], 64), roll(taps[0], 66))
        onward = jnp.where((lane == 0) | (lane == 63), 0.0, onward)
        back = jnp.where(odd_q, roll(taps[2], 62), roll(taps[2], 64))
        back = jnp.where((lane == 126) | (lane == 61), 0.0, back)
        return with_corners(rows, taps[1] + (onward + back))

    def gelu_and_slope(pre):
        square = pre * pre
        th = jnp.tanh(ROOT * (pre + 0.044715 * (square * pre)))
        cdf = 0.5 * (1.0 + th)
        slope = cdf + (0.5 * pre) * (1.0 - th * th) * (ROOT * (1.0 + (3.0 * 0.044715) * square))
        return (pre * cdf).astype(BF16).astype(F32), slope

    def conv(weights, padded, y_ref):
        y_ref[...] = dot(weights, padded[0:K3, :], ((1,), (0,)))

    def conv_group(y_ref, v, halo=True):
        prev = EXTRA if v == 0 else v - 1
        above, below = y_ref[0:CH, grp(v)], y_ref[2 * CH : K3, grp(v)]
        if halo or v < GROUPS - 1:
            above = above + y_ref[2 * CH : K3, grp(v + 1)]
        if halo or v > 0:
            below = below + y_ref[0:CH, grp(prev)]
        both = jnp.where(low, above, below)
        return y_ref[CH : 2 * CH, grp(v)] + roll(both, 64)

    def stack_rows(grad_v, gs_ref):
        turned = None
        for v in range(GROUPS + 1):
            before = turned
            if v == EXTRA:
                gs_ref[CH : 2 * CH, grp(v)] = zero.astype(BF16)
                gs_ref[2 * CH : K3, grp(v)] = jnp.where(low, before, 0.0).astype(BF16)
                gs_ref[0:CH, grp(v - 1)] = jnp.where(low, before, 0.0).astype(BF16)
                gs_ref[0:CH, grp(v)] = jnp.where(
                    low, 0.0, roll(grad_v[:, grp(0)].astype(F32), 64)
                ).astype(BF16)
                continue
            here = grad_v[:, grp(v)]
            turned = roll(here.astype(F32), 64)
            gs_ref[CH : 2 * CH, grp(v)] = here
            gs_ref[2 * CH : K3, grp(v)] = jnp.where(
                low, 0.0 if v == 0 else before, turned
            ).astype(BF16)
            if v > 0:
                gs_ref[0:CH, grp(v - 1)] = jnp.where(low, before, turned).astype(BF16)

    def transpose_conv(weights, gs_ref, y_ref):
        y_ref[...] = dot(weights, gs_ref[...], ((0,), (0,)))

    def inner_group(y_ref, v):
        left = jnp.where(last_col, 0.0, roll(y_ref[0:CH, grp(v)], -1))
        right = jnp.where(first_col, 0.0, roll(y_ref[2 * CH : K3, grp(v)], 1))
        return y_ref[CH : 2 * CH, grp(v)] + (left + right)

    def adjoint_messages(y_ref, sends):
        def sides(v):
            return jnp.where(
                edge_col,
                jnp.where(last_col, y_ref[2 * CH : K3, grp(v)], y_ref[0:CH, grp(v)]),
                0.0,
            )

        cols = [zero, zero, zero, zero]
        for v in range(GROUPS):
            cols[v % 4] = cols[v % 4] + roll(sides(v), 2 * v)
        corners = sides(EXTRA)
        firsts = first_weight * corners
        seconds = corners - firsts
        cols = (
            (cols[0] + cols[1])
            + (cols[2] + cols[3])
            + roll(jnp.where(low, seconds, 0.0), -2)
            + roll(jnp.where(low, 0.0, seconds), 64)
        ).astype(BF16)
        rows = (inner_group(y_ref, EXTRA) + firsts).astype(BF16)
        for e in range(4):
            move = mover(e, own_line[e], own_turn[e])
            source = cols if e % 2 else rows
            sends[e] = dot(source, move, ((1,), (1,))).astype(BF16)

    def returned_lines(messages):
        rows, cols = zero, zero
        for e in range(4):
            is_col = (fwd_line[e] & 1) == 1
            rows = rows + jnp.where(is_col, 0.0, messages[e])
            cols = cols + jnp.where(is_col, messages[e], 0.0)
        return rows, cols

    def pulled_back(y_ref, rows, cols, v):
        total = inner_group(y_ref, v) + jnp.where(edge_col, roll(cols, -2 * v), 0.0)
        if v == 0:
            total = total + jnp.where(low, rows, 0.0)
        if v == GROUPS - 1:
            total = total + jnp.where(low, 0.0, rows)
        return total

    def put_part(grads, which):
        for d in range(n_dp):
            for a in range(3):
                at = a * CH + d * rows_dev
                to = a * rows_pad
                part[which, d, to : to + rows_dev, :] = grads[at : at + rows_dev, 0:LANES]
                part[
                    which, d, 3 * rows_pad : 3 * rows_pad + rows_dev, a * 32 : a * 32 + 32
                ] = grads[at : at + rows_dev, LANES : LANES + 32]

    def x_group(v):
        return x_v[:, grp(v)].astype(F32)

    def g_group(v):
        return g_v[:, grp(v)].astype(F32)

    def act_group(v):
        return ea_v[CH : 2 * CH, grp(v)].astype(F32)

    load_x.wait()
    forward_messages(lines_of(x_group), fwd_send.at[0])
    load_g.wait()
    tap_messages(lines_of(g_group), tap_send)
    pl.semaphore_wait(barrier, len(everyone))
    in_fwd = [halo_copy(fwd_send.at[0], fwd_recv.at[0], 0, e, reader[e]) for e in range(4)]
    two_tap = [halo_copy(tap_send, tap_recv, 1, e, toward[e]) for e in range(4)]
    for copy in in_fwd + two_tap:
        copy.start()

    part[...] = jnp.zeros(part.shape, F32)
    ex_v[K3 : K3 + 16, :] = jnp.ones((16, WIDE), BF16)
    ea_v[K3 : K3 + 16, :] = jnp.ones((16, WIDE), BF16)
    for v in range(GROUPS):
        fill_inner(ex_v, v, x_group(v))
    stack_rows(g_v, gs2_v)
    for copy in (load_w1, load_w2, load_b1, load_b2):
        copy.wait()
    w_one = stacked(w1_ref, lambda i, j: 3 * i + j)
    w_two = stacked(w2_ref, lambda i, j: 3 * i + j)
    w_two_by_col = stacked(w2_ref, lambda i, j: 3 * j + i)
    bias_one = jnp.broadcast_to(column(b1_ref[...].reshape(1, CH)), (CH, LANES))
    bias_two = jnp.broadcast_to(column(b2_ref[...].reshape(1, CH)), (CH, LANES))
    transpose_conv(w_two, gs2_v, y_two)

    inner = slice(0, GROUPS * LANES)
    y_fwd[:, inner] = dot(w_one, ex_v[0:K3, inner], ((1,), (0,)))
    pre_cols = [zero, zero, zero, zero]
    back_cols = [zero, zero, zero, zero]
    ends = {}
    for v in range(GROUPS):
        pre = conv_group(y_fwd, v, halo=False) + bias_one
        back = inner_group(y_two, v)
        pre_cols[v % 4] = pre_cols[v % 4] + roll(jnp.where(edge_col, pre, 0.0), 2 * v)
        back_cols[v % 4] = back_cols[v % 4] + roll(jnp.where(edge_col, back, 0.0), 2 * v)
        if v in (0, GROUPS - 1):
            ends[v] = (pre, back)
        act, slope = gelu_and_slope(pre)
        fill_inner(ea_v, v, act)
        dpre_v[:, grp(v)] = (back * slope).astype(BF16)
    pre_rows, back_rows = [jnp.where(low, a, b) for a, b in zip(ends[0], ends[GROUPS - 1])]
    pre_cols = (pre_cols[0] + pre_cols[1]) + (pre_cols[2] + pre_cols[3])
    back_cols = (back_cols[0] + back_cols[1]) + (back_cols[2] + back_cols[3])

    for copy in in_fwd:
        copy.wait_recv()
    in_spread = fill_outer(ex_v, fwd_recv.at[0])
    more_rows, more_cols = halo_share(w_one, ex_v, in_spread.astype(BF16))
    act_rows, slope_rows = gelu_and_slope(pre_rows + more_rows)
    act_cols, slope_cols = gelu_and_slope(pre_cols + more_cols)
    for copy in two_tap:
        copy.wait_recv()
    edge_weights = (
        w_two_by_col[:, 0:CH],
        w_two[:, 2 * CH : K3],
        w_two_by_col[:, 2 * CH : K3],
        w_two[:, 0:CH],
    )
    more_rows, more_cols = with_corners(
        *returned_lines([dot(edge_weights[e], tap_recv[e], ((0,), (0,))) for e in range(4)])
    )
    dpre_rows = (back_rows + more_rows) * slope_rows
    dpre_cols = (back_cols + more_cols) * slope_cols
    act_lines = (act_rows.astype(BF16), act_cols.astype(BF16))
    forward_messages(act_lines, fwd_send.at[1])
    act_fwd = [halo_copy(fwd_send.at[1], fwd_recv.at[1], 2, e, reader[e]) for e in range(4)]
    for copy in act_fwd:
        copy.start()

    second_col, last_but_one = (lane & 63) == 1, (lane & 63) == 62
    for v in range(GROUPS):
        put = roll(act_cols, -2 * v)
        row_half = low if v == 0 else jnp.logical_not(low)
        back = jnp.where(edge_col, roll(dpre_cols, -2 * v).astype(BF16), dpre_v[:, grp(v)])
        if v in (0, GROUPS - 1):
            back = jnp.where(row_half, dpre_rows.astype(BF16), back)
            here = jnp.where(edge_col, put, act_group(v))
            fill_inner(ea_v, v, jnp.where(row_half, act_rows, here))
        else:
            for at, mask, values in (
                (0, second_col, roll(put, 1)),
                (CH, edge_col, put),
                (2 * CH, last_but_one, roll(put, -1)),
            ):
                ea_v[at : at + CH, grp(v)] = jnp.where(
                    mask, values.astype(BF16), ea_v[at : at + CH, grp(v)]
                )
        dpre_v[:, grp(v)] = back

    by_edge = [dot(tap_recv[e], line_of(act_lines, e), ((1,), (1,))) for e in range(4)]
    tail = jnp.zeros((CH, CH), F32)

    def halo_blocks(i):
        blocks = [tail, tail, tail]
        if i != 1:
            blocks = [by_edge[i][b * CH : (b + 1) * CH] for b in range(3)]
        blocks[0] = blocks[0] + by_edge[3][i * CH : (i + 1) * CH]
        blocks[2] = blocks[2] + by_edge[1][i * CH : (i + 1) * CH]
        return jnp.concatenate(blocks + [jnp.zeros((CH, 16), F32)], axis=1)

    halo_two = jnp.concatenate([halo_blocks(i) for i in range(3)], axis=0)
    put_part(dot(gs2_v[:, inner], ea_v[:, inner], ((1,), (1,))) + halo_two, 1)
    stack_rows(dpre_v, gs1_v)
    fill_columns(ex_v, in_spread)
    put_part(dot(gs1_v[...], ex_v[...], ((1,), (1,))), 0)
    core_copy = remote(part.at[1 - core], buf_core, red_ssem.at[0], red_rsem.at[0], core_peer)
    core_copy.start()

    transpose_conv(w_one, gs1_v, y_one)
    adjoint_messages(y_one, adj_send)
    one_adj = [halo_copy(adj_send, adj_recv, 3, e, toward[e]) for e in range(4)]
    for copy in one_adj:
        copy.start()

    core_copy.wait_recv()
    for d in range(n_dp):
        sum_core[d] = (part[core, d] + buf_core[d]).astype(BF16)
    y_copies = [
        remote(
            sum_core.at[pl.ds(y * 2, 2)],
            buf_y.at[my_y],
            red_ssem.at[1 + s],
            red_rsem.at[1 + s],
            y_peers[s],
        )
        for s, y in enumerate(y_at)
    ]
    for copy in y_copies:
        copy.start()
    buf_y[my_y] = sum_core[pl.ds(my_y * 2, 2)]

    for copy in act_fwd:
        copy.wait_recv()
    fill_columns(ea_v, fill_outer(ea_v, fwd_recv.at[1]))
    conv(w_two, ea_v, y_fwd)
    for v in range(GROUPS):
        out_ref[0, 0, :, grp(v)] = (x_group(v) + conv_group(y_fwd, v) + bias_two).astype(BF16)

    def summed(buf, count):
        total = buf[0].astype(F32)
        for s in range(1, count):
            total = total + buf[s].astype(F32)
        return total

    for copy in y_copies:
        copy.wait_recv()
    sum_y[...] = summed(buf_y, n_y).astype(BF16)
    at = n_y
    z_copies = [
        remote(
            sum_y.at[lax.rem(z, 2)],
            buf_z.at[my_z],
            red_ssem.at[at + s],
            red_rsem.at[at + s],
            z_peers[s],
        )
        for s, z in enumerate(z_at)
    ]
    for copy in z_copies:
        copy.start()
    buf_z[my_z] = sum_y[z_lo]

    for copy in one_adj:
        copy.wait_recv()
    rows, cols = returned_lines([adj_recv[e].astype(F32) for e in range(4)])
    for v in range(GROUPS):
        gin_ref[0, 0, :, grp(v)] = (g_group(v) + pulled_back(y_one, rows, cols, v)).astype(BF16)

    for copy in z_copies:
        copy.wait_recv()
    buf_x[core, my_x] = summed(buf_z, n_z)
    at = n_y + n_z - 1
    x_copies = [
        remote(
            buf_x.at[core, my_x],
            buf_x.at[core, my_x],
            red_ssem.at[at + s],
            red_rsem.at[at + s],
            dev,
        )
        for s, dev in enumerate(x_peers)
    ]
    for copy in x_copies:
        copy.start()
    for copy in x_copies:
        copy.wait_recv()

    for which, gw_ref, gb_ref in ((0, gw1_ref, gb1_ref), (1, gw2_ref, gb2_ref)):
        total = summed(buf_x.at[which], n_x)
        for a in range(3):
            full = jnp.concatenate(
                [
                    total[a * rows_pad : a * rows_pad + rows_dev],
                    total[3 * rows_pad : 3 * rows_pad + rows_dev, a * 32 : a * 32 + 32],
                ],
                axis=1,
            )
            for b in range(3):
                gw_ref[3 * a + b] = full[:, b * CH : (b + 1) * CH]
            if a == 1:
                eye_r = lax.broadcasted_iota(jnp.int32, (rows_dev, rows_dev), 0)
                eye_c = lax.broadcasted_iota(jnp.int32, (rows_dev, rows_dev), 1)
                spread = jnp.broadcast_to(full[:, K3 : K3 + 1], (rows_dev, rows_dev))
                gb_ref[...] = jnp.sum(jnp.where(eye_r == eye_c, spread, 0.0), axis=0)

    for copy in in_fwd + two_tap + act_fwd + one_adj + [core_copy]:
        copy.wait_send()
    for copy in y_copies + z_copies + x_copies:
        copy.wait_send()


def write_kernel(count, *refs):
    sources, results, sem = refs[:count], refs[count : 2 * count], refs[2 * count]
    copies = [
        pltpu.make_async_copy(src, dst, sem.at[i])
        for i, (src, dst) in enumerate(zip(sources, results))
    ]
    for copy in copies:
        copy.start()
    for copy in copies:
        copy.wait()


def on_device(n_dp, n_space, x, g, w1, b1, w2, b2, neighbours, corner_rule):
    rows_dev = CH // n_dp
    rows_pad = (rows_dev + 7) // 8 * 8
    n_y, n_x, n_z = n_dp // 2, 4, n_space // 4
    share = (4 * rows_pad, LANES)
    field = x.shape
    shapes = (
        jax.ShapeDtypeStruct(field, BF16),
        jax.ShapeDtypeStruct(field, BF16),
        jax.ShapeDtypeStruct((9, rows_dev, CH), F32),
        jax.ShapeDtypeStruct((rows_dev,), F32),
        jax.ShapeDtypeStruct((9, rows_dev, CH), F32),
        jax.ShapeDtypeStruct((rows_dev,), F32),
    )
    hbm = pl.BlockSpec(memory_space=pltpu.HBM)
    vmem = pl.BlockSpec(memory_space=pltpu.VMEM)
    dma = pltpu.SemaphoreType.DMA
    tile = (CH, GROUPS * LANES)
    reductions = 1 + (n_y - 1) + (n_z - 1) + (2 * n_x - 1)
    operands = [
        pltpu.with_memory_space_constraint(leaf, pltpu.HBM)
        for leaf in (x, g, w1, b1, w2, b2, neighbours.transpose(2, 1, 0), corner_rule.T)
    ]
    results = pl.pallas_call(
        functools.partial(block_kernel, n_dp, n_space),
        out_shape=tuple(pltpu.VMEM(leaf.shape, leaf.dtype) for leaf in shapes),
        in_specs=[hbm] * 8,
        out_specs=(vmem,) * len(shapes),
        scratch_shapes=[
            pltpu.VMEM(tile, BF16),
            pltpu.VMEM(tile, BF16),
            pltpu.VMEM((9, CH, CH), BF16),
            pltpu.VMEM((CH,), F32),
            pltpu.VMEM((9, CH, CH), BF16),
            pltpu.VMEM((CH,), F32),
            pltpu.SMEM((3, 4, n_space), jnp.int32),
            pltpu.SMEM((4, n_space), jnp.int32),
            pltpu.VMEM(tile, BF16),
            pltpu.VMEM((K3 + 16, WIDE), BF16),
            pltpu.VMEM((K3 + 16, WIDE), BF16),
            pltpu.VMEM((K3, WIDE), BF16),
            pltpu.VMEM((K3, WIDE), BF16),
            pltpu.VMEM((K3, WIDE), F32),
            pltpu.VMEM((K3, WIDE), F32),
            pltpu.VMEM((K3, WIDE), F32),
            pltpu.VMEM((2, 4, CH, LANES), BF16),
            pltpu.VMEM((2, 4, CH, LANES), BF16),
            pltpu.VMEM((4, K3, LANES), BF16),
            pltpu.VMEM((4, K3, LANES), BF16),
            pltpu.VMEM((4, CH, LANES), BF16),
            pltpu.VMEM((4, CH, LANES), BF16),
            pltpu.VMEM((2, n_dp) + share, F32),
            pltpu.VMEM((n_dp,) + share, F32),
            pltpu.VMEM((n_dp,) + share, BF16),
            pltpu.VMEM((n_y, 2) + share, BF16),
            pltpu.VMEM((2,) + share, BF16),
            pltpu.VMEM((n_z,) + share, BF16),
            pltpu.VMEM((2, n_x) + share, F32),
            dma((8,)),
            dma((16,)),
            dma((16,)),
            dma((reductions,)),
            dma((reductions,)),
        ],
        compiler_params=pltpu.CompilerParams(
            collective_id=0, has_side_effects=True, vmem_limit_bytes=40 << 20
        ),
        name="unet_block",
    )(*operands)
    return pl.pallas_call(
        functools.partial(write_kernel, len(shapes)),
        out_shape=shapes,
        in_specs=[vmem] * len(shapes),
        out_specs=(hbm,) * len(shapes),
        scratch_shapes=[dma((len(shapes),))],
        name="write_results",
    )(*(pltpu.with_memory_space_constraint(leaf, pltpu.VMEM) for leaf in results))


def solution(mesh):
    tiled = P("dp", "space", None, None)
    return jax.shard_map(
        functools.partial(on_device, mesh.shape["dp"], mesh.shape["space"]),
        mesh=mesh,
        in_specs=(tiled, tiled, P(), P(), P(), P(), P(), P()),
        out_specs=(tiled, tiled, P(None, "dp", None), P("dp"), P(None, "dp", None), P("dp")),
        check_vma=False,
    )
```

```python
import functools
import math

import jax
import jax.numpy as jnp
from jax import lax
from jax.experimental import pallas as pl
from jax.experimental.pallas import tpu as pltpu
from jax.sharding import PartitionSpec as P

MESH = pl.DeviceIdType.MESH
F32 = jnp.float32
BF16 = jnp.bfloat16
LANES = 128
CH = 48
SIDE = 64
GROUPS = 32
EXTRA = 32
WIDE = (GROUPS + 1) * LANES
K3 = 3 * CH
ROOT = math.sqrt(2.0 / math.pi)


def grp(v):
    return slice(v * LANES, (v + 1) * LANES)


def roll(values, shift):
    shift = shift % LANES
    return pltpu.roll(values, shift, 1) if shift else values


def dot(a, b, dims):
    return lax.dot_general(a, b, (dims, ((), ())), preferred_element_type=F32)


def line_lane(edge, q):
    odd = (q & 1) == 1
    col_left = jnp.where(odd, q + 63, q)
    col_right = jnp.where(odd, (q + 126) & 127, q + 63)
    return jnp.where(
        edge == 0, q, jnp.where(edge == 2, q + 64, jnp.where(edge == 3, col_left, col_right))
    )


def halo_index(edge, lane):
    if edge == 0:
        return jnp.where(lane >= 64, lane - 64, -1000)
    if edge == 2:
        return jnp.where(lane < 64, lane, -1000)
    even = (lane & 1) == 0
    if edge == 3:
        return jnp.where(even, jnp.where(lane < 64, lane, lane - 63), -1000)
    return jnp.where(even, -1000, jnp.where(lane == 127, 1, jnp.where(lane >= 63, lane - 63, lane + 2)))


def line_index(line, lane):
    even = (lane & 1) == 0
    row = jnp.where(line == 0, lane, lane - 64)
    row = jnp.where((row >= 0) & (row < 64), row, -1000)
    left = jnp.where(even, jnp.where(lane < 64, lane, lane - 63), -1000)
    right = jnp.where(
        even, -1000, jnp.where(lane == 127, 1, jnp.where(lane >= 63, lane - 63, lane + 2))
    )
    return jnp.where((line & 1) == 0, row, jnp.where(line == 3, left, right))


def shifted_mover(edge, line, rotation, shift, end_weight):
    lane = lax.broadcasted_iota(jnp.int32, (8, LANES), 1)
    p = line_index(line, lane)
    q = jnp.where((rotation == 1) | (rotation == 2), 63 - p, p)
    valid = p >= 0
    tap = q + 1 - shift
    source = jnp.where(valid & (tap >= 0) & (tap < 64), line_lane(edge, tap), -1)
    rows = lax.broadcasted_iota(jnp.int32, (LANES, LANES), 0)
    table = jnp.where(rows == jnp.broadcast_to(source[0:1], (LANES, LANES)), 1.0, 0.0)
    if shift != 1:
        end = 0 if shift == 0 else 63
        corner = jnp.where(valid & (q == end), line_lane(edge, q), -1)
        table = table + jnp.where(
            rows == jnp.broadcast_to(corner[0:1], (LANES, LANES)), end_weight, 0.0
        )
    return table.astype(BF16)


def mover(edge, line, rotation):
    lane = lax.broadcasted_iota(jnp.int32, (8, LANES), 1)
    q = halo_index(edge, lane)
    turned = jnp.where((rotation == 1) | (rotation == 2), 63 - q, q)
    source = jnp.where(q < 0, -1, line_lane(line, turned))
    rows = lax.broadcasted_iota(jnp.int32, (LANES, LANES), 0)
    return jnp.where(rows == jnp.broadcast_to(source[0:1], (LANES, LANES)), 1.0, 0.0).astype(BF16)


def column(vector):
    rows = lax.broadcasted_iota(jnp.int32, (CH, CH), 0)
    cols = lax.broadcasted_iota(jnp.int32, (CH, CH), 1)
    spread = jnp.broadcast_to(vector, (CH, CH))
    return jnp.sum(jnp.where(rows == cols, spread, 0.0), axis=1, keepdims=True)


def block_kernel(
    n_dp,
    n_space,
    x_hbm,
    g_hbm,
    w1_hbm,
    b1_hbm,
    w2_hbm,
    b2_hbm,
    nb_hbm,
    rule_hbm,
    out_ref,
    gin_ref,
    gw1_ref,
    gb1_ref,
    gw2_ref,
    gb2_ref,
    x_v,
    g_v,
    w1_ref,
    b1_ref,
    w2_ref,
    b2_ref,
    nb_ref,
    rule_ref,
    act_first,
    dpre_first,
    pre_v,
    back_v,
    dpre_v,
    ex_v,
    ea_v,
    gs2_v,
    gs1_v,
    y_fwd,
    y_two,
    y_one,
    fwd_send,
    fwd_recv,
    tap_send,
    tap_recv,
    tap_move,
    adj_send,
    adj_recv,
    part,
    buf_core,
    sum_core,
    buf_y,
    sum_y,
    buf_z,
    buf_x,
    load_sem,
    halo_ssem,
    halo_rsem,
    red_ssem,
    red_rsem,
    ready_sem,
):
    hop = n_space // 4
    n_y, n_x, n_z = n_dp // 2, 4, n_space // 4
    rows_dev = CH // n_dp
    rows_pad = (rows_dev + 7) // 8 * 8
    me = lax.axis_index("space")
    my_dp = lax.axis_index("dp")
    core = lax.rem(me, 2)
    my_x = lax.div(me, hop)
    my_y, z_lo = lax.div(my_dp, 2), lax.rem(my_dp, 2)
    my_z = lax.div(lax.rem(me, hop), 2) * 2 + z_lo
    offsets = (-1, hop, 1, -hop)
    toward = [lax.rem(me + off + n_space, n_space) for off in offsets]
    reader = [lax.rem(me - off + n_space, n_space) for off in offsets]

    loads = [
        pltpu.make_async_copy(src, dst, load_sem.at[i])
        for i, (src, dst) in enumerate(
            (
                (nb_hbm, nb_ref),
                (rule_hbm, rule_ref),
                (x_hbm.at[0, 0], x_v),
                (g_hbm.at[0, 0], g_v),
                (w1_hbm, w1_ref),
                (w2_hbm, w2_ref),
                (b1_hbm, b1_ref),
                (b2_hbm, b2_ref),
            )
        )
    ]
    load_nb, load_rule, load_x, load_g, load_w1, load_w2, load_b1, load_b2 = loads

    core_peer = {"space": me + 1 - 2 * core}
    y_at = [lax.rem(my_y + s, n_y) for s in range(1, n_y)]
    y_peers = [{"dp": y * 2 + z_lo} for y in y_at]
    z_at = [lax.rem(my_z + s, n_z) for s in range(1, n_z)]
    z_peers = [
        {
            "dp": my_y * 2 + lax.rem(z, 2),
            "space": my_x * hop + lax.div(z, 2) * 2 + core,
        }
        for z in z_at
    ]
    in_x = lax.rem(me, hop)
    x_peers = [
        {"space": lax.rem(my_x + s, n_x) * hop + in_x + other * (1 - 2 * core)}
        for s in range(n_x)
        for other in range(2)
        if s or other
    ]

    barrier = pltpu.get_barrier_semaphore()
    near = [{"space": dev} for dev in toward] + [core_peer]
    near += [dev for s, dev in enumerate(y_peers, 1) if s in (1, n_y - 1)]
    near += [dev for s, dev in enumerate(z_peers, 1) if s in (1, 2, n_z - 2, n_z - 1)]
    near += [{"space": lax.rem(my_x + 2, n_x) * hop + in_x}]
    for dev in near:
        pl.semaphore_signal(barrier, inc=1, device_id=dev, device_id_type=MESH)
    for copy in loads:
        copy.start()

    lane = lax.broadcasted_iota(jnp.int32, (CH, LANES), 1)
    low = lane < 64
    first_col = (lane & 63) == 0
    last_col = (lane & 63) == 63
    edge_col = first_col | last_col
    zero = jnp.zeros((CH, LANES), F32)
    blank = jnp.zeros((CH, LANES), BF16)

    def remote(src, dst, ssem, rsem, device):
        return pltpu.make_async_remote_copy(
            src_ref=src,
            dst_ref=dst,
            send_sem=ssem,
            recv_sem=rsem,
            device_id=device,
            device_id_type=MESH,
        )

    def halo_copy(sends, recvs, slot, edge, dev):
        at = slot * 4 + edge
        return remote(
            sends.at[edge], recvs.at[edge], halo_ssem.at[at], halo_rsem.at[at], {"space": dev}
        )

    load_nb.wait()
    load_rule.wait()
    fwd_line = [nb_ref[1, e, reader[e]] for e in range(4)]
    fwd_turn = [nb_ref[2, e, reader[e]] for e in range(4)]
    own_line = [nb_ref[1, e, me] for e in range(4)]
    own_turn = [nb_ref[2, e, me] for e in range(4)]
    fwd_movers = [mover(e, fwd_line[e], fwd_turn[e]) for e in range(4)]

    def collected(values_of):
        cols = [zero, zero]
        for v in range(GROUPS):
            cols[v % 2] = cols[v % 2] + roll(jnp.where(edge_col, values_of(v), 0.0), 2 * v)
        return cols[0] + cols[1]

    def lines_of(group_of):
        return [form.astype(BF16) for form in edges_of(group_of)]

    def edges_of(group_of):
        return jnp.where(low, group_of(0), group_of(GROUPS - 1)), collected(group_of)

    def line_of(lines, edge):
        return jnp.where((fwd_line[edge] & 1) == 1, lines[1], lines[0])

    def forward_messages(lines, sends):
        for e in range(4):
            sends[e] = dot(line_of(lines, e), fwd_movers[e], ((1,), (0,))).astype(BF16)

    rules = [rule_ref[c, me] for c in range(4)]
    rule_at = jnp.where(
        lane == 64,
        rules[0],
        jnp.where(lane == 127, rules[1], jnp.where(lane == 0, rules[2], rules[3])),
    )
    first_weight = jnp.where(rule_at == 0, 1.0, jnp.where(rule_at == 1, 0.0, 0.5))
    def end_weights(edge):
        ends = ((0, 1), (1, 3), (2, 3), (0, 2))[edge]
        weights = []
        for c in ends:
            rule = rule_ref[c, reader[edge]]
            first = jnp.where(rule == 0, 1.0, jnp.where(rule == 1, 0.0, 0.5))
            weights.append(1.0 - first if edge % 2 else first)
        return weights

    def tap_movers(moves):
        for e in range(4):
            first, last = end_weights(e)
            for s in range(3):
                moves[e, :, s * LANES : (s + 1) * LANES] = shifted_mover(
                    e, fwd_line[e], fwd_turn[e], s, first if s == 0 else last
                )

    def shifted_taps(lines, moves):
        wide = dot(lines, moves, ((1,), (0,))).astype(BF16)
        return jnp.concatenate([wide[:, s * LANES : (s + 1) * LANES] for s in range(3)], axis=0)

    def fill_inner(padded, v, here):
        padded[0:CH, grp(v)] = jnp.where(first_col, blank, roll(here, 1))
        padded[CH : 2 * CH, grp(v)] = here
        padded[2 * CH : K3, grp(v)] = jnp.where(last_col, blank, roll(here, -1))

    def fill_outer(padded, recvs):
        spread = recvs[1].astype(F32) + recvs[3].astype(F32)
        outer = recvs[0].astype(F32) + recvs[2].astype(F32)
        second = jnp.where(low, roll(spread, 2), roll(spread, 64))
        mean = ((outer + second) * 0.5).astype(BF16).astype(F32)
        corners = jnp.where(rule_at == 0, outer, jnp.where(rule_at == 1, second, mean))
        fill_inner(padded, EXTRA, outer.astype(BF16))
        put_sides(padded, EXTRA, corners.astype(BF16))
        return spread.astype(BF16)

    def put_sides(padded, v, sides):
        padded[0:CH, grp(v)] = jnp.where(first_col, sides, padded[0:CH, grp(v)])
        padded[2 * CH : K3, grp(v)] = jnp.where(last_col, sides, padded[2 * CH : K3, grp(v)])

    def fill_columns(padded, spread):
        for v in range(GROUPS):
            put_sides(padded, v, roll(spread, -2 * v))

    def stacked(w_ref, tap_of):
        return jnp.concatenate(
            [
                jnp.concatenate([w_ref[tap_of(i, j)] for j in range(3)], axis=1)
                for i in range(3)
            ],
            axis=0,
        )

    odd_q = ((lane & 1) == 0) & (lane >= 64) | ((lane & 1) == 1) & ((lane < 63) | (lane == 127))

    def with_corners(rows, cols):
        to_rows = jnp.where(edge_col, jnp.where(low, cols, roll(cols, 66)), 0.0)
        near = (lane == 0) | (lane == 63)
        far = (lane == 126) | (lane == 61)
        to_cols = jnp.where(near, rows, jnp.where(far, roll(rows, 62), 0.0))
        return rows + to_rows, cols + to_cols

    def halo_share(weights, padded, spread):
        outer = dot(weights, padded[0:K3, grp(EXTRA)], ((1,), (0,)))
        rows = roll(jnp.where(low, outer[2 * CH : K3], outer[0:CH]), 64)
        left = dot(weights[:, 0:CH], spread, ((1,), (0,)))
        right = dot(weights[:, 2 * CH : K3], spread, ((1,), (0,)))
        even_lane = (lane & 1) == 0
        taps = [
            jnp.where(even_lane, left[a * CH : (a + 1) * CH], right[a * CH : (a + 1) * CH])
            for a in range(3)
        ]
        onward = jnp.where(odd_q, roll(taps[0], 64), roll(taps[0], 66))
        onward = jnp.where((lane == 0) | (lane == 63), 0.0, onward)
        back = jnp.where(odd_q, roll(taps[2], 62), roll(taps[2], 64))
        back = jnp.where((lane == 126) | (lane == 61), 0.0, back)
        return with_corners(rows, taps[1] + (onward + back))

    def gelu_and_slope(pre):
        square = pre * pre
        th = jnp.tanh(ROOT * (pre + 0.044715 * (square * pre)))
        cdf = 0.5 * (1.0 + th)
        slope = cdf + (0.5 * pre) * (1.0 - th * th) * (ROOT * (1.0 + (3.0 * 0.044715) * square))
        return (pre * cdf).astype(BF16).astype(F32), slope

    def conv(weights, padded, y_ref):
        y_ref[...] = dot(weights, padded[0:K3, :], ((1,), (0,)))

    def conv_group(y_ref, v, halo=True):
        prev = EXTRA if v == 0 else v - 1
        above, below = y_ref[0:CH, grp(v)], y_ref[2 * CH : K3, grp(v)]
        if halo or v < GROUPS - 1:
            above = above + y_ref[2 * CH : K3, grp(v + 1)]
        if halo or v > 0:
            below = below + y_ref[0:CH, grp(prev)]
        both = jnp.where(low, above, below)
        return y_ref[CH : 2 * CH, grp(v)] + roll(both, 64)

    def stack_rows(grad_v, gs_ref):
        turned = None
        for v in range(GROUPS):
            before, here = turned, grad_v[:, grp(v)]
            turned = roll(here, 64)
            gs_ref[CH : 2 * CH, grp(v)] = here
            gs_ref[2 * CH : K3, grp(v)] = jnp.where(low, blank if v == 0 else before, turned)
            if v > 0:
                gs_ref[0:CH, grp(v - 1)] = jnp.where(low, before, turned)
        gs_ref[CH : 2 * CH, grp(EXTRA)] = blank
        gs_ref[2 * CH : K3, grp(EXTRA)] = jnp.where(low, turned, blank)
        gs_ref[0:CH, grp(EXTRA - 1)] = jnp.where(low, turned, blank)
        gs_ref[0:CH, grp(EXTRA)] = jnp.where(low, blank, roll(grad_v[:, grp(0)], 64))

    def transpose_conv(weights, gs_ref, y_ref):
        y_ref[...] = dot(weights, gs_ref[...], ((0,), (0,)))

    def inner_group(y_ref, v):
        left = jnp.where(last_col, 0.0, roll(y_ref[0:CH, grp(v)], -1))
        right = jnp.where(first_col, 0.0, roll(y_ref[2 * CH : K3, grp(v)], 1))
        return y_ref[CH : 2 * CH, grp(v)] + (left + right)

    def adjoint_messages(y_ref, sends):
        def sides(v):
            return jnp.where(
                edge_col,
                jnp.where(last_col, y_ref[2 * CH : K3, grp(v)], y_ref[0:CH, grp(v)]),
                0.0,
            )

        cols = [zero, zero, zero, zero]
        for v in range(GROUPS):
            cols[v % 4] = cols[v % 4] + roll(sides(v), 2 * v)
        corners = sides(EXTRA)
        firsts = first_weight * corners
        seconds = corners - firsts
        cols = (
            (cols[0] + cols[1])
            + (cols[2] + cols[3])
            + roll(jnp.where(low, seconds, 0.0), -2)
            + roll(jnp.where(low, 0.0, seconds), 64)
        ).astype(BF16)
        rows = (inner_group(y_ref, EXTRA) + firsts).astype(BF16)
        for e in range(4):
            move = mover(e, own_line[e], own_turn[e])
            source = cols if e % 2 else rows
            sends[e] = dot(source, move, ((1,), (1,))).astype(BF16)

    def returned_lines(messages):
        rows, cols = zero, zero
        for e in range(4):
            is_col = (fwd_line[e] & 1) == 1
            rows = rows + jnp.where(is_col, 0.0, messages[e])
            cols = cols + jnp.where(is_col, messages[e], 0.0)
        return rows, cols

    def pulled_back(y_ref, rows, cols, v):
        total = inner_group(y_ref, v) + jnp.where(edge_col, roll(cols, -2 * v), 0.0)
        if v == 0:
            total = total + jnp.where(low, rows, 0.0)
        if v == GROUPS - 1:
            total = total + jnp.where(low, 0.0, rows)
        return total

    def put_part(grads, which):
        for d in range(n_dp):
            for a in range(3):
                at = a * CH + d * rows_dev
                to = a * rows_pad
                part[which, d, to : to + rows_dev, :] = grads[at : at + rows_dev, 0:LANES]
                part[
                    which, d, 3 * rows_pad : 3 * rows_pad + rows_dev, a * 32 : a * 32 + 32
                ] = grads[at : at + rows_dev, LANES : LANES + 32]

    def x_group(v):
        return x_v[:, grp(v)].astype(F32)

    def g_group(v):
        return g_v[:, grp(v)].astype(F32)

    def act_group(v):
        return ea_v[CH : 2 * CH, grp(v)].astype(F32)

    load_x.wait()
    forward_messages(lines_of(x_group), fwd_send.at[0])
    load_g.wait()
    tap_send[0], tap_send[1] = lines_of(g_group)
    pl.semaphore_wait(barrier, len(near))
    in_fwd = [halo_copy(fwd_send.at[0], fwd_recv.at[0], 0, e, reader[e]) for e in range(4)]
    two_tap = [
        remote(
            tap_send.at[e % 2],
            tap_recv.at[e],
            halo_ssem.at[4 + e],
            halo_rsem.at[4 + e],
            {"space": toward[e]},
        )
        for e in range(4)
    ]
    for copy in in_fwd + two_tap:
        copy.start()

    for dev in near:
        pl.semaphore_signal(ready_sem, inc=1, device_id=dev, device_id_type=MESH)
    tap_movers(tap_move)
    part[...] = jnp.zeros(part.shape, F32)
    ex_v[K3 : K3 + 16, :] = jnp.ones((16, WIDE), BF16)
    ea_v[K3 : K3 + 16, :] = jnp.ones((16, WIDE), BF16)
    for v in range(GROUPS):
        fill_inner(ex_v, v, x_v[:, grp(v)])
    stack_rows(g_v, gs2_v)
    for copy in (load_w1, load_w2, load_b1, load_b2):
        copy.wait()
    w_one = stacked(w1_ref, lambda i, j: 3 * i + j)
    w_two = stacked(w2_ref, lambda i, j: 3 * i + j)
    w_two_by_col = stacked(w2_ref, lambda i, j: 3 * j + i)
    bias_one = jnp.broadcast_to(column(b1_ref[...].reshape(1, CH)), (CH, LANES))
    bias_two = jnp.broadcast_to(column(b2_ref[...].reshape(1, CH)), (CH, LANES))
    transpose_conv(w_two, gs2_v, y_two)

    inner = slice(0, GROUPS * LANES)
    y_fwd[:, inner] = dot(w_one, ex_v[0:K3, inner], ((1,), (0,)))
    for v in range(GROUPS):
        pre_v[:, grp(v)] = conv_group(y_fwd, v, halo=False) + bias_one
    for v in range(GROUPS):
        back_v[:, grp(v)] = inner_group(y_two, v)
    for v in range(GROUPS):
        act, slope = gelu_and_slope(pre_v[:, grp(v)])
        act_first[:, grp(v)] = act.astype(BF16)
        dpre_first[:, grp(v)] = (back_v[:, grp(v)] * slope).astype(BF16)
    pre_rows, pre_cols = edges_of(lambda v: pre_v[:, grp(v)])
    back_rows, back_cols = edges_of(lambda v: back_v[:, grp(v)])

    for copy in in_fwd + two_tap:
        copy.wait_recv()
    in_spread = fill_outer(ex_v, fwd_recv.at[0])
    more_rows, more_cols = halo_share(w_one, ex_v, in_spread)
    act_rows, slope_rows = gelu_and_slope(pre_rows + more_rows)
    act_cols, slope_cols = gelu_and_slope(pre_cols + more_cols)
    taps = [shifted_taps(tap_recv[e], tap_move[e]) for e in range(4)]
    edge_weights = (
        w_two_by_col[:, 0:CH],
        w_two[:, 2 * CH : K3],
        w_two_by_col[:, 2 * CH : K3],
        w_two[:, 0:CH],
    )
    more_rows, more_cols = with_corners(
        *returned_lines([dot(edge_weights[e], taps[e], ((0,), (0,))) for e in range(4)])
    )
    dpre_rows = (back_rows + more_rows) * slope_rows
    dpre_cols = (back_cols + more_cols) * slope_cols
    act_lines = (act_rows.astype(BF16), act_cols.astype(BF16))
    forward_messages(act_lines, fwd_send.at[1])
    act_fwd = [halo_copy(fwd_send.at[1], fwd_recv.at[1], 2, e, reader[e]) for e in range(4)]
    for copy in act_fwd:
        copy.start()

    back_lines = (dpre_rows.astype(BF16), dpre_cols.astype(BF16))
    for v in range(GROUPS):
        here = jnp.where(edge_col, roll(act_lines[1], -2 * v), act_first[:, grp(v)])
        back = jnp.where(edge_col, roll(back_lines[1], -2 * v), dpre_first[:, grp(v)])
        if v in (0, GROUPS - 1):
            row_half = low if v == 0 else jnp.logical_not(low)
            here = jnp.where(row_half, act_lines[0], here)
            back = jnp.where(row_half, back_lines[0], back)
        fill_inner(ea_v, v, here)
        dpre_v[:, grp(v)] = back

    by_edge = [dot(taps[e], line_of(act_lines, e), ((1,), (1,))) for e in range(4)]
    tail = jnp.zeros((CH, CH), F32)

    def halo_blocks(i):
        blocks = [tail, tail, tail]
        if i != 1:
            blocks = [by_edge[i][b * CH : (b + 1) * CH] for b in range(3)]
        blocks[0] = blocks[0] + by_edge[3][i * CH : (i + 1) * CH]
        blocks[2] = blocks[2] + by_edge[1][i * CH : (i + 1) * CH]
        return jnp.concatenate(blocks + [jnp.zeros((CH, 16), F32)], axis=1)

    halo_two = jnp.concatenate([halo_blocks(i) for i in range(3)], axis=0)
    put_part(dot(gs2_v[:, inner], ea_v[:, inner], ((1,), (1,))) + halo_two, 1)
    stack_rows(dpre_v, gs1_v)
    fill_columns(ex_v, in_spread)
    put_part(dot(gs1_v[...], ex_v[...], ((1,), (1,))), 0)
    core_copy = remote(part.at[1 - core], buf_core, red_ssem.at[0], red_rsem.at[0], core_peer)
    core_copy.start()

    transpose_conv(w_one, gs1_v, y_one)
    adjoint_messages(y_one, adj_send)
    one_adj = [halo_copy(adj_send, adj_recv, 3, e, toward[e]) for e in range(4)]
    for copy in one_adj:
        copy.start()

    core_copy.wait_recv()
    for d in range(n_dp):
        sum_core[d] = (part[core, d] + buf_core[d]).astype(BF16)
    y_copies = [
        remote(
            sum_core.at[pl.ds(y * 2, 2)],
            buf_y.at[my_y],
            red_ssem.at[1 + s],
            red_rsem.at[1 + s],
            y_peers[s],
        )
        for s, y in enumerate(y_at)
    ]
    pl.semaphore_wait(ready_sem, len(near))
    for copy in y_copies:
        copy.start()
    buf_y[my_y] = sum_core[pl.ds(my_y * 2, 2)]

    for copy in act_fwd:
        copy.wait_recv()
    fill_columns(ea_v, fill_outer(ea_v, fwd_recv.at[1]))
    conv(w_two, ea_v, y_fwd)
    for v in range(GROUPS):
        out_ref[0, 0, :, grp(v)] = (x_group(v) + conv_group(y_fwd, v) + bias_two).astype(BF16)

    def summed(buf, count):
        total = buf[0].astype(F32)
        for s in range(1, count):
            total = total + buf[s].astype(F32)
        return total

    for copy in y_copies:
        copy.wait_recv()
    sum_y[...] = summed(buf_y, n_y).astype(BF16)
    at = n_y
    z_copies = [
        remote(
            sum_y.at[lax.rem(z, 2)],
            buf_z.at[my_z],
            red_ssem.at[at + s],
            red_rsem.at[at + s],
            z_peers[s],
        )
        for s, z in enumerate(z_at)
    ]
    for copy in z_copies:
        copy.start()
    buf_z[my_z] = sum_y[z_lo]

    for copy in one_adj:
        copy.wait_recv()
    rows, cols = returned_lines([adj_recv[e].astype(F32) for e in range(4)])
    for v in range(GROUPS):
        gin_ref[0, 0, :, grp(v)] = (g_group(v) + pulled_back(y_one, rows, cols, v)).astype(BF16)

    for copy in z_copies:
        copy.wait_recv()
    buf_x[core, my_x] = summed(buf_z, n_z)
    at = n_y + n_z - 1
    x_copies = [
        remote(
            buf_x.at[core, my_x],
            buf_x.at[core, my_x],
            red_ssem.at[at + s],
            red_rsem.at[at + s],
            dev,
        )
        for s, dev in enumerate(x_peers)
    ]
    for copy in x_copies:
        copy.start()
    for copy in x_copies:
        copy.wait_recv()

    for which, gw_ref, gb_ref in ((0, gw1_ref, gb1_ref), (1, gw2_ref, gb2_ref)):
        total = summed(buf_x.at[which], n_x)
        for a in range(3):
            full = jnp.concatenate(
                [
                    total[a * rows_pad : a * rows_pad + rows_dev],
                    total[3 * rows_pad : 3 * rows_pad + rows_dev, a * 32 : a * 32 + 32],
                ],
                axis=1,
            )
            for b in range(3):
                gw_ref[3 * a + b] = full[:, b * CH : (b + 1) * CH]
            if a == 1:
                eye_r = lax.broadcasted_iota(jnp.int32, (rows_dev, rows_dev), 0)
                eye_c = lax.broadcasted_iota(jnp.int32, (rows_dev, rows_dev), 1)
                spread = jnp.broadcast_to(full[:, K3 : K3 + 1], (rows_dev, rows_dev))
                gb_ref[...] = jnp.sum(jnp.where(eye_r == eye_c, spread, 0.0), axis=0)

    for copy in in_fwd + two_tap + act_fwd + one_adj + [core_copy]:
        copy.wait_send()
    for copy in y_copies + z_copies + x_copies:
        copy.wait_send()


def write_kernel(count, *refs):
    sources, results, sem = refs[:count], refs[count : 2 * count], refs[2 * count]
    copies = [
        pltpu.make_async_copy(src, dst, sem.at[i])
        for i, (src, dst) in enumerate(zip(sources, results))
    ]
    for copy in copies:
        copy.start()
    for copy in copies:
        copy.wait()


def on_device(n_dp, n_space, x, g, w1, b1, w2, b2, neighbours, corner_rule):
    rows_dev = CH // n_dp
    rows_pad = (rows_dev + 7) // 8 * 8
    n_y, n_x, n_z = n_dp // 2, 4, n_space // 4
    share = (4 * rows_pad, LANES)
    field = x.shape
    shapes = (
        jax.ShapeDtypeStruct(field, BF16),
        jax.ShapeDtypeStruct(field, BF16),
        jax.ShapeDtypeStruct((9, rows_dev, CH), F32),
        jax.ShapeDtypeStruct((rows_dev,), F32),
        jax.ShapeDtypeStruct((9, rows_dev, CH), F32),
        jax.ShapeDtypeStruct((rows_dev,), F32),
    )
    hbm = pl.BlockSpec(memory_space=pltpu.HBM)
    vmem = pl.BlockSpec(memory_space=pltpu.VMEM)
    dma = pltpu.SemaphoreType.DMA
    tile = (CH, GROUPS * LANES)
    reductions = 1 + (n_y - 1) + (n_z - 1) + (2 * n_x - 1)
    operands = [
        pltpu.with_memory_space_constraint(leaf, pltpu.HBM)
        for leaf in (x, g, w1, b1, w2, b2, neighbours.transpose(2, 1, 0), corner_rule.T)
    ]
    results = pl.pallas_call(
        functools.partial(block_kernel, n_dp, n_space),
        out_shape=tuple(pltpu.VMEM(leaf.shape, leaf.dtype) for leaf in shapes),
        in_specs=[hbm] * 8,
        out_specs=(vmem,) * len(shapes),
        scratch_shapes=[
            pltpu.VMEM(tile, BF16),
            pltpu.VMEM(tile, BF16),
            pltpu.VMEM((9, CH, CH), BF16),
            pltpu.VMEM((CH,), F32),
            pltpu.VMEM((9, CH, CH), BF16),
            pltpu.VMEM((CH,), F32),
            pltpu.SMEM((3, 4, n_space), jnp.int32),
            pltpu.SMEM((4, n_space), jnp.int32),
            pltpu.VMEM(tile, BF16),
            pltpu.VMEM(tile, BF16),
            pltpu.VMEM(tile, F32),
            pltpu.VMEM(tile, F32),
            pltpu.VMEM(tile, BF16),
            pltpu.VMEM((K3 + 16, WIDE), BF16),
            pltpu.VMEM((K3 + 16, WIDE), BF16),
            pltpu.VMEM((K3, WIDE), BF16),
            pltpu.VMEM((K3, WIDE), BF16),
            pltpu.VMEM((K3, WIDE), F32),
            pltpu.VMEM((K3, WIDE), F32),
            pltpu.VMEM((K3, WIDE), F32),
            pltpu.VMEM((2, 4, CH, LANES), BF16),
            pltpu.VMEM((2, 4, CH, LANES), BF16),
            pltpu.VMEM((2, CH, LANES), BF16),
            pltpu.VMEM((4, CH, LANES), BF16),
            pltpu.VMEM((4, LANES, 3 * LANES), BF16),
            pltpu.VMEM((4, CH, LANES), BF16),
            pltpu.VMEM((4, CH, LANES), BF16),
            pltpu.VMEM((2, n_dp) + share, F32),
            pltpu.VMEM((n_dp,) + share, F32),
            pltpu.VMEM((n_dp,) + share, BF16),
            pltpu.VMEM((n_y, 2) + share, BF16),
            pltpu.VMEM((2,) + share, BF16),
            pltpu.VMEM((n_z,) + share, BF16),
            pltpu.VMEM((2, n_x) + share, F32),
            dma((8,)),
            dma((16,)),
            dma((16,)),
            dma((reductions,)),
            dma((reductions,)),
            pltpu.SemaphoreType.REGULAR,
        ],
        compiler_params=pltpu.CompilerParams(
            collective_id=0, has_side_effects=True, vmem_limit_bytes=40 << 20
        ),
        name="unet_block",
    )(*operands)
    return pl.pallas_call(
        functools.partial(write_kernel, len(shapes)),
        out_shape=shapes,
        in_specs=[vmem] * len(shapes),
        out_specs=(hbm,) * len(shapes),
        scratch_shapes=[dma((len(shapes),))],
        name="write_results",
    )(*(pltpu.with_memory_space_constraint(leaf, pltpu.VMEM) for leaf in results))


def solution(mesh):
    tiled = P("dp", "space", None, None)
    return jax.shard_map(
        functools.partial(on_device, mesh.shape["dp"], mesh.shape["space"]),
        mesh=mesh,
        in_specs=(tiled, tiled, P(), P(), P(), P(), P(), P()),
        out_specs=(tiled, tiled, P(None, "dp", None), P("dp"), P(None, "dp", None), P("dp")),
        check_vma=False,
    )
```

```python
import functools
import math

import jax
import jax.numpy as jnp
from jax import lax
from jax.experimental import pallas as pl
from jax.experimental.pallas import tpu as pltpu
from jax.sharding import PartitionSpec as P

MESH = pl.DeviceIdType.MESH
F32 = jnp.float32
BF16 = jnp.bfloat16
LANES = 128
CH = 48
SIDE = 64
GROUPS = 32
EXTRA = 32
WIDE = (GROUPS + 1) * LANES
K3 = 3 * CH
ROOT = math.sqrt(2.0 / math.pi)


def grp(v):
    return slice(v * LANES, (v + 1) * LANES)


def roll(values, shift):
    shift = shift % LANES
    return pltpu.roll(values, shift, 1) if shift else values


def dot(a, b, dims):
    return lax.dot_general(a, b, (dims, ((), ())), preferred_element_type=F32)


def line_lane(edge, q):
    odd = (q & 1) == 1
    col_left = jnp.where(odd, q + 63, q)
    col_right = jnp.where(odd, (q + 126) & 127, q + 63)
    return jnp.where(
        edge == 0, q, jnp.where(edge == 2, q + 64, jnp.where(edge == 3, col_left, col_right))
    )


def halo_index(edge, lane):
    if edge == 0:
        return jnp.where(lane >= 64, lane - 64, -1000)
    if edge == 2:
        return jnp.where(lane < 64, lane, -1000)
    even = (lane & 1) == 0
    if edge == 3:
        return jnp.where(even, jnp.where(lane < 64, lane, lane - 63), -1000)
    return jnp.where(even, -1000, jnp.where(lane == 127, 1, jnp.where(lane >= 63, lane - 63, lane + 2)))


def line_index(line, lane):
    even = (lane & 1) == 0
    row = jnp.where(line == 0, lane, lane - 64)
    row = jnp.where((row >= 0) & (row < 64), row, -1000)
    left = jnp.where(even, jnp.where(lane < 64, lane, lane - 63), -1000)
    right = jnp.where(
        even, -1000, jnp.where(lane == 127, 1, jnp.where(lane >= 63, lane - 63, lane + 2))
    )
    return jnp.where((line & 1) == 0, row, jnp.where(line == 3, left, right))


def shifted_mover(edge, line, rotation, shift, end_weight):
    lane = lax.broadcasted_iota(jnp.int32, (8, LANES), 1)
    p = line_index(line, lane)
    q = jnp.where((rotation == 1) | (rotation == 2), 63 - p, p)
    valid = p >= 0
    tap = q + 1 - shift
    source = jnp.where(valid & (tap >= 0) & (tap < 64), line_lane(edge, tap), -1)
    rows = lax.broadcasted_iota(jnp.int32, (LANES, LANES), 0)
    table = jnp.where(rows == jnp.broadcast_to(source[0:1], (LANES, LANES)), 1.0, 0.0)
    if shift != 1:
        end = 0 if shift == 0 else 63
        corner = jnp.where(valid & (q == end), line_lane(edge, q), -1)
        table = table + jnp.where(
            rows == jnp.broadcast_to(corner[0:1], (LANES, LANES)), end_weight, 0.0
        )
    return table.astype(BF16)


def mover(edge, line, rotation):
    lane = lax.broadcasted_iota(jnp.int32, (8, LANES), 1)
    q = halo_index(edge, lane)
    turned = jnp.where((rotation == 1) | (rotation == 2), 63 - q, q)
    source = jnp.where(q < 0, -1, line_lane(line, turned))
    rows = lax.broadcasted_iota(jnp.int32, (LANES, LANES), 0)
    return jnp.where(rows == jnp.broadcast_to(source[0:1], (LANES, LANES)), 1.0, 0.0).astype(BF16)


def column(vector):
    rows = lax.broadcasted_iota(jnp.int32, (CH, CH), 0)
    cols = lax.broadcasted_iota(jnp.int32, (CH, CH), 1)
    spread = jnp.broadcast_to(vector, (CH, CH))
    return jnp.sum(jnp.where(rows == cols, spread, 0.0), axis=1, keepdims=True)


def block_kernel(
    n_dp,
    n_space,
    x_hbm,
    g_hbm,
    w1_hbm,
    b1_hbm,
    w2_hbm,
    b2_hbm,
    nb_hbm,
    rule_hbm,
    out_ref,
    gin_ref,
    gw1_ref,
    gb1_ref,
    gw2_ref,
    gb2_ref,
    x_v,
    g_v,
    w1_ref,
    b1_ref,
    w2_ref,
    b2_ref,
    nb_ref,
    rule_ref,
    act_first,
    dpre_first,
    pre_v,
    back_v,
    dpre_v,
    ex_v,
    ea_v,
    gs2_v,
    gs1_v,
    y_fwd,
    y_two,
    y_one,
    fwd_send,
    fwd_recv,
    tap_send,
    tap_recv,
    tap_move,
    adj_send,
    adj_recv,
    part,
    part_out,
    part_own,
    buf_core,
    sum_core,
    buf_y,
    sum_y,
    buf_z,
    buf_x,
    load_sem,
    halo_ssem,
    halo_rsem,
    red_ssem,
    red_rsem,
    ready_sem,
):
    hop = n_space // 4
    n_y, n_x, n_z = n_dp // 2, 4, n_space // 4
    rows_dev = CH // n_dp
    rows_pad = (rows_dev + 7) // 8 * 8
    me = lax.axis_index("space")
    my_dp = lax.axis_index("dp")
    core = lax.rem(me, 2)
    my_x = lax.div(me, hop)
    my_y, z_lo = lax.div(my_dp, 2), lax.rem(my_dp, 2)
    my_z = lax.div(lax.rem(me, hop), 2) * 2 + z_lo
    offsets = (-1, hop, 1, -hop)
    toward = [lax.rem(me + off + n_space, n_space) for off in offsets]
    reader = [lax.rem(me - off + n_space, n_space) for off in offsets]

    loads = [
        pltpu.make_async_copy(src, dst, load_sem.at[i])
        for i, (src, dst) in enumerate(
            (
                (nb_hbm, nb_ref),
                (rule_hbm, rule_ref),
                (x_hbm.at[0, 0], x_v),
                (g_hbm.at[0, 0], g_v),
                (w1_hbm, w1_ref),
                (w2_hbm, w2_ref),
                (b1_hbm, b1_ref),
                (b2_hbm, b2_ref),
            )
        )
    ]
    load_nb, load_rule, load_x, load_g, load_w1, load_w2, load_b1, load_b2 = loads

    core_peer = {"space": me + 1 - 2 * core}
    y_at = [lax.rem(my_y + s, n_y) for s in range(1, n_y)]
    y_peers = [{"dp": y * 2 + z_lo} for y in y_at]
    z_at = [lax.rem(my_z + s, n_z) for s in range(1, n_z)]
    z_peers = [
        {
            "dp": my_y * 2 + lax.rem(z, 2),
            "space": my_x * hop + lax.div(z, 2) * 2 + core,
        }
        for z in z_at
    ]
    in_x = lax.rem(me, hop)
    x_peers = [
        {"space": lax.rem(my_x + s, n_x) * hop + in_x + other * (1 - 2 * core)}
        for s in range(n_x)
        for other in range(2)
        if s or other
    ]

    barrier = pltpu.get_barrier_semaphore()
    near = [{"space": dev} for dev in toward] + [core_peer]
    near += [dev for s, dev in enumerate(y_peers, 1) if s in (1, n_y - 1)]
    near += [dev for s, dev in enumerate(z_peers, 1) if s in (1, 2, n_z - 2, n_z - 1)]
    near += [{"space": lax.rem(my_x + 2, n_x) * hop + in_x}]
    for dev in near:
        pl.semaphore_signal(barrier, inc=1, device_id=dev, device_id_type=MESH)
    for copy in loads:
        copy.start()

    lane = lax.broadcasted_iota(jnp.int32, (CH, LANES), 1)
    low = lane < 64
    first_col = (lane & 63) == 0
    last_col = (lane & 63) == 63
    edge_col = first_col | last_col
    zero = jnp.zeros((CH, LANES), F32)
    blank = jnp.zeros((CH, LANES), BF16)

    def remote(src, dst, ssem, rsem, device):
        return pltpu.make_async_remote_copy(
            src_ref=src,
            dst_ref=dst,
            send_sem=ssem,
            recv_sem=rsem,
            device_id=device,
            device_id_type=MESH,
        )

    def halo_copy(sends, recvs, slot, edge, dev):
        at = slot * 4 + edge
        return remote(
            sends.at[edge], recvs.at[edge], halo_ssem.at[at], halo_rsem.at[at], {"space": dev}
        )

    load_nb.wait()
    load_rule.wait()
    fwd_line = [nb_ref[1, e, reader[e]] for e in range(4)]
    fwd_turn = [nb_ref[2, e, reader[e]] for e in range(4)]
    own_line = [nb_ref[1, e, me] for e in range(4)]
    own_turn = [nb_ref[2, e, me] for e in range(4)]
    fwd_movers = [mover(e, fwd_line[e], fwd_turn[e]) for e in range(4)]

    def collected(values_of):
        cols = [zero, zero]
        for v in range(GROUPS):
            cols[v % 2] = cols[v % 2] + roll(jnp.where(edge_col, values_of(v), 0.0), 2 * v)
        return cols[0] + cols[1]

    def lines_of(group_of):
        return [form.astype(BF16) for form in edges_of(group_of)]

    def edges_of(group_of):
        return jnp.where(low, group_of(0), group_of(GROUPS - 1)), collected(group_of)

    def line_of(lines, edge):
        return jnp.where((fwd_line[edge] & 1) == 1, lines[1], lines[0])

    def forward_messages(lines, sends):
        for e in range(4):
            sends[e] = dot(line_of(lines, e), fwd_movers[e], ((1,), (0,))).astype(BF16)

    rules = [rule_ref[c, me] for c in range(4)]
    rule_at = jnp.where(
        lane == 64,
        rules[0],
        jnp.where(lane == 127, rules[1], jnp.where(lane == 0, rules[2], rules[3])),
    )
    first_weight = jnp.where(rule_at == 0, 1.0, jnp.where(rule_at == 1, 0.0, 0.5))
    def end_weights(edge):
        ends = ((0, 1), (1, 3), (2, 3), (0, 2))[edge]
        weights = []
        for c in ends:
            rule = rule_ref[c, reader[edge]]
            first = jnp.where(rule == 0, 1.0, jnp.where(rule == 1, 0.0, 0.5))
            weights.append(1.0 - first if edge % 2 else first)
        return weights

    def tap_movers(moves):
        for e in range(4):
            first, last = end_weights(e)
            for s in range(3):
                moves[e, :, s * LANES : (s + 1) * LANES] = shifted_mover(
                    e, fwd_line[e], fwd_turn[e], s, first if s == 0 else last
                )

    def shifted_taps(lines, moves):
        wide = dot(lines, moves, ((1,), (0,))).astype(BF16)
        return jnp.concatenate([wide[:, s * LANES : (s + 1) * LANES] for s in range(3)], axis=0)

    def fill_inner(padded, v, here):
        padded[0:CH, grp(v)] = jnp.where(first_col, blank, roll(here, 1))
        padded[CH : 2 * CH, grp(v)] = here
        padded[2 * CH : K3, grp(v)] = jnp.where(last_col, blank, roll(here, -1))

    def fill_outer(padded, recvs):
        spread = recvs[1].astype(F32) + recvs[3].astype(F32)
        outer = recvs[0].astype(F32) + recvs[2].astype(F32)
        second = jnp.where(low, roll(spread, 2), roll(spread, 64))
        mean = ((outer + second) * 0.5).astype(BF16).astype(F32)
        corners = jnp.where(rule_at == 0, outer, jnp.where(rule_at == 1, second, mean))
        fill_inner(padded, EXTRA, outer.astype(BF16))
        put_sides(padded, EXTRA, corners.astype(BF16))
        return spread.astype(BF16)

    def put_sides(padded, v, sides):
        padded[0:CH, grp(v)] = jnp.where(first_col, sides, padded[0:CH, grp(v)])
        padded[2 * CH : K3, grp(v)] = jnp.where(last_col, sides, padded[2 * CH : K3, grp(v)])

    def fill_columns(padded, spread):
        for v in range(GROUPS):
            put_sides(padded, v, roll(spread, -2 * v))

    def stacked(w_ref, tap_of):
        return jnp.concatenate(
            [
                jnp.concatenate([w_ref[tap_of(i, j)] for j in range(3)], axis=1)
                for i in range(3)
            ],
            axis=0,
        )

    odd_q = ((lane & 1) == 0) & (lane >= 64) | ((lane & 1) == 1) & ((lane < 63) | (lane == 127))

    def with_corners(rows, cols):
        to_rows = jnp.where(edge_col, jnp.where(low, cols, roll(cols, 66)), 0.0)
        near = (lane == 0) | (lane == 63)
        far = (lane == 126) | (lane == 61)
        to_cols = jnp.where(near, rows, jnp.where(far, roll(rows, 62), 0.0))
        return rows + to_rows, cols + to_cols

    def halo_share(weights, padded, spread):
        outer = dot(weights, padded[0:K3, grp(EXTRA)], ((1,), (0,)))
        rows = roll(jnp.where(low, outer[2 * CH : K3], outer[0:CH]), 64)
        left = dot(weights[:, 0:CH], spread, ((1,), (0,)))
        right = dot(weights[:, 2 * CH : K3], spread, ((1,), (0,)))
        even_lane = (lane & 1) == 0
        taps = [
            jnp.where(even_lane, left[a * CH : (a + 1) * CH], right[a * CH : (a + 1) * CH])
            for a in range(3)
        ]
        onward = jnp.where(odd_q, roll(taps[0], 64), roll(taps[0], 66))
        onward = jnp.where((lane == 0) | (lane == 63), 0.0, onward)
        back = jnp.where(odd_q, roll(taps[2], 62), roll(taps[2], 64))
        back = jnp.where((lane == 126) | (lane == 61), 0.0, back)
        return with_corners(rows, taps[1] + (onward + back))

    def gelu_and_slope(pre):
        square = pre * pre
        th = jnp.tanh(ROOT * (pre + 0.044715 * (square * pre)))
        cdf = 0.5 * (1.0 + th)
        slope = cdf + (0.5 * pre) * (1.0 - th * th) * (ROOT * (1.0 + (3.0 * 0.044715) * square))
        return (pre * cdf).astype(BF16).astype(F32), slope

    def conv(weights, padded, y_ref):
        y_ref[...] = dot(weights, padded[0:K3, :], ((1,), (0,)))

    def conv_group(y_ref, v, halo=True):
        prev = EXTRA if v == 0 else v - 1
        above, below = y_ref[0:CH, grp(v)], y_ref[2 * CH : K3, grp(v)]
        if halo or v < GROUPS - 1:
            above = above + y_ref[2 * CH : K3, grp(v + 1)]
        if halo or v > 0:
            below = below + y_ref[0:CH, grp(prev)]
        both = jnp.where(low, above, below)
        return y_ref[CH : 2 * CH, grp(v)] + roll(both, 64)

    def stack_rows(grad_v, gs_ref):
        turned = None
        for v in range(GROUPS):
            before, here = turned, grad_v[:, grp(v)]
            turned = roll(here, 64)
            gs_ref[CH : 2 * CH, grp(v)] = here
            gs_ref[2 * CH : K3, grp(v)] = jnp.where(low, blank if v == 0 else before, turned)
            if v > 0:
                gs_ref[0:CH, grp(v - 1)] = jnp.where(low, before, turned)
        gs_ref[CH : 2 * CH, grp(EXTRA)] = blank
        gs_ref[2 * CH : K3, grp(EXTRA)] = jnp.where(low, turned, blank)
        gs_ref[0:CH, grp(EXTRA - 1)] = jnp.where(low, turned, blank)
        gs_ref[0:CH, grp(EXTRA)] = jnp.where(low, blank, roll(grad_v[:, grp(0)], 64))

    def transpose_conv(weights, gs_ref, y_ref):
        y_ref[...] = dot(weights, gs_ref[...], ((0,), (0,)))

    def inner_group(y_ref, v):
        left = jnp.where(last_col, 0.0, roll(y_ref[0:CH, grp(v)], -1))
        right = jnp.where(first_col, 0.0, roll(y_ref[2 * CH : K3, grp(v)], 1))
        return y_ref[CH : 2 * CH, grp(v)] + (left + right)

    def adjoint_messages(y_ref, sends):
        def sides(v):
            return jnp.where(
                edge_col,
                jnp.where(last_col, y_ref[2 * CH : K3, grp(v)], y_ref[0:CH, grp(v)]),
                0.0,
            )

        cols = [zero, zero, zero, zero]
        for v in range(GROUPS):
            cols[v % 4] = cols[v % 4] + roll(sides(v), 2 * v)
        corners = sides(EXTRA)
        firsts = first_weight * corners
        seconds = corners - firsts
        cols = (
            (cols[0] + cols[1])
            + (cols[2] + cols[3])
            + roll(jnp.where(low, seconds, 0.0), -2)
            + roll(jnp.where(low, 0.0, seconds), 64)
        ).astype(BF16)
        rows = (inner_group(y_ref, EXTRA) + firsts).astype(BF16)
        for e in range(4):
            move = mover(e, own_line[e], own_turn[e])
            source = cols if e % 2 else rows
            sends[e] = dot(source, move, ((1,), (1,))).astype(BF16)

    def returned_lines(messages):
        rows, cols = zero, zero
        for e in range(4):
            is_col = (fwd_line[e] & 1) == 1
            rows = rows + jnp.where(is_col, 0.0, messages[e])
            cols = cols + jnp.where(is_col, messages[e], 0.0)
        return rows, cols

    def pulled_back(y_ref, rows, cols, v):
        total = inner_group(y_ref, v) + jnp.where(edge_col, roll(cols, -2 * v), 0.0)
        if v == 0:
            total = total + jnp.where(low, rows, 0.0)
        if v == GROUPS - 1:
            total = total + jnp.where(low, 0.0, rows)
        return total

    def cut(grads):
        for d in range(n_dp):
            for a in range(3):
                at = a * CH + d * rows_dev
                to = a * rows_pad
                part[d, to : to + rows_dev, :] = grads[at : at + rows_dev, 0:LANES]
                part[d, 3 * rows_pad : 3 * rows_pad + rows_dev, a * 32 : a * 32 + 32] = grads[
                    at : at + rows_dev, LANES : LANES + 32
                ]

    def x_group(v):
        return x_v[:, grp(v)].astype(F32)

    def g_group(v):
        return g_v[:, grp(v)].astype(F32)

    def act_group(v):
        return ea_v[CH : 2 * CH, grp(v)].astype(F32)

    load_x.wait()
    forward_messages(lines_of(x_group), fwd_send.at[0])
    load_g.wait()
    tap_send[0], tap_send[1] = lines_of(g_group)
    pl.semaphore_wait(barrier, len(near))
    in_fwd = [halo_copy(fwd_send.at[0], fwd_recv.at[0], 0, e, reader[e]) for e in range(4)]
    two_tap = [
        remote(
            tap_send.at[e % 2],
            tap_recv.at[e],
            halo_ssem.at[4 + e],
            halo_rsem.at[4 + e],
            {"space": toward[e]},
        )
        for e in range(4)
    ]
    for copy in in_fwd + two_tap:
        copy.start()

    for dev in near:
        pl.semaphore_signal(ready_sem, inc=1, device_id=dev, device_id_type=MESH)
    tap_movers(tap_move)
    part[...] = jnp.zeros(part.shape, F32)
    part_out[...] = jnp.zeros(part_out.shape, F32)
    part_own[...] = jnp.zeros(part_own.shape, F32)
    ex_v[K3 : K3 + 16, :] = jnp.ones((16, WIDE), BF16)
    ea_v[K3 : K3 + 16, :] = jnp.ones((16, WIDE), BF16)
    for v in range(GROUPS):
        fill_inner(ex_v, v, x_v[:, grp(v)])
    stack_rows(g_v, gs2_v)
    for copy in (load_w1, load_w2, load_b1, load_b2):
        copy.wait()
    w_one = stacked(w1_ref, lambda i, j: 3 * i + j)
    w_two = stacked(w2_ref, lambda i, j: 3 * i + j)
    w_two_by_col = stacked(w2_ref, lambda i, j: 3 * j + i)
    bias_one = jnp.broadcast_to(column(b1_ref[...].reshape(1, CH)), (CH, LANES))
    bias_two = jnp.broadcast_to(column(b2_ref[...].reshape(1, CH)), (CH, LANES))
    transpose_conv(w_two, gs2_v, y_two)

    inner = slice(0, GROUPS * LANES)
    y_fwd[:, inner] = dot(w_one, ex_v[0:K3, inner], ((1,), (0,)))
    for v in range(GROUPS):
        pre_v[:, grp(v)] = conv_group(y_fwd, v, halo=False) + bias_one
    for v in range(GROUPS):
        back_v[:, grp(v)] = inner_group(y_two, v)
    for v in range(GROUPS):
        act, slope = gelu_and_slope(pre_v[:, grp(v)])
        act_first[:, grp(v)] = act.astype(BF16)
        dpre_first[:, grp(v)] = (back_v[:, grp(v)] * slope).astype(BF16)
    pre_rows, pre_cols = edges_of(lambda v: pre_v[:, grp(v)])
    back_rows, back_cols = edges_of(lambda v: back_v[:, grp(v)])

    for copy in in_fwd + two_tap:
        copy.wait_recv()
    in_spread = fill_outer(ex_v, fwd_recv.at[0])
    more_rows, more_cols = halo_share(w_one, ex_v, in_spread)
    act_rows, slope_rows = gelu_and_slope(pre_rows + more_rows)
    act_cols, slope_cols = gelu_and_slope(pre_cols + more_cols)
    taps = [shifted_taps(tap_recv[e], tap_move[e]) for e in range(4)]
    edge_weights = (
        w_two_by_col[:, 0:CH],
        w_two[:, 2 * CH : K3],
        w_two_by_col[:, 2 * CH : K3],
        w_two[:, 0:CH],
    )
    more_rows, more_cols = with_corners(
        *returned_lines([dot(edge_weights[e], taps[e], ((0,), (0,))) for e in range(4)])
    )
    dpre_rows = (back_rows + more_rows) * slope_rows
    dpre_cols = (back_cols + more_cols) * slope_cols
    act_lines = (act_rows.astype(BF16), act_cols.astype(BF16))
    back_lines = (dpre_rows.astype(BF16), dpre_cols.astype(BF16))

    def patched(first, lines, v):
        here = jnp.where(edge_col, roll(lines[1], -2 * v), first[:, grp(v)])
        if v in (0, GROUPS - 1):
            here = jnp.where(low if v == 0 else jnp.logical_not(low), lines[0], here)
        return here

    def grad_two(target):
        for v in range(GROUPS):
            fill_inner(ea_v, v, patched(act_first, act_lines, v))
        by_edge = [dot(taps[e], line_of(act_lines, e), ((1,), (1,))) for e in range(4)]

        def halo_blocks(i):
            blocks = [jnp.zeros((CH, CH), F32)] * 3
            if i != 1:
                blocks = [by_edge[i][b * CH : (b + 1) * CH] for b in range(3)]
            blocks[0] = blocks[0] + by_edge[3][i * CH : (i + 1) * CH]
            blocks[2] = blocks[2] + by_edge[1][i * CH : (i + 1) * CH]
            return jnp.concatenate(blocks + [jnp.zeros((CH, 16), F32)], axis=1)

        halo_two = jnp.concatenate([halo_blocks(i) for i in range(3)], axis=0)
        target[:, 0 : K3 + 16] = dot(gs2_v[:, inner], ea_v[:, inner], ((1,), (1,))) + halo_two

    def grad_one(target):
        for v in range(GROUPS):
            dpre_v[:, grp(v)] = patched(dpre_first, back_lines, v)
        stack_rows(dpre_v, gs1_v)
        fill_columns(ex_v, in_spread)
        target[:, 0 : K3 + 16] = dot(gs1_v[...], ex_v[...], ((1,), (1,)))

    @pl.when(core == 0)
    def _():
        grad_two(part_out)

    @pl.when(core == 1)
    def _():
        grad_one(part_out)

    core_copy = remote(part_out, buf_core, red_ssem.at[0], red_rsem.at[0], core_peer)
    core_copy.start()

    @pl.when(core == 0)
    def _():
        grad_one(part_own)

    @pl.when(core == 1)
    def _():
        grad_two(part_own)

    core_copy.wait_recv()
    cut(part_own[...] + buf_core[...])
    sum_core[...] = part[...].astype(BF16)
    y_copies = [
        remote(
            sum_core.at[pl.ds(y * 2, 2)],
            buf_y.at[my_y],
            red_ssem.at[1 + s],
            red_rsem.at[1 + s],
            y_peers[s],
        )
        for s, y in enumerate(y_at)
    ]
    pl.semaphore_wait(ready_sem, len(near))
    for copy in y_copies:
        copy.start()
    buf_y[my_y] = sum_core[pl.ds(my_y * 2, 2)]

    forward_messages(act_lines, fwd_send.at[1])
    act_fwd = [halo_copy(fwd_send.at[1], fwd_recv.at[1], 2, e, reader[e]) for e in range(4)]
    for copy in act_fwd:
        copy.start()
    transpose_conv(w_one, gs1_v, y_one)
    adjoint_messages(y_one, adj_send)
    one_adj = [halo_copy(adj_send, adj_recv, 3, e, toward[e]) for e in range(4)]
    for copy in one_adj:
        copy.start()

    def summed(buf, count):
        total = buf[0].astype(F32)
        for s in range(1, count):
            total = total + buf[s].astype(F32)
        return total

    for copy in y_copies:
        copy.wait_recv()
    sum_y[...] = summed(buf_y, n_y).astype(BF16)
    at = n_y
    z_copies = [
        remote(
            sum_y.at[lax.rem(z, 2)],
            buf_z.at[my_z],
            red_ssem.at[at + s],
            red_rsem.at[at + s],
            z_peers[s],
        )
        for s, z in enumerate(z_at)
    ]
    for copy in z_copies:
        copy.start()
    buf_z[my_z] = sum_y[z_lo]

    for copy in act_fwd:
        copy.wait_recv()
    fill_columns(ea_v, fill_outer(ea_v, fwd_recv.at[1]))
    conv(w_two, ea_v, y_fwd)
    for v in range(GROUPS):
        out_ref[0, 0, :, grp(v)] = (x_group(v) + conv_group(y_fwd, v) + bias_two).astype(BF16)

    for copy in one_adj:
        copy.wait_recv()
    rows, cols = returned_lines([adj_recv[e].astype(F32) for e in range(4)])
    for v in range(GROUPS):
        gin_ref[0, 0, :, grp(v)] = (g_group(v) + pulled_back(y_one, rows, cols, v)).astype(BF16)

    for copy in z_copies:
        copy.wait_recv()
    buf_x[core, my_x] = summed(buf_z, n_z)
    at = n_y + n_z - 1
    x_copies = [
        remote(
            buf_x.at[core, my_x],
            buf_x.at[core, my_x],
            red_ssem.at[at + s],
            red_rsem.at[at + s],
            dev,
        )
        for s, dev in enumerate(x_peers)
    ]
    for copy in x_copies:
        copy.start()
    for copy in x_copies:
        copy.wait_recv()

    for which, gw_ref, gb_ref in ((0, gw1_ref, gb1_ref), (1, gw2_ref, gb2_ref)):
        total = summed(buf_x.at[which], n_x)
        for a in range(3):
            full = jnp.concatenate(
                [
                    total[a * rows_pad : a * rows_pad + rows_dev],
                    total[3 * rows_pad : 3 * rows_pad + rows_dev, a * 32 : a * 32 + 32],
                ],
                axis=1,
            )
            for b in range(3):
                gw_ref[3 * a + b] = full[:, b * CH : (b + 1) * CH]
            if a == 1:
                eye_r = lax.broadcasted_iota(jnp.int32, (rows_dev, rows_dev), 0)
                eye_c = lax.broadcasted_iota(jnp.int32, (rows_dev, rows_dev), 1)
                spread = jnp.broadcast_to(full[:, K3 : K3 + 1], (rows_dev, rows_dev))
                gb_ref[...] = jnp.sum(jnp.where(eye_r == eye_c, spread, 0.0), axis=0)

    for copy in in_fwd + two_tap + act_fwd + one_adj + [core_copy]:
        copy.wait_send()
    for copy in y_copies + z_copies + x_copies:
        copy.wait_send()


def write_kernel(count, *refs):
    sources, results, sem = refs[:count], refs[count : 2 * count], refs[2 * count]
    copies = [
        pltpu.make_async_copy(src, dst, sem.at[i])
        for i, (src, dst) in enumerate(zip(sources, results))
    ]
    for copy in copies:
        copy.start()
    for copy in copies:
        copy.wait()


def on_device(n_dp, n_space, x, g, w1, b1, w2, b2, neighbours, corner_rule):
    rows_dev = CH // n_dp
    rows_pad = (rows_dev + 7) // 8 * 8
    n_y, n_x, n_z = n_dp // 2, 4, n_space // 4
    share = (4 * rows_pad, LANES)
    field = x.shape
    shapes = (
        jax.ShapeDtypeStruct(field, BF16),
        jax.ShapeDtypeStruct(field, BF16),
        jax.ShapeDtypeStruct((9, rows_dev, CH), F32),
        jax.ShapeDtypeStruct((rows_dev,), F32),
        jax.ShapeDtypeStruct((9, rows_dev, CH), F32),
        jax.ShapeDtypeStruct((rows_dev,), F32),
    )
    hbm = pl.BlockSpec(memory_space=pltpu.HBM)
    vmem = pl.BlockSpec(memory_space=pltpu.VMEM)
    dma = pltpu.SemaphoreType.DMA
    tile = (CH, GROUPS * LANES)
    reductions = 1 + (n_y - 1) + (n_z - 1) + (2 * n_x - 1)
    operands = [
        pltpu.with_memory_space_constraint(leaf, pltpu.HBM)
        for leaf in (x, g, w1, b1, w2, b2, neighbours.transpose(2, 1, 0), corner_rule.T)
    ]
    results = pl.pallas_call(
        functools.partial(block_kernel, n_dp, n_space),
        out_shape=tuple(pltpu.VMEM(leaf.shape, leaf.dtype) for leaf in shapes),
        in_specs=[hbm] * 8,
        out_specs=(vmem,) * len(shapes),
        scratch_shapes=[
            pltpu.VMEM(tile, BF16),
            pltpu.VMEM(tile, BF16),
            pltpu.VMEM((9, CH, CH), BF16),
            pltpu.VMEM((CH,), F32),
            pltpu.VMEM((9, CH, CH), BF16),
            pltpu.VMEM((CH,), F32),
            pltpu.SMEM((3, 4, n_space), jnp.int32),
            pltpu.SMEM((4, n_space), jnp.int32),
            pltpu.VMEM(tile, BF16),
            pltpu.VMEM(tile, BF16),
            pltpu.VMEM(tile, F32),
            pltpu.VMEM(tile, F32),
            pltpu.VMEM(tile, BF16),
            pltpu.VMEM((K3 + 16, WIDE), BF16),
            pltpu.VMEM((K3 + 16, WIDE), BF16),
            pltpu.VMEM((K3, WIDE), BF16),
            pltpu.VMEM((K3, WIDE), BF16),
            pltpu.VMEM((K3, WIDE), F32),
            pltpu.VMEM((K3, WIDE), F32),
            pltpu.VMEM((K3, WIDE), F32),
            pltpu.VMEM((2, 4, CH, LANES), BF16),
            pltpu.VMEM((2, 4, CH, LANES), BF16),
            pltpu.VMEM((2, CH, LANES), BF16),
            pltpu.VMEM((4, CH, LANES), BF16),
            pltpu.VMEM((4, LANES, 3 * LANES), BF16),
            pltpu.VMEM((4, CH, LANES), BF16),
            pltpu.VMEM((4, CH, LANES), BF16),
            pltpu.VMEM((n_dp,) + share, F32),
            pltpu.VMEM((K3, 2 * LANES), F32),
            pltpu.VMEM((K3, 2 * LANES), F32),
            pltpu.VMEM((K3, 2 * LANES), F32),
            pltpu.VMEM((n_dp,) + share, BF16),
            pltpu.VMEM((n_y, 2) + share, BF16),
            pltpu.VMEM((2,) + share, BF16),
            pltpu.VMEM((n_z,) + share, BF16),
            pltpu.VMEM((2, n_x) + share, F32),
            dma((8,)),
            dma((16,)),
            dma((16,)),
            dma((reductions,)),
            dma((reductions,)),
            pltpu.SemaphoreType.REGULAR,
        ],
        compiler_params=pltpu.CompilerParams(
            collective_id=0, has_side_effects=True, vmem_limit_bytes=40 << 20
        ),
        name="unet_block",
    )(*operands)
    return pl.pallas_call(
        functools.partial(write_kernel, len(shapes)),
        out_shape=shapes,
        in_specs=[vmem] * len(shapes),
        out_specs=(hbm,) * len(shapes),
        scratch_shapes=[dma((len(shapes),))],
        name="write_results",
    )(*(pltpu.with_memory_space_constraint(leaf, pltpu.VMEM) for leaf in results))


def solution(mesh):
    tiled = P("dp", "space", None, None)
    return jax.shard_map(
        functools.partial(on_device, mesh.shape["dp"], mesh.shape["space"]),
        mesh=mesh,
        in_specs=(tiled, tiled, P(), P(), P(), P(), P(), P()),
        out_specs=(tiled, tiled, P(None, "dp", None), P("dp"), P(None, "dp", None), P("dp")),
        check_vma=False,
    )
```

```python
import functools
import math

import jax
import jax.numpy as jnp
from jax import lax
from jax.experimental import pallas as pl
from jax.experimental.pallas import tpu as pltpu
from jax.sharding import PartitionSpec as P

MESH = pl.DeviceIdType.MESH
F32 = jnp.float32
BF16 = jnp.bfloat16
LANES = 128
CH = 48
SIDE = 64
GROUPS = 32
EXTRA = 32
WIDE = (GROUPS + 1) * LANES
K3 = 3 * CH
ROOT = math.sqrt(2.0 / math.pi)


def grp(v):
    return slice(v * LANES, (v + 1) * LANES)


def roll(values, shift):
    shift = shift % LANES
    return pltpu.roll(values, shift, 1) if shift else values


def dot(a, b, dims):
    return lax.dot_general(a, b, (dims, ((), ())), preferred_element_type=F32)


def line_lane(edge, q):
    odd = (q & 1) == 1
    col_left = jnp.where(odd, q + 63, q)
    col_right = jnp.where(odd, (q + 126) & 127, q + 63)
    return jnp.where(
        edge == 0, q, jnp.where(edge == 2, q + 64, jnp.where(edge == 3, col_left, col_right))
    )


def halo_index(edge, lane):
    if edge == 0:
        return jnp.where(lane >= 64, lane - 64, -1000)
    if edge == 2:
        return jnp.where(lane < 64, lane, -1000)
    even = (lane & 1) == 0
    if edge == 3:
        return jnp.where(even, jnp.where(lane < 64, lane, lane - 63), -1000)
    return jnp.where(even, -1000, jnp.where(lane == 127, 1, jnp.where(lane >= 63, lane - 63, lane + 2)))


def line_index(line, lane):
    even = (lane & 1) == 0
    row = jnp.where(line == 0, lane, lane - 64)
    row = jnp.where((row >= 0) & (row < 64), row, -1000)
    left = jnp.where(even, jnp.where(lane < 64, lane, lane - 63), -1000)
    right = jnp.where(
        even, -1000, jnp.where(lane == 127, 1, jnp.where(lane >= 63, lane - 63, lane + 2))
    )
    return jnp.where((line & 1) == 0, row, jnp.where(line == 3, left, right))


def shifted_mover(edge, line, rotation, shift, end_weight):
    lane = lax.broadcasted_iota(jnp.int32, (8, LANES), 1)
    p = line_index(line, lane)
    q = jnp.where((rotation == 1) | (rotation == 2), 63 - p, p)
    valid = p >= 0
    tap = q + 1 - shift
    source = jnp.where(valid & (tap >= 0) & (tap < 64), line_lane(edge, tap), -1)
    rows = lax.broadcasted_iota(jnp.int32, (LANES, LANES), 0)
    table = jnp.where(rows == jnp.broadcast_to(source[0:1], (LANES, LANES)), 1.0, 0.0)
    if shift != 1:
        end = 0 if shift == 0 else 63
        corner = jnp.where(valid & (q == end), line_lane(edge, q), -1)
        table = table + jnp.where(
            rows == jnp.broadcast_to(corner[0:1], (LANES, LANES)), end_weight, 0.0
        )
    return table.astype(BF16)


def mover(edge, line, rotation):
    lane = lax.broadcasted_iota(jnp.int32, (8, LANES), 1)
    q = halo_index(edge, lane)
    turned = jnp.where((rotation == 1) | (rotation == 2), 63 - q, q)
    source = jnp.where(q < 0, -1, line_lane(line, turned))
    rows = lax.broadcasted_iota(jnp.int32, (LANES, LANES), 0)
    return jnp.where(rows == jnp.broadcast_to(source[0:1], (LANES, LANES)), 1.0, 0.0).astype(BF16)


def column(vector):
    rows = lax.broadcasted_iota(jnp.int32, (CH, CH), 0)
    cols = lax.broadcasted_iota(jnp.int32, (CH, CH), 1)
    spread = jnp.broadcast_to(vector, (CH, CH))
    return jnp.sum(jnp.where(rows == cols, spread, 0.0), axis=1, keepdims=True)


def far_first(copies, steps, around):
    return [
        copies[i]
        for i in sorted(range(len(copies)), key=lambda i: -min(steps[i], around - steps[i]))
    ]


def block_kernel(
    n_dp,
    n_space,
    x_hbm,
    g_hbm,
    w1_hbm,
    b1_hbm,
    w2_hbm,
    b2_hbm,
    nb_hbm,
    rule_hbm,
    out_ref,
    gin_ref,
    gw1_ref,
    gb1_ref,
    gw2_ref,
    gb2_ref,
    x_v,
    g_v,
    w1_ref,
    b1_ref,
    w2_ref,
    b2_ref,
    nb_ref,
    rule_ref,
    act_first,
    dpre_first,
    pre_v,
    back_v,
    dpre_v,
    ex_v,
    ea_v,
    gs2_v,
    gs1_v,
    y_fwd,
    y_two,
    y_one,
    fwd_send,
    fwd_recv,
    tap_send,
    tap_recv,
    tap_move,
    adj_send,
    adj_recv,
    part,
    part_out,
    part_own,
    buf_core,
    sum_core,
    buf_y,
    sum_y,
    buf_z,
    buf_x,
    load_sem,
    halo_ssem,
    halo_rsem,
    red_ssem,
    red_rsem,
    ready_sem,
):
    hop = n_space // 4
    n_y, n_x, n_z = n_dp // 2, 4, n_space // 4
    rows_dev = CH // n_dp
    rows_pad = (rows_dev + 7) // 8 * 8
    me = lax.axis_index("space")
    my_dp = lax.axis_index("dp")
    core = lax.rem(me, 2)
    my_x = lax.div(me, hop)
    my_y, z_lo = lax.div(my_dp, 2), lax.rem(my_dp, 2)
    my_z = lax.div(lax.rem(me, hop), 2) * 2 + z_lo
    offsets = (-1, hop, 1, -hop)
    toward = [lax.rem(me + off + n_space, n_space) for off in offsets]
    reader = [lax.rem(me - off + n_space, n_space) for off in offsets]

    loads = [
        pltpu.make_async_copy(src, dst, load_sem.at[i])
        for i, (src, dst) in enumerate(
            (
                (nb_hbm, nb_ref),
                (rule_hbm, rule_ref),
                (x_hbm.at[0, 0], x_v),
                (g_hbm.at[0, 0], g_v),
                (w1_hbm, w1_ref),
                (w2_hbm, w2_ref),
                (b1_hbm, b1_ref),
                (b2_hbm, b2_ref),
            )
        )
    ]
    load_nb, load_rule, load_x, load_g, load_w1, load_w2, load_b1, load_b2 = loads

    core_peer = {"space": me + 1 - 2 * core}
    y_at = [lax.rem(my_y + s, n_y) for s in range(1, n_y)]
    y_peers = [{"dp": y * 2 + z_lo} for y in y_at]
    z_at = [lax.rem(my_z + s, n_z) for s in range(1, n_z)]
    z_peers = [
        {
            "dp": my_y * 2 + lax.rem(z, 2),
            "space": my_x * hop + lax.div(z, 2) * 2 + core,
        }
        for z in z_at
    ]
    in_x = lax.rem(me, hop)
    x_peers = [
        {"space": lax.rem(my_x + s, n_x) * hop + in_x + other * (1 - 2 * core)}
        for s in range(n_x)
        for other in range(2)
        if s or other
    ]

    barrier = pltpu.get_barrier_semaphore()
    near = [{"space": dev} for dev in toward] + [core_peer]
    near += [dev for s, dev in enumerate(y_peers, 1) if s in (1, n_y - 1)]
    near += [dev for s, dev in enumerate(z_peers, 1) if s in (1, 2, n_z - 2, n_z - 1)]
    near += [{"space": lax.rem(my_x + 2, n_x) * hop + in_x}]
    for dev in near:
        pl.semaphore_signal(barrier, inc=1, device_id=dev, device_id_type=MESH)
    for copy in loads:
        copy.start()

    lane = lax.broadcasted_iota(jnp.int32, (CH, LANES), 1)
    low = lane < 64
    first_col = (lane & 63) == 0
    last_col = (lane & 63) == 63
    edge_col = first_col | last_col
    zero = jnp.zeros((CH, LANES), F32)
    blank = jnp.zeros((CH, LANES), BF16)

    def remote(src, dst, ssem, rsem, device):
        return pltpu.make_async_remote_copy(
            src_ref=src,
            dst_ref=dst,
            send_sem=ssem,
            recv_sem=rsem,
            device_id=device,
            device_id_type=MESH,
        )

    def halo_copy(sends, recvs, slot, edge, dev):
        at = slot * 4 + edge
        return remote(
            sends.at[edge], recvs.at[edge], halo_ssem.at[at], halo_rsem.at[at], {"space": dev}
        )

    load_nb.wait()
    load_rule.wait()
    fwd_line = [nb_ref[1, e, reader[e]] for e in range(4)]
    fwd_turn = [nb_ref[2, e, reader[e]] for e in range(4)]
    own_line = [nb_ref[1, e, me] for e in range(4)]
    own_turn = [nb_ref[2, e, me] for e in range(4)]
    fwd_movers = [mover(e, fwd_line[e], fwd_turn[e]) for e in range(4)]

    def collected(values_of):
        cols = [zero, zero]
        for v in range(GROUPS):
            cols[v % 2] = cols[v % 2] + roll(jnp.where(edge_col, values_of(v), 0.0), 2 * v)
        return cols[0] + cols[1]

    def lines_of(group_of):
        return [form.astype(BF16) for form in edges_of(group_of)]

    def edges_of(group_of):
        return jnp.where(low, group_of(0), group_of(GROUPS - 1)), collected(group_of)

    def line_of(lines, edge):
        return jnp.where((fwd_line[edge] & 1) == 1, lines[1], lines[0])

    def forward_messages(lines, sends):
        for e in range(4):
            sends[e] = dot(line_of(lines, e), fwd_movers[e], ((1,), (0,))).astype(BF16)

    rules = [rule_ref[c, me] for c in range(4)]
    rule_at = jnp.where(
        lane == 64,
        rules[0],
        jnp.where(lane == 127, rules[1], jnp.where(lane == 0, rules[2], rules[3])),
    )
    first_weight = jnp.where(rule_at == 0, 1.0, jnp.where(rule_at == 1, 0.0, 0.5))
    def end_weights(edge):
        ends = ((0, 1), (1, 3), (2, 3), (0, 2))[edge]
        weights = []
        for c in ends:
            rule = rule_ref[c, reader[edge]]
            first = jnp.where(rule == 0, 1.0, jnp.where(rule == 1, 0.0, 0.5))
            weights.append(1.0 - first if edge % 2 else first)
        return weights

    def tap_movers(moves):
        for e in range(4):
            first, last = end_weights(e)
            for s in range(3):
                moves[e, :, s * LANES : (s + 1) * LANES] = shifted_mover(
                    e, fwd_line[e], fwd_turn[e], s, first if s == 0 else last
                )

    def shifted_taps(lines, moves):
        wide = dot(lines, moves, ((1,), (0,))).astype(BF16)
        return jnp.concatenate([wide[:, s * LANES : (s + 1) * LANES] for s in range(3)], axis=0)

    def fill_inner(padded, v, here):
        padded[0:CH, grp(v)] = jnp.where(first_col, blank, roll(here, 1))
        padded[CH : 2 * CH, grp(v)] = here
        padded[2 * CH : K3, grp(v)] = jnp.where(last_col, blank, roll(here, -1))

    def fill_outer(padded, recvs):
        spread = recvs[1].astype(F32) + recvs[3].astype(F32)
        outer = recvs[0].astype(F32) + recvs[2].astype(F32)
        second = jnp.where(low, roll(spread, 2), roll(spread, 64))
        mean = ((outer + second) * 0.5).astype(BF16).astype(F32)
        corners = jnp.where(rule_at == 0, outer, jnp.where(rule_at == 1, second, mean))
        fill_inner(padded, EXTRA, outer.astype(BF16))
        put_sides(padded, EXTRA, corners.astype(BF16))
        return spread.astype(BF16)

    def put_sides(padded, v, sides):
        padded[0:CH, grp(v)] = jnp.where(first_col, sides, padded[0:CH, grp(v)])
        padded[2 * CH : K3, grp(v)] = jnp.where(last_col, sides, padded[2 * CH : K3, grp(v)])

    def fill_columns(padded, spread):
        for v in range(GROUPS):
            put_sides(padded, v, roll(spread, -2 * v))

    def stacked(w_ref, tap_of):
        return jnp.concatenate(
            [
                jnp.concatenate([w_ref[tap_of(i, j)] for j in range(3)], axis=1)
                for i in range(3)
            ],
            axis=0,
        )

    odd_q = ((lane & 1) == 0) & (lane >= 64) | ((lane & 1) == 1) & ((lane < 63) | (lane == 127))

    def with_corners(rows, cols):
        to_rows = jnp.where(edge_col, jnp.where(low, cols, roll(cols, 66)), 0.0)
        near = (lane == 0) | (lane == 63)
        far = (lane == 126) | (lane == 61)
        to_cols = jnp.where(near, rows, jnp.where(far, roll(rows, 62), 0.0))
        return rows + to_rows, cols + to_cols

    def halo_share(weights, padded, spread):
        outer = dot(weights, padded[0:K3, grp(EXTRA)], ((1,), (0,)))
        rows = roll(jnp.where(low, outer[2 * CH : K3], outer[0:CH]), 64)
        left = dot(weights[:, 0:CH], spread, ((1,), (0,)))
        right = dot(weights[:, 2 * CH : K3], spread, ((1,), (0,)))
        even_lane = (lane & 1) == 0
        taps = [
            jnp.where(even_lane, left[a * CH : (a + 1) * CH], right[a * CH : (a + 1) * CH])
            for a in range(3)
        ]
        onward = jnp.where(odd_q, roll(taps[0], 64), roll(taps[0], 66))
        onward = jnp.where((lane == 0) | (lane == 63), 0.0, onward)
        back = jnp.where(odd_q, roll(taps[2], 62), roll(taps[2], 64))
        back = jnp.where((lane == 126) | (lane == 61), 0.0, back)
        return with_corners(rows, taps[1] + (onward + back))

    def gelu_and_slope(pre):
        square = pre * pre
        th = jnp.tanh(ROOT * (pre + 0.044715 * (square * pre)))
        cdf = 0.5 * (1.0 + th)
        slope = cdf + (0.5 * pre) * (1.0 - th * th) * (ROOT * (1.0 + (3.0 * 0.044715) * square))
        return (pre * cdf).astype(BF16).astype(F32), slope

    def conv(weights, padded, y_ref):
        y_ref[...] = dot(weights, padded[0:K3, :], ((1,), (0,)))

    def conv_group(y_ref, v, halo=True):
        prev = EXTRA if v == 0 else v - 1
        above, below = y_ref[0:CH, grp(v)], y_ref[2 * CH : K3, grp(v)]
        if halo or v < GROUPS - 1:
            above = above + y_ref[2 * CH : K3, grp(v + 1)]
        if halo or v > 0:
            below = below + y_ref[0:CH, grp(prev)]
        both = jnp.where(low, above, below)
        return y_ref[CH : 2 * CH, grp(v)] + roll(both, 64)

    def stack_rows(grad_v, gs_ref):
        turned = None
        for v in range(GROUPS):
            before, here = turned, grad_v[:, grp(v)]
            turned = roll(here, 64)
            gs_ref[CH : 2 * CH, grp(v)] = here
            gs_ref[2 * CH : K3, grp(v)] = jnp.where(low, blank if v == 0 else before, turned)
            if v > 0:
                gs_ref[0:CH, grp(v - 1)] = jnp.where(low, before, turned)
        gs_ref[CH : 2 * CH, grp(EXTRA)] = blank
        gs_ref[2 * CH : K3, grp(EXTRA)] = jnp.where(low, turned, blank)
        gs_ref[0:CH, grp(EXTRA - 1)] = jnp.where(low, turned, blank)
        gs_ref[0:CH, grp(EXTRA)] = jnp.where(low, blank, roll(grad_v[:, grp(0)], 64))

    def transpose_conv(weights, gs_ref, y_ref):
        y_ref[...] = dot(weights, gs_ref[...], ((0,), (0,)))

    def inner_group(y_ref, v):
        left = jnp.where(last_col, 0.0, roll(y_ref[0:CH, grp(v)], -1))
        right = jnp.where(first_col, 0.0, roll(y_ref[2 * CH : K3, grp(v)], 1))
        return y_ref[CH : 2 * CH, grp(v)] + (left + right)

    def adjoint_messages(y_ref, sends):
        def sides(v):
            return jnp.where(
                edge_col,
                jnp.where(last_col, y_ref[2 * CH : K3, grp(v)], y_ref[0:CH, grp(v)]),
                0.0,
            )

        cols = [zero, zero, zero, zero]
        for v in range(GROUPS):
            cols[v % 4] = cols[v % 4] + roll(sides(v), 2 * v)
        corners = sides(EXTRA)
        firsts = first_weight * corners
        seconds = corners - firsts
        cols = (
            (cols[0] + cols[1])
            + (cols[2] + cols[3])
            + roll(jnp.where(low, seconds, 0.0), -2)
            + roll(jnp.where(low, 0.0, seconds), 64)
        ).astype(BF16)
        rows = (inner_group(y_ref, EXTRA) + firsts).astype(BF16)
        for e in range(4):
            move = mover(e, own_line[e], own_turn[e])
            source = cols if e % 2 else rows
            sends[e] = dot(source, move, ((1,), (1,))).astype(BF16)

    def returned_lines(messages):
        rows, cols = zero, zero
        for e in range(4):
            is_col = (fwd_line[e] & 1) == 1
            rows = rows + jnp.where(is_col, 0.0, messages[e])
            cols = cols + jnp.where(is_col, messages[e], 0.0)
        return rows, cols

    def pulled_back(y_ref, rows, cols, v):
        total = inner_group(y_ref, v) + jnp.where(edge_col, roll(cols, -2 * v), 0.0)
        if v == 0:
            total = total + jnp.where(low, rows, 0.0)
        if v == GROUPS - 1:
            total = total + jnp.where(low, 0.0, rows)
        return total

    def cut(grads):
        for d in range(n_dp):
            for a in range(3):
                at = a * CH + d * rows_dev
                to = a * rows_pad
                part[d, to : to + rows_dev, :] = grads[at : at + rows_dev, 0:LANES]
                part[d, 3 * rows_pad : 3 * rows_pad + rows_dev, a * 32 : a * 32 + 32] = grads[
                    at : at + rows_dev, LANES : LANES + 32
                ]

    def x_group(v):
        return x_v[:, grp(v)].astype(F32)

    def g_group(v):
        return g_v[:, grp(v)].astype(F32)

    def act_group(v):
        return ea_v[CH : 2 * CH, grp(v)].astype(F32)

    load_x.wait()
    forward_messages(lines_of(x_group), fwd_send.at[0])
    load_g.wait()
    tap_send[0], tap_send[1] = lines_of(g_group)
    pl.semaphore_wait(barrier, len(near))
    in_fwd = [halo_copy(fwd_send.at[0], fwd_recv.at[0], 0, e, reader[e]) for e in range(4)]
    two_tap = [
        remote(
            tap_send.at[e % 2],
            tap_recv.at[e],
            halo_ssem.at[4 + e],
            halo_rsem.at[4 + e],
            {"space": toward[e]},
        )
        for e in range(4)
    ]
    for copy in in_fwd[::2] + two_tap[::2] + in_fwd[1::2] + two_tap[1::2]:
        copy.start()

    for dev in near:
        pl.semaphore_signal(ready_sem, inc=1, device_id=dev, device_id_type=MESH)
    tap_movers(tap_move)
    part[...] = jnp.zeros(part.shape, F32)
    part_out[...] = jnp.zeros(part_out.shape, F32)
    part_own[...] = jnp.zeros(part_own.shape, F32)
    ex_v[K3 : K3 + 16, :] = jnp.ones((16, WIDE), BF16)
    ea_v[K3 : K3 + 16, :] = jnp.ones((16, WIDE), BF16)
    for v in range(GROUPS):
        fill_inner(ex_v, v, x_v[:, grp(v)])
    stack_rows(g_v, gs2_v)
    for copy in (load_w1, load_w2, load_b1, load_b2):
        copy.wait()
    w_one = stacked(w1_ref, lambda i, j: 3 * i + j)
    w_two = stacked(w2_ref, lambda i, j: 3 * i + j)
    w_two_by_col = stacked(w2_ref, lambda i, j: 3 * j + i)
    bias_one = jnp.broadcast_to(column(b1_ref[...].reshape(1, CH)), (CH, LANES))
    bias_two = jnp.broadcast_to(column(b2_ref[...].reshape(1, CH)), (CH, LANES))
    transpose_conv(w_two, gs2_v, y_two)

    inner = slice(0, GROUPS * LANES)
    y_fwd[:, inner] = dot(w_one, ex_v[0:K3, inner], ((1,), (0,)))
    for v in range(GROUPS):
        pre_v[:, grp(v)] = conv_group(y_fwd, v, halo=False) + bias_one
    for v in range(GROUPS):
        back_v[:, grp(v)] = inner_group(y_two, v)
    for v in range(GROUPS):
        act, slope = gelu_and_slope(pre_v[:, grp(v)])
        act_first[:, grp(v)] = act.astype(BF16)
        dpre_first[:, grp(v)] = (back_v[:, grp(v)] * slope).astype(BF16)
    pre_rows, pre_cols = edges_of(lambda v: pre_v[:, grp(v)])
    back_rows, back_cols = edges_of(lambda v: back_v[:, grp(v)])

    for copy in in_fwd + two_tap:
        copy.wait_recv()
    in_spread = fill_outer(ex_v, fwd_recv.at[0])
    more_rows, more_cols = halo_share(w_one, ex_v, in_spread)
    act_rows, slope_rows = gelu_and_slope(pre_rows + more_rows)
    act_cols, slope_cols = gelu_and_slope(pre_cols + more_cols)
    taps = [shifted_taps(tap_recv[e], tap_move[e]) for e in range(4)]
    edge_weights = (
        w_two_by_col[:, 0:CH],
        w_two[:, 2 * CH : K3],
        w_two_by_col[:, 2 * CH : K3],
        w_two[:, 0:CH],
    )
    more_rows, more_cols = with_corners(
        *returned_lines([dot(edge_weights[e], taps[e], ((0,), (0,))) for e in range(4)])
    )
    dpre_rows = (back_rows + more_rows) * slope_rows
    dpre_cols = (back_cols + more_cols) * slope_cols
    act_lines = (act_rows.astype(BF16), act_cols.astype(BF16))
    back_lines = (dpre_rows.astype(BF16), dpre_cols.astype(BF16))

    def patched(first, lines, v):
        here = jnp.where(edge_col, roll(lines[1], -2 * v), first[:, grp(v)])
        if v in (0, GROUPS - 1):
            here = jnp.where(low if v == 0 else jnp.logical_not(low), lines[0], here)
        return here

    def grad_two(target):
        for v in range(GROUPS):
            fill_inner(ea_v, v, patched(act_first, act_lines, v))
        by_edge = [dot(taps[e], line_of(act_lines, e), ((1,), (1,))) for e in range(4)]

        def halo_blocks(i):
            blocks = [jnp.zeros((CH, CH), F32)] * 3
            if i != 1:
                blocks = [by_edge[i][b * CH : (b + 1) * CH] for b in range(3)]
            blocks[0] = blocks[0] + by_edge[3][i * CH : (i + 1) * CH]
            blocks[2] = blocks[2] + by_edge[1][i * CH : (i + 1) * CH]
            return jnp.concatenate(blocks + [jnp.zeros((CH, 16), F32)], axis=1)

        halo_two = jnp.concatenate([halo_blocks(i) for i in range(3)], axis=0)
        target[:, 0 : K3 + 16] = dot(gs2_v[:, inner], ea_v[:, inner], ((1,), (1,))) + halo_two

    def grad_one(target):
        for v in range(GROUPS):
            dpre_v[:, grp(v)] = patched(dpre_first, back_lines, v)
        stack_rows(dpre_v, gs1_v)
        fill_columns(ex_v, in_spread)
        target[:, 0 : K3 + 16] = dot(gs1_v[...], ex_v[...], ((1,), (1,)))

    @pl.when(core == 0)
    def _():
        grad_two(part_out)

    @pl.when(core == 1)
    def _():
        grad_one(part_out)

    core_copy = remote(part_out, buf_core, red_ssem.at[0], red_rsem.at[0], core_peer)
    core_copy.start()

    @pl.when(core == 0)
    def _():
        grad_one(part_own)

    @pl.when(core == 1)
    def _():
        grad_two(part_own)

    core_copy.wait_recv()
    cut(part_own[...] + buf_core[...])
    sum_core[...] = part[...].astype(BF16)
    y_copies = [
        remote(
            sum_core.at[pl.ds(y * 2, 2)],
            buf_y.at[my_y],
            red_ssem.at[1 + s],
            red_rsem.at[1 + s],
            y_peers[s],
        )
        for s, y in enumerate(y_at)
    ]
    pl.semaphore_wait(ready_sem, len(near))
    for copy in far_first(y_copies, list(range(1, n_y)), n_y):
        copy.start()
    buf_y[my_y] = sum_core[pl.ds(my_y * 2, 2)]

    forward_messages(act_lines, fwd_send.at[1])
    act_fwd = [halo_copy(fwd_send.at[1], fwd_recv.at[1], 2, e, reader[e]) for e in range(4)]
    for copy in act_fwd:
        copy.start()
    transpose_conv(w_one, gs1_v, y_one)
    adjoint_messages(y_one, adj_send)
    one_adj = [halo_copy(adj_send, adj_recv, 3, e, toward[e]) for e in range(4)]
    for copy in one_adj:
        copy.start()

    def summed(buf, count):
        total = buf[0].astype(F32)
        for s in range(1, count):
            total = total + buf[s].astype(F32)
        return total

    for copy in y_copies:
        copy.wait_recv()
    sum_y[...] = summed(buf_y, n_y).astype(BF16)
    at = n_y
    z_copies = [
        remote(
            sum_y.at[lax.rem(z, 2)],
            buf_z.at[my_z],
            red_ssem.at[at + s],
            red_rsem.at[at + s],
            z_peers[s],
        )
        for s, z in enumerate(z_at)
    ]
    for copy in far_first(z_copies, list(range(1, n_z)), n_z):
        copy.start()
    buf_z[my_z] = sum_y[z_lo]

    for copy in act_fwd:
        copy.wait_recv()
    fill_columns(ea_v, fill_outer(ea_v, fwd_recv.at[1]))
    conv(w_two, ea_v, y_fwd)
    for v in range(GROUPS):
        out_ref[0, 0, :, grp(v)] = (x_group(v) + conv_group(y_fwd, v) + bias_two).astype(BF16)

    for copy in one_adj:
        copy.wait_recv()
    rows, cols = returned_lines([adj_recv[e].astype(F32) for e in range(4)])
    for v in range(GROUPS):
        gin_ref[0, 0, :, grp(v)] = (g_group(v) + pulled_back(y_one, rows, cols, v)).astype(BF16)

    for copy in z_copies:
        copy.wait_recv()
    buf_x[core, my_x] = summed(buf_z, n_z)
    at = n_y + n_z - 1
    x_copies = [
        remote(
            buf_x.at[core, my_x],
            buf_x.at[core, my_x],
            red_ssem.at[at + s],
            red_rsem.at[at + s],
            dev,
        )
        for s, dev in enumerate(x_peers)
    ]
    for copy in far_first(x_copies, [(i + 1) // 2 for i in range(2 * n_x - 1)], n_x):
        copy.start()
    for copy in x_copies:
        copy.wait_recv()

    for which, gw_ref, gb_ref in ((0, gw1_ref, gb1_ref), (1, gw2_ref, gb2_ref)):
        total = summed(buf_x.at[which], n_x)
        for a in range(3):
            full = jnp.concatenate(
                [
                    total[a * rows_pad : a * rows_pad + rows_dev],
                    total[3 * rows_pad : 3 * rows_pad + rows_dev, a * 32 : a * 32 + 32],
                ],
                axis=1,
            )
            for b in range(3):
                gw_ref[3 * a + b] = full[:, b * CH : (b + 1) * CH]
            if a == 1:
                eye_r = lax.broadcasted_iota(jnp.int32, (rows_dev, rows_dev), 0)
                eye_c = lax.broadcasted_iota(jnp.int32, (rows_dev, rows_dev), 1)
                spread = jnp.broadcast_to(full[:, K3 : K3 + 1], (rows_dev, rows_dev))
                gb_ref[...] = jnp.sum(jnp.where(eye_r == eye_c, spread, 0.0), axis=0)

    for copy in in_fwd + two_tap + act_fwd + one_adj + [core_copy]:
        copy.wait_send()
    for copy in y_copies + z_copies + x_copies:
        copy.wait_send()


def write_kernel(count, *refs):
    sources, results, sem = refs[:count], refs[count : 2 * count], refs[2 * count]
    copies = [
        pltpu.make_async_copy(src, dst, sem.at[i])
        for i, (src, dst) in enumerate(zip(sources, results))
    ]
    for copy in copies:
        copy.start()
    for copy in copies:
        copy.wait()


def on_device(n_dp, n_space, x, g, w1, b1, w2, b2, neighbours, corner_rule):
    rows_dev = CH // n_dp
    rows_pad = (rows_dev + 7) // 8 * 8
    n_y, n_x, n_z = n_dp // 2, 4, n_space // 4
    share = (4 * rows_pad, LANES)
    field = x.shape
    shapes = (
        jax.ShapeDtypeStruct(field, BF16),
        jax.ShapeDtypeStruct(field, BF16),
        jax.ShapeDtypeStruct((9, rows_dev, CH), F32),
        jax.ShapeDtypeStruct((rows_dev,), F32),
        jax.ShapeDtypeStruct((9, rows_dev, CH), F32),
        jax.ShapeDtypeStruct((rows_dev,), F32),
    )
    hbm = pl.BlockSpec(memory_space=pltpu.HBM)
    vmem = pl.BlockSpec(memory_space=pltpu.VMEM)
    dma = pltpu.SemaphoreType.DMA
    tile = (CH, GROUPS * LANES)
    reductions = 1 + (n_y - 1) + (n_z - 1) + (2 * n_x - 1)
    operands = [
        pltpu.with_memory_space_constraint(leaf, pltpu.HBM)
        for leaf in (x, g, w1, b1, w2, b2, neighbours.transpose(2, 1, 0), corner_rule.T)
    ]
    results = pl.pallas_call(
        functools.partial(block_kernel, n_dp, n_space),
        out_shape=tuple(pltpu.VMEM(leaf.shape, leaf.dtype) for leaf in shapes),
        in_specs=[hbm] * 8,
        out_specs=(vmem,) * len(shapes),
        scratch_shapes=[
            pltpu.VMEM(tile, BF16),
            pltpu.VMEM(tile, BF16),
            pltpu.VMEM((9, CH, CH), BF16),
            pltpu.VMEM((CH,), F32),
            pltpu.VMEM((9, CH, CH), BF16),
            pltpu.VMEM((CH,), F32),
            pltpu.SMEM((3, 4, n_space), jnp.int32),
            pltpu.SMEM((4, n_space), jnp.int32),
            pltpu.VMEM(tile, BF16),
            pltpu.VMEM(tile, BF16),
            pltpu.VMEM(tile, F32),
            pltpu.VMEM(tile, F32),
            pltpu.VMEM(tile, BF16),
            pltpu.VMEM((K3 + 16, WIDE), BF16),
            pltpu.VMEM((K3 + 16, WIDE), BF16),
            pltpu.VMEM((K3, WIDE), BF16),
            pltpu.VMEM((K3, WIDE), BF16),
            pltpu.VMEM((K3, WIDE), F32),
            pltpu.VMEM((K3, WIDE), F32),
            pltpu.VMEM((K3, WIDE), F32),
            pltpu.VMEM((2, 4, CH, LANES), BF16),
            pltpu.VMEM((2, 4, CH, LANES), BF16),
            pltpu.VMEM((2, CH, LANES), BF16),
            pltpu.VMEM((4, CH, LANES), BF16),
            pltpu.VMEM((4, LANES, 3 * LANES), BF16),
            pltpu.VMEM((4, CH, LANES), BF16),
            pltpu.VMEM((4, CH, LANES), BF16),
            pltpu.VMEM((n_dp,) + share, F32),
            pltpu.VMEM((K3, 2 * LANES), F32),
            pltpu.VMEM((K3, 2 * LANES), F32),
            pltpu.VMEM((K3, 2 * LANES), F32),
            pltpu.VMEM((n_dp,) + share, BF16),
            pltpu.VMEM((n_y, 2) + share, BF16),
            pltpu.VMEM((2,) + share, BF16),
            pltpu.VMEM((n_z,) + share, BF16),
            pltpu.VMEM((2, n_x) + share, F32),
            dma((8,)),
            dma((16,)),
            dma((16,)),
            dma((reductions,)),
            dma((reductions,)),
            pltpu.SemaphoreType.REGULAR,
        ],
        compiler_params=pltpu.CompilerParams(
            collective_id=0, has_side_effects=True, vmem_limit_bytes=40 << 20
        ),
        name="unet_block",
    )(*operands)
    return pl.pallas_call(
        functools.partial(write_kernel, len(shapes)),
        out_shape=shapes,
        in_specs=[vmem] * len(shapes),
        out_specs=(hbm,) * len(shapes),
        scratch_shapes=[dma((len(shapes),))],
        name="write_results",
    )(*(pltpu.with_memory_space_constraint(leaf, pltpu.VMEM) for leaf in results))


def solution(mesh):
    tiled = P("dp", "space", None, None)
    return jax.shard_map(
        functools.partial(on_device, mesh.shape["dp"], mesh.shape["space"]),
        mesh=mesh,
        in_specs=(tiled, tiled, P(), P(), P(), P(), P(), P()),
        out_specs=(tiled, tiled, P(None, "dp", None), P("dp"), P(None, "dp", None), P("dp")),
        check_vma=False,
    )
```

```python
import functools
import math

import jax
import jax.numpy as jnp
from jax import lax
from jax.experimental import pallas as pl
from jax.experimental.pallas import tpu as pltpu
from jax.sharding import PartitionSpec as P

MESH = pl.DeviceIdType.MESH
F32 = jnp.float32
BF16 = jnp.bfloat16
LANES = 128
CH = 48
SIDE = 64
GROUPS = 32
EXTRA = 32
WIDE = (GROUPS + 1) * LANES
K3 = 3 * CH
ROOT = math.sqrt(2.0 / math.pi)


def grp(v):
    return slice(v * LANES, (v + 1) * LANES)


def roll(values, shift):
    shift = shift % LANES
    return pltpu.roll(values, shift, 1) if shift else values


def dot(a, b, dims):
    return lax.dot_general(a, b, (dims, ((), ())), preferred_element_type=F32)


def line_lane(edge, q):
    odd = (q & 1) == 1
    col_left = jnp.where(odd, q + 63, q)
    col_right = jnp.where(odd, (q + 126) & 127, q + 63)
    return jnp.where(
        edge == 0, q, jnp.where(edge == 2, q + 64, jnp.where(edge == 3, col_left, col_right))
    )


def halo_index(edge, lane):
    if edge == 0:
        return jnp.where(lane >= 64, lane - 64, -1000)
    if edge == 2:
        return jnp.where(lane < 64, lane, -1000)
    even = (lane & 1) == 0
    if edge == 3:
        return jnp.where(even, jnp.where(lane < 64, lane, lane - 63), -1000)
    return jnp.where(even, -1000, jnp.where(lane == 127, 1, jnp.where(lane >= 63, lane - 63, lane + 2)))


def line_index(line, lane):
    even = (lane & 1) == 0
    row = jnp.where(line == 0, lane, lane - 64)
    row = jnp.where((row >= 0) & (row < 64), row, -1000)
    left = jnp.where(even, jnp.where(lane < 64, lane, lane - 63), -1000)
    right = jnp.where(
        even, -1000, jnp.where(lane == 127, 1, jnp.where(lane >= 63, lane - 63, lane + 2))
    )
    return jnp.where((line & 1) == 0, row, jnp.where(line == 3, left, right))


def shifted_mover(edge, line, rotation, shift, end_weight):
    lane = lax.broadcasted_iota(jnp.int32, (8, LANES), 1)
    p = line_index(line, lane)
    q = jnp.where((rotation == 1) | (rotation == 2), 63 - p, p)
    valid = p >= 0
    tap = q + 1 - shift
    source = jnp.where(valid & (tap >= 0) & (tap < 64), line_lane(edge, tap), -1)
    rows = lax.broadcasted_iota(jnp.int32, (LANES, LANES), 0)
    table = jnp.where(rows == jnp.broadcast_to(source[0:1], (LANES, LANES)), 1.0, 0.0)
    if shift != 1:
        end = 0 if shift == 0 else 63
        corner = jnp.where(valid & (q == end), line_lane(edge, q), -1)
        table = table + jnp.where(
            rows == jnp.broadcast_to(corner[0:1], (LANES, LANES)), end_weight, 0.0
        )
    return table.astype(BF16)


def mover(edge, line, rotation):
    lane = lax.broadcasted_iota(jnp.int32, (8, LANES), 1)
    q = halo_index(edge, lane)
    turned = jnp.where((rotation == 1) | (rotation == 2), 63 - q, q)
    source = jnp.where(q < 0, -1, line_lane(line, turned))
    rows = lax.broadcasted_iota(jnp.int32, (LANES, LANES), 0)
    return jnp.where(rows == jnp.broadcast_to(source[0:1], (LANES, LANES)), 1.0, 0.0).astype(BF16)


def column(vector):
    rows = lax.broadcasted_iota(jnp.int32, (CH, CH), 0)
    cols = lax.broadcasted_iota(jnp.int32, (CH, CH), 1)
    spread = jnp.broadcast_to(vector, (CH, CH))
    return jnp.sum(jnp.where(rows == cols, spread, 0.0), axis=1, keepdims=True)


def far_first(copies, steps, around):
    return [
        copies[i]
        for i in sorted(range(len(copies)), key=lambda i: -min(steps[i], around - steps[i]))
    ]


def block_kernel(
    n_dp,
    n_space,
    x_hbm,
    g_hbm,
    w1_hbm,
    b1_hbm,
    w2_hbm,
    b2_hbm,
    nb_hbm,
    rule_hbm,
    out_ref,
    gin_ref,
    gw1_ref,
    gb1_ref,
    gw2_ref,
    gb2_ref,
    x_v,
    g_v,
    w1_ref,
    b1_ref,
    w2_ref,
    b2_ref,
    nb_ref,
    rule_ref,
    act_first,
    dpre_first,
    pre_v,
    back_v,
    dpre_v,
    ex_v,
    ea_v,
    gs2_v,
    gs1_v,
    y_fwd,
    y_two,
    y_one,
    fwd_send,
    fwd_recv,
    tap_send,
    tap_recv,
    tap_move,
    adj_send,
    adj_recv,
    part,
    part_out,
    part_own,
    buf_core,
    sum_core,
    buf_y,
    sum_y,
    buf_z,
    buf_x,
    load_sem,
    halo_ssem,
    halo_rsem,
    red_ssem,
    red_rsem,
    ready_sem,
):
    hop = n_space // 4
    n_y, n_x, n_z = n_dp // 2, 4, n_space // 4
    rows_dev = CH // n_dp
    rows_pad = (rows_dev + 7) // 8 * 8
    me = lax.axis_index("space")
    my_dp = lax.axis_index("dp")
    core = lax.rem(me, 2)
    my_x = lax.div(me, hop)
    my_y, z_lo = lax.div(my_dp, 2), lax.rem(my_dp, 2)
    my_z = lax.div(lax.rem(me, hop), 2) * 2 + z_lo
    offsets = (-1, hop, 1, -hop)
    toward = [lax.rem(me + off + n_space, n_space) for off in offsets]
    reader = [lax.rem(me - off + n_space, n_space) for off in offsets]

    loads = [
        pltpu.make_async_copy(src, dst, load_sem.at[i])
        for i, (src, dst) in enumerate(
            (
                (nb_hbm, nb_ref),
                (rule_hbm, rule_ref),
                (x_hbm.at[0, 0], x_v),
                (g_hbm.at[0, 0], g_v),
                (w1_hbm, w1_ref),
                (w2_hbm, w2_ref),
                (b1_hbm, b1_ref),
                (b2_hbm, b2_ref),
            )
        )
    ]
    load_nb, load_rule, load_x, load_g, load_w1, load_w2, load_b1, load_b2 = loads

    core_peer = {"space": me + 1 - 2 * core}
    y_at = [lax.rem(my_y + s, n_y) for s in range(1, n_y)]
    y_peers = [{"dp": y * 2 + z_lo} for y in y_at]
    z_at = [lax.rem(my_z + s, n_z) for s in range(1, n_z)]
    z_peers = [
        {
            "dp": my_y * 2 + lax.rem(z, 2),
            "space": my_x * hop + lax.div(z, 2) * 2 + core,
        }
        for z in z_at
    ]
    in_x = lax.rem(me, hop)
    x_peers = [
        {"space": lax.rem(my_x + s, n_x) * hop + in_x + other * (1 - 2 * core)}
        for s in range(n_x)
        for other in range(2)
        if s or other
    ]

    barrier = pltpu.get_barrier_semaphore()
    near = [{"space": dev} for dev in toward] + [core_peer]
    near += [dev for s, dev in enumerate(y_peers, 1) if s in (1, n_y - 1)]
    near += [dev for s, dev in enumerate(z_peers, 1) if s in (1, 2, n_z - 2, n_z - 1)]
    near += [{"space": lax.rem(my_x + 2, n_x) * hop + in_x}]
    for dev in near:
        pl.semaphore_signal(barrier, inc=1, device_id=dev, device_id_type=MESH)
    for copy in loads:
        copy.start()

    lane = lax.broadcasted_iota(jnp.int32, (CH, LANES), 1)
    low = lane < 64
    first_col = (lane & 63) == 0
    last_col = (lane & 63) == 63
    edge_col = first_col | last_col
    zero = jnp.zeros((CH, LANES), F32)
    blank = jnp.zeros((CH, LANES), BF16)

    def remote(src, dst, ssem, rsem, device):
        return pltpu.make_async_remote_copy(
            src_ref=src,
            dst_ref=dst,
            send_sem=ssem,
            recv_sem=rsem,
            device_id=device,
            device_id_type=MESH,
        )

    def halo_copy(sends, recvs, slot, edge, dev):
        at = slot * 4 + edge
        return remote(
            sends.at[edge], recvs.at[edge], halo_ssem.at[at], halo_rsem.at[at], {"space": dev}
        )

    load_nb.wait()
    load_rule.wait()
    fwd_line = [nb_ref[1, e, reader[e]] for e in range(4)]
    fwd_turn = [nb_ref[2, e, reader[e]] for e in range(4)]
    own_line = [nb_ref[1, e, me] for e in range(4)]
    own_turn = [nb_ref[2, e, me] for e in range(4)]
    fwd_movers = [mover(e, fwd_line[e], fwd_turn[e]) for e in range(4)]

    def collected(values_of):
        cols = [zero, zero]
        for v in range(GROUPS):
            cols[v % 2] = cols[v % 2] + roll(jnp.where(edge_col, values_of(v), 0.0), 2 * v)
        return cols[0] + cols[1]

    def lines_of(group_of):
        return [form.astype(BF16) for form in edges_of(group_of)]

    def edges_of(group_of):
        return jnp.where(low, group_of(0), group_of(GROUPS - 1)), collected(group_of)

    def line_of(lines, edge):
        return jnp.where((fwd_line[edge] & 1) == 1, lines[1], lines[0])

    def forward_messages(lines, sends):
        for e in range(4):
            sends[e] = dot(line_of(lines, e), fwd_movers[e], ((1,), (0,))).astype(BF16)

    rules = [rule_ref[c, me] for c in range(4)]
    rule_at = jnp.where(
        lane == 64,
        rules[0],
        jnp.where(lane == 127, rules[1], jnp.where(lane == 0, rules[2], rules[3])),
    )
    first_weight = jnp.where(rule_at == 0, 1.0, jnp.where(rule_at == 1, 0.0, 0.5))
    def end_weights(edge):
        ends = ((0, 1), (1, 3), (2, 3), (0, 2))[edge]
        weights = []
        for c in ends:
            rule = rule_ref[c, reader[edge]]
            first = jnp.where(rule == 0, 1.0, jnp.where(rule == 1, 0.0, 0.5))
            weights.append(1.0 - first if edge % 2 else first)
        return weights

    def tap_movers(moves):
        for e in range(4):
            first, last = end_weights(e)
            for s in range(3):
                moves[e, :, s * LANES : (s + 1) * LANES] = shifted_mover(
                    e, fwd_line[e], fwd_turn[e], s, first if s == 0 else last
                )

    def shifted_taps(lines, moves):
        wide = dot(lines, moves, ((1,), (0,))).astype(BF16)
        return jnp.concatenate([wide[:, s * LANES : (s + 1) * LANES] for s in range(3)], axis=0)

    def fill_inner(padded, v, here):
        padded[0:CH, grp(v)] = jnp.where(first_col, blank, roll(here, 1))
        padded[CH : 2 * CH, grp(v)] = here
        padded[2 * CH : K3, grp(v)] = jnp.where(last_col, blank, roll(here, -1))

    def fill_outer(padded, recvs):
        spread = recvs[1].astype(F32) + recvs[3].astype(F32)
        outer = recvs[0].astype(F32) + recvs[2].astype(F32)
        second = jnp.where(low, roll(spread, 2), roll(spread, 64))
        mean = ((outer + second) * 0.5).astype(BF16).astype(F32)
        corners = jnp.where(rule_at == 0, outer, jnp.where(rule_at == 1, second, mean))
        fill_inner(padded, EXTRA, outer.astype(BF16))
        put_sides(padded, EXTRA, corners.astype(BF16))
        return spread.astype(BF16)

    def put_sides(padded, v, sides):
        padded[0:CH, grp(v)] = jnp.where(first_col, sides, padded[0:CH, grp(v)])
        padded[2 * CH : K3, grp(v)] = jnp.where(last_col, sides, padded[2 * CH : K3, grp(v)])

    def fill_columns(padded, spread):
        for v in range(GROUPS):
            put_sides(padded, v, roll(spread, -2 * v))

    def stacked(w_ref, tap_of):
        return jnp.concatenate(
            [
                jnp.concatenate([w_ref[tap_of(i, j)] for j in range(3)], axis=1)
                for i in range(3)
            ],
            axis=0,
        )

    odd_q = ((lane & 1) == 0) & (lane >= 64) | ((lane & 1) == 1) & ((lane < 63) | (lane == 127))

    def with_corners(rows, cols):
        to_rows = jnp.where(edge_col, jnp.where(low, cols, roll(cols, 66)), 0.0)
        near = (lane == 0) | (lane == 63)
        far = (lane == 126) | (lane == 61)
        to_cols = jnp.where(near, rows, jnp.where(far, roll(rows, 62), 0.0))
        return rows + to_rows, cols + to_cols

    def halo_share(weights, padded, spread):
        outer = dot(weights, padded[0:K3, grp(EXTRA)], ((1,), (0,)))
        rows = roll(jnp.where(low, outer[2 * CH : K3], outer[0:CH]), 64)
        left = dot(weights[:, 0:CH], spread, ((1,), (0,)))
        right = dot(weights[:, 2 * CH : K3], spread, ((1,), (0,)))
        even_lane = (lane & 1) == 0
        taps = [
            jnp.where(even_lane, left[a * CH : (a + 1) * CH], right[a * CH : (a + 1) * CH])
            for a in range(3)
        ]
        onward = jnp.where(odd_q, roll(taps[0], 64), roll(taps[0], 66))
        onward = jnp.where((lane == 0) | (lane == 63), 0.0, onward)
        back = jnp.where(odd_q, roll(taps[2], 62), roll(taps[2], 64))
        back = jnp.where((lane == 126) | (lane == 61), 0.0, back)
        return with_corners(rows, taps[1] + (onward + back))

    def gelu_and_slope(pre):
        square = pre * pre
        th = jnp.tanh(ROOT * (pre + 0.044715 * (square * pre)))
        cdf = 0.5 * (1.0 + th)
        slope = cdf + (0.5 * pre) * (1.0 - th * th) * (ROOT * (1.0 + (3.0 * 0.044715) * square))
        return (pre * cdf).astype(BF16).astype(F32), slope

    def conv(weights, padded, y_ref):
        y_ref[...] = dot(weights, padded[0:K3, :], ((1,), (0,)))

    def conv_group(y_ref, v, halo=True):
        prev = EXTRA if v == 0 else v - 1
        above, below = y_ref[0:CH, grp(v)], y_ref[2 * CH : K3, grp(v)]
        if halo or v < GROUPS - 1:
            above = above + y_ref[2 * CH : K3, grp(v + 1)]
        if halo or v > 0:
            below = below + y_ref[0:CH, grp(prev)]
        both = jnp.where(low, above, below)
        return y_ref[CH : 2 * CH, grp(v)] + roll(both, 64)

    def stack_rows(grad_v, gs_ref):
        turned = None
        for v in range(GROUPS):
            before, here = turned, grad_v[:, grp(v)]
            turned = roll(here, 64)
            gs_ref[CH : 2 * CH, grp(v)] = here
            gs_ref[2 * CH : K3, grp(v)] = jnp.where(low, blank if v == 0 else before, turned)
            if v > 0:
                gs_ref[0:CH, grp(v - 1)] = jnp.where(low, before, turned)
        gs_ref[CH : 2 * CH, grp(EXTRA)] = blank
        gs_ref[2 * CH : K3, grp(EXTRA)] = jnp.where(low, turned, blank)
        gs_ref[0:CH, grp(EXTRA - 1)] = jnp.where(low, turned, blank)
        gs_ref[0:CH, grp(EXTRA)] = jnp.where(low, blank, roll(grad_v[:, grp(0)], 64))

    def transpose_conv(weights, gs_ref, y_ref):
        y_ref[...] = dot(weights, gs_ref[...], ((0,), (0,)))

    def inner_group(y_ref, v):
        left = jnp.where(last_col, 0.0, roll(y_ref[0:CH, grp(v)], -1))
        right = jnp.where(first_col, 0.0, roll(y_ref[2 * CH : K3, grp(v)], 1))
        return y_ref[CH : 2 * CH, grp(v)] + (left + right)

    def adjoint_messages(y_ref, sends):
        def sides(v):
            return jnp.where(
                edge_col,
                jnp.where(last_col, y_ref[2 * CH : K3, grp(v)], y_ref[0:CH, grp(v)]),
                0.0,
            )

        cols = [zero, zero, zero, zero]
        for v in range(GROUPS):
            cols[v % 4] = cols[v % 4] + roll(sides(v), 2 * v)
        corners = sides(EXTRA)
        firsts = first_weight * corners
        seconds = corners - firsts
        cols = (
            (cols[0] + cols[1])
            + (cols[2] + cols[3])
            + roll(jnp.where(low, seconds, 0.0), -2)
            + roll(jnp.where(low, 0.0, seconds), 64)
        ).astype(BF16)
        rows = (inner_group(y_ref, EXTRA) + firsts).astype(BF16)
        for e in range(4):
            move = mover(e, own_line[e], own_turn[e])
            source = cols if e % 2 else rows
            sends[e] = dot(source, move, ((1,), (1,))).astype(BF16)

    def returned_lines(messages):
        rows, cols = zero, zero
        for e in range(4):
            is_col = (fwd_line[e] & 1) == 1
            rows = rows + jnp.where(is_col, 0.0, messages[e])
            cols = cols + jnp.where(is_col, messages[e], 0.0)
        return rows, cols

    def pulled_back(y_ref, rows, cols, v):
        total = inner_group(y_ref, v) + jnp.where(edge_col, roll(cols, -2 * v), 0.0)
        if v == 0:
            total = total + jnp.where(low, rows, 0.0)
        if v == GROUPS - 1:
            total = total + jnp.where(low, 0.0, rows)
        return total

    def pack(target, grads):
        target[0:K3, :] = grads[:, 0:LANES]
        for a in range(3):
            target[K3 : K3 + CH, a * 32 : a * 32 + 32] = grads[a * CH : (a + 1) * CH, LANES:]

    def cut(grads):
        for d in range(n_dp):
            for a in range(3):
                at = a * CH + d * rows_dev
                to = a * rows_pad
                part[d, to : to + rows_dev, :] = grads[at : at + rows_dev]
            at = K3 + d * rows_dev
            part[d, 3 * rows_pad : 3 * rows_pad + rows_dev, :] = grads[at : at + rows_dev]

    def x_group(v):
        return x_v[:, grp(v)].astype(F32)

    def g_group(v):
        return g_v[:, grp(v)].astype(F32)

    def act_group(v):
        return ea_v[CH : 2 * CH, grp(v)].astype(F32)

    load_x.wait()
    forward_messages(lines_of(x_group), fwd_send.at[0])
    load_g.wait()
    tap_send[0], tap_send[1] = lines_of(g_group)
    pl.semaphore_wait(barrier, len(near))
    in_fwd = [halo_copy(fwd_send.at[0], fwd_recv.at[0], 0, e, reader[e]) for e in range(4)]
    two_tap = [
        remote(
            tap_send.at[e % 2],
            tap_recv.at[e],
            halo_ssem.at[4 + e],
            halo_rsem.at[4 + e],
            {"space": toward[e]},
        )
        for e in range(4)
    ]
    for copy in in_fwd[::2] + two_tap[::2] + in_fwd[1::2] + two_tap[1::2]:
        copy.start()

    for dev in near:
        pl.semaphore_signal(ready_sem, inc=1, device_id=dev, device_id_type=MESH)
    tap_movers(tap_move)
    part[...] = jnp.zeros(part.shape, F32)
    part_out[...] = jnp.zeros(part_out.shape, F32)
    part_own[...] = jnp.zeros(part_own.shape, F32)
    ex_v[K3 : K3 + 16, :] = jnp.ones((16, WIDE), BF16)
    ea_v[K3 : K3 + 16, :] = jnp.ones((16, WIDE), BF16)
    for v in range(GROUPS):
        fill_inner(ex_v, v, x_v[:, grp(v)])
    stack_rows(g_v, gs2_v)
    for copy in (load_w1, load_w2, load_b1, load_b2):
        copy.wait()
    w_one = stacked(w1_ref, lambda i, j: 3 * i + j)
    w_two = stacked(w2_ref, lambda i, j: 3 * i + j)
    w_two_by_col = stacked(w2_ref, lambda i, j: 3 * j + i)
    bias_one = jnp.broadcast_to(column(b1_ref[...].reshape(1, CH)), (CH, LANES))
    bias_two = jnp.broadcast_to(column(b2_ref[...].reshape(1, CH)), (CH, LANES))
    transpose_conv(w_two, gs2_v, y_two)

    inner = slice(0, GROUPS * LANES)
    y_fwd[:, inner] = dot(w_one, ex_v[0:K3, inner], ((1,), (0,)))
    for v in range(GROUPS):
        pre_v[:, grp(v)] = conv_group(y_fwd, v, halo=False) + bias_one
    for v in range(GROUPS):
        back_v[:, grp(v)] = inner_group(y_two, v)
    for v in range(GROUPS):
        act, slope = gelu_and_slope(pre_v[:, grp(v)])
        act_first[:, grp(v)] = act.astype(BF16)
        dpre_first[:, grp(v)] = (back_v[:, grp(v)] * slope).astype(BF16)
    pre_rows, pre_cols = edges_of(lambda v: pre_v[:, grp(v)])
    back_rows, back_cols = edges_of(lambda v: back_v[:, grp(v)])

    for copy in in_fwd + two_tap:
        copy.wait_recv()
    in_spread = fill_outer(ex_v, fwd_recv.at[0])
    more_rows, more_cols = halo_share(w_one, ex_v, in_spread)
    act_rows, slope_rows = gelu_and_slope(pre_rows + more_rows)
    act_cols, slope_cols = gelu_and_slope(pre_cols + more_cols)
    taps = [shifted_taps(tap_recv[e], tap_move[e]) for e in range(4)]
    edge_weights = (
        w_two_by_col[:, 0:CH],
        w_two[:, 2 * CH : K3],
        w_two_by_col[:, 2 * CH : K3],
        w_two[:, 0:CH],
    )
    more_rows, more_cols = with_corners(
        *returned_lines([dot(edge_weights[e], taps[e], ((0,), (0,))) for e in range(4)])
    )
    dpre_rows = (back_rows + more_rows) * slope_rows
    dpre_cols = (back_cols + more_cols) * slope_cols
    act_lines = (act_rows.astype(BF16), act_cols.astype(BF16))
    back_lines = (dpre_rows.astype(BF16), dpre_cols.astype(BF16))

    def patched(first, lines, v):
        here = jnp.where(edge_col, roll(lines[1], -2 * v), first[:, grp(v)])
        if v in (0, GROUPS - 1):
            here = jnp.where(low if v == 0 else jnp.logical_not(low), lines[0], here)
        return here

    def grad_two(target):
        for v in range(GROUPS):
            fill_inner(ea_v, v, patched(act_first, act_lines, v))
        by_edge = [dot(taps[e], line_of(act_lines, e), ((1,), (1,))) for e in range(4)]

        def halo_blocks(i):
            blocks = [jnp.zeros((CH, CH), F32)] * 3
            if i != 1:
                blocks = [by_edge[i][b * CH : (b + 1) * CH] for b in range(3)]
            blocks[0] = blocks[0] + by_edge[3][i * CH : (i + 1) * CH]
            blocks[2] = blocks[2] + by_edge[1][i * CH : (i + 1) * CH]
            return jnp.concatenate(blocks + [jnp.zeros((CH, 16), F32)], axis=1)

        halo_two = jnp.concatenate([halo_blocks(i) for i in range(3)], axis=0)
        pack(target, dot(gs2_v[:, inner], ea_v[:, inner], ((1,), (1,))) + halo_two)

    def grad_one(target):
        for v in range(GROUPS):
            dpre_v[:, grp(v)] = patched(dpre_first, back_lines, v)
        stack_rows(dpre_v, gs1_v)
        fill_columns(ex_v, in_spread)
        pack(target, dot(gs1_v[...], ex_v[...], ((1,), (1,))))

    @pl.when(core == 0)
    def _():
        grad_two(part_out)

    @pl.when(core == 1)
    def _():
        grad_one(part_out)

    core_copy = remote(part_out, buf_core, red_ssem.at[0], red_rsem.at[0], core_peer)
    core_copy.start()

    @pl.when(core == 0)
    def _():
        grad_one(part_own)

    @pl.when(core == 1)
    def _():
        grad_two(part_own)

    core_copy.wait_recv()
    cut(part_own[...] + buf_core[...])
    sum_core[...] = part[...].astype(BF16)
    y_copies = [
        remote(
            sum_core.at[pl.ds(y * 2, 2)],
            buf_y.at[my_y],
            red_ssem.at[1 + s],
            red_rsem.at[1 + s],
            y_peers[s],
        )
        for s, y in enumerate(y_at)
    ]
    pl.semaphore_wait(ready_sem, len(near))
    for copy in far_first(y_copies, list(range(1, n_y)), n_y):
        copy.start()
    buf_y[my_y] = sum_core[pl.ds(my_y * 2, 2)]

    forward_messages(act_lines, fwd_send.at[1])
    act_fwd = [halo_copy(fwd_send.at[1], fwd_recv.at[1], 2, e, reader[e]) for e in range(4)]
    for copy in act_fwd:
        copy.start()
    transpose_conv(w_one, gs1_v, y_one)
    adjoint_messages(y_one, adj_send)
    one_adj = [halo_copy(adj_send, adj_recv, 3, e, toward[e]) for e in range(4)]
    for copy in one_adj:
        copy.start()

    def summed(buf, count):
        total = buf[0].astype(F32)
        for s in range(1, count):
            total = total + buf[s].astype(F32)
        return total

    for copy in y_copies:
        copy.wait_recv()
    sum_y[...] = summed(buf_y, n_y).astype(BF16)
    at = n_y
    z_copies = [
        remote(
            sum_y.at[lax.rem(z, 2)],
            buf_z.at[my_z],
            red_ssem.at[at + s],
            red_rsem.at[at + s],
            z_peers[s],
        )
        for s, z in enumerate(z_at)
    ]
    for copy in far_first(z_copies, list(range(1, n_z)), n_z):
        copy.start()
    buf_z[my_z] = sum_y[z_lo]

    for copy in act_fwd:
        copy.wait_recv()
    fill_columns(ea_v, fill_outer(ea_v, fwd_recv.at[1]))
    conv(w_two, ea_v, y_fwd)
    for v in range(GROUPS):
        out_ref[0, 0, :, grp(v)] = (x_group(v) + conv_group(y_fwd, v) + bias_two).astype(BF16)

    for copy in one_adj:
        copy.wait_recv()
    rows, cols = returned_lines([adj_recv[e].astype(F32) for e in range(4)])
    for v in range(GROUPS):
        gin_ref[0, 0, :, grp(v)] = (g_group(v) + pulled_back(y_one, rows, cols, v)).astype(BF16)

    for copy in z_copies:
        copy.wait_recv()
    buf_x[core, my_x] = summed(buf_z, n_z)
    at = n_y + n_z - 1
    x_copies = [
        remote(
            buf_x.at[core, my_x],
            buf_x.at[core, my_x],
            red_ssem.at[at + s],
            red_rsem.at[at + s],
            dev,
        )
        for s, dev in enumerate(x_peers)
    ]
    for copy in far_first(x_copies, [(i + 1) // 2 for i in range(2 * n_x - 1)], n_x):
        copy.start()
    for copy in x_copies:
        copy.wait_recv()

    for which, gw_ref, gb_ref in ((0, gw1_ref, gb1_ref), (1, gw2_ref, gb2_ref)):
        total = summed(buf_x.at[which], n_x)
        for a in range(3):
            full = jnp.concatenate(
                [
                    total[a * rows_pad : a * rows_pad + rows_dev],
                    total[3 * rows_pad : 3 * rows_pad + rows_dev, a * 32 : a * 32 + 32],
                ],
                axis=1,
            )
            for b in range(3):
                gw_ref[3 * a + b] = full[:, b * CH : (b + 1) * CH]
            if a == 1:
                eye_r = lax.broadcasted_iota(jnp.int32, (rows_dev, rows_dev), 0)
                eye_c = lax.broadcasted_iota(jnp.int32, (rows_dev, rows_dev), 1)
                spread = jnp.broadcast_to(full[:, K3 : K3 + 1], (rows_dev, rows_dev))
                gb_ref[...] = jnp.sum(jnp.where(eye_r == eye_c, spread, 0.0), axis=0)

    for copy in in_fwd + two_tap + act_fwd + one_adj + [core_copy]:
        copy.wait_send()
    for copy in y_copies + z_copies + x_copies:
        copy.wait_send()


def write_kernel(count, *refs):
    sources, results, sem = refs[:count], refs[count : 2 * count], refs[2 * count]
    copies = [
        pltpu.make_async_copy(src, dst, sem.at[i])
        for i, (src, dst) in enumerate(zip(sources, results))
    ]
    for copy in copies:
        copy.start()
    for copy in copies:
        copy.wait()


def on_device(n_dp, n_space, x, g, w1, b1, w2, b2, neighbours, corner_rule):
    rows_dev = CH // n_dp
    rows_pad = (rows_dev + 7) // 8 * 8
    n_y, n_x, n_z = n_dp // 2, 4, n_space // 4
    share = (4 * rows_pad, LANES)
    field = x.shape
    shapes = (
        jax.ShapeDtypeStruct(field, BF16),
        jax.ShapeDtypeStruct(field, BF16),
        jax.ShapeDtypeStruct((9, rows_dev, CH), F32),
        jax.ShapeDtypeStruct((rows_dev,), F32),
        jax.ShapeDtypeStruct((9, rows_dev, CH), F32),
        jax.ShapeDtypeStruct((rows_dev,), F32),
    )
    hbm = pl.BlockSpec(memory_space=pltpu.HBM)
    vmem = pl.BlockSpec(memory_space=pltpu.VMEM)
    dma = pltpu.SemaphoreType.DMA
    tile = (CH, GROUPS * LANES)
    reductions = 1 + (n_y - 1) + (n_z - 1) + (2 * n_x - 1)
    operands = [
        pltpu.with_memory_space_constraint(leaf, pltpu.HBM)
        for leaf in (x, g, w1, b1, w2, b2, neighbours.transpose(2, 1, 0), corner_rule.T)
    ]
    results = pl.pallas_call(
        functools.partial(block_kernel, n_dp, n_space),
        out_shape=tuple(pltpu.VMEM(leaf.shape, leaf.dtype) for leaf in shapes),
        in_specs=[hbm] * 8,
        out_specs=(vmem,) * len(shapes),
        scratch_shapes=[
            pltpu.VMEM(tile, BF16),
            pltpu.VMEM(tile, BF16),
            pltpu.VMEM((9, CH, CH), BF16),
            pltpu.VMEM((CH,), F32),
            pltpu.VMEM((9, CH, CH), BF16),
            pltpu.VMEM((CH,), F32),
            pltpu.SMEM((3, 4, n_space), jnp.int32),
            pltpu.SMEM((4, n_space), jnp.int32),
            pltpu.VMEM(tile, BF16),
            pltpu.VMEM(tile, BF16),
            pltpu.VMEM(tile, F32),
            pltpu.VMEM(tile, F32),
            pltpu.VMEM(tile, BF16),
            pltpu.VMEM((K3 + 16, WIDE), BF16),
            pltpu.VMEM((K3 + 16, WIDE), BF16),
            pltpu.VMEM((K3, WIDE), BF16),
            pltpu.VMEM((K3, WIDE), BF16),
            pltpu.VMEM((K3, WIDE), F32),
            pltpu.VMEM((K3, WIDE), F32),
            pltpu.VMEM((K3, WIDE), F32),
            pltpu.VMEM((2, 4, CH, LANES), BF16),
            pltpu.VMEM((2, 4, CH, LANES), BF16),
            pltpu.VMEM((2, CH, LANES), BF16),
            pltpu.VMEM((4, CH, LANES), BF16),
            pltpu.VMEM((4, LANES, 3 * LANES), BF16),
            pltpu.VMEM((4, CH, LANES), BF16),
            pltpu.VMEM((4, CH, LANES), BF16),
            pltpu.VMEM((n_dp,) + share, F32),
            pltpu.VMEM((K3 + CH, LANES), F32),
            pltpu.VMEM((K3 + CH, LANES), F32),
            pltpu.VMEM((K3 + CH, LANES), F32),
            pltpu.VMEM((n_dp,) + share, BF16),
            pltpu.VMEM((n_y, 2) + share, BF16),
            pltpu.VMEM((2,) + share, BF16),
            pltpu.VMEM((n_z,) + share, BF16),
            pltpu.VMEM((2, n_x) + share, F32),
            dma((8,)),
            dma((16,)),
            dma((16,)),
            dma((reductions,)),
            dma((reductions,)),
            pltpu.SemaphoreType.REGULAR,
        ],
        compiler_params=pltpu.CompilerParams(
            collective_id=0, has_side_effects=True, vmem_limit_bytes=40 << 20
        ),
        name="unet_block",
    )(*operands)
    return pl.pallas_call(
        functools.partial(write_kernel, len(shapes)),
        out_shape=shapes,
        in_specs=[vmem] * len(shapes),
        out_specs=(hbm,) * len(shapes),
        scratch_shapes=[dma((len(shapes),))],
        name="write_results",
    )(*(pltpu.with_memory_space_constraint(leaf, pltpu.VMEM) for leaf in results))


def solution(mesh):
    tiled = P("dp", "space", None, None)
    return jax.shard_map(
        functools.partial(on_device, mesh.shape["dp"], mesh.shape["space"]),
        mesh=mesh,
        in_specs=(tiled, tiled, P(), P(), P(), P(), P(), P()),
        out_specs=(tiled, tiled, P(None, "dp", None), P("dp"), P(None, "dp", None), P("dp")),
        check_vma=False,
    )
```
